512 devices in a mesh: dp: 2 (over z_hi), fsdp: 16 (over z_lo, core), tile: 16 (over y, x).
Axes of the slice: x: 4, y: 4, z: 16 (z_hi: 2, z_lo: 8; z = z_hi * 8 + z_lo), core: 2. Of those that a mesh axis runs over, the one named last changes fastest.
Arguments:
- tokens: bfloat16 [32, 8, 512, 1536], P(('dp', 'fsdp'), None, 'tile'), may hold values from -6 to 6
- norm_gain: float32 [1536], replicated, may hold values from 0.25 to 1.75
- query_key_value_weight: bfloat16 [1536, 2304], P('fsdp'), may hold values from -5 to 5
- out_weight: bfloat16 [768, 1536], P('fsdp'), may hold values from -0.21875 to 0.21875
- head_weight: bfloat16 [1536, 320], P('fsdp'), may hold values from -0.15625 to 0.15625
- coarse: float32 [32, 20, 8, 512], P(('dp', 'fsdp'), None, None, 'tile'), may hold values from -36 to 36
- grad_fine: float32 [32, 20, 32, 2048], P(('dp', 'fsdp'), None, None, 'tile'), may hold values from -0.6 to 0.6
Outputs:
- fine_grid: float32 [32, 20, 32, 2048], P(('dp', 'fsdp'), None, None, 'tile')
- grad_tokens: bfloat16 [32, 8, 512, 1536], P(('dp', 'fsdp'), None, 'tile')
- grad_head: float32 [1536, 320], P('fsdp')
The draws below stay inside these ranges and needn't reach their ends.
All inputs are finite; a program needn't handle non-finite values.
Results may differ from the reference program's by a relative error of at most 0.0059.
Values may be sent and summed in bfloat16 or wider, within the bound.
No kernel may reach another device: no remote copies, remote signals or barrier semaphores. Data moves between devices by JAX's collectives and lax.ppermute only.
A program may use at most 64 MiB of HBM per device.

```python
import jax
import jax.numpy as jnp
from jax import lax

D = 1536
HEADS = 8
HEAD_DIM = 96
VARS = 20
MARGIN = 8
LAT = 8
LON_DEV = 32
INNER = 768
HEAD_OUT = 320
LON = 512
SAMPLES = 32
N_TILE = 16


def draw_query_key_value_weight(key, part):
    base_key = jax.random.fold_in(key, 101)
    entries = jax.random.normal(base_key, (D, 3 * INNER), jnp.float32) * D ** (-0.5)
    entries = jnp.clip(entries, -6.0 * D ** (-0.5), 6.0 * D ** (-0.5))
    return jnp.clip(entries, -5.0, 5.0).astype(jnp.bfloat16)


def steps_of(rng, shape, split, low, top_value):
    loudness, own = 1.0, jax.random.fold_in(rng, 6)
    for position, shards_of in split:
        steps = jnp.exp(jax.random.uniform(jax.random.fold_in(own, position), (shards_of,), jnp.float32, low / len(split), top_value / len(split)))
        loudness = loudness * jnp.repeat(steps, shape[position] // shards_of).reshape([-1 if axis == position else 1 for axis in range(len(shape))])
    return loudness


def scatter_about(key, shape, spread, reach, split=(), held_as=jnp.bfloat16):
    array = jax.random.normal(key, shape, jnp.float32) * spread
    if len(split) > 0:
        array = steps_of(key, shape, split, -0.22, 0.18) * array
    return jnp.clip(array, min=-reach, max=reach).astype(held_as)


def setup_inputs(seed: int = 0) -> dict:
    arg_keys = jax.random.split(jax.random.key(seed), 8)
    tokens = scatter_about(arg_keys[0], (SAMPLES, LAT, LON, D), 1.0, 6.0, ((0, 32), (2, 16)))
    norm_gain = jnp.clip(1.0 + 0.15 * jax.random.normal(arg_keys[1], (D,), jnp.float32), 0.25, 1.75)
    query_key_value_weight = draw_query_key_value_weight(jax.random.fold_in(arg_keys[7], 71), 0)
    out_weight = scatter_about(arg_keys[3], (INNER, D), INNER ** -0.5, 0.21875, ((0, 16),))
    head_weight = scatter_about(arg_keys[4], (D, HEAD_OUT), D ** -0.5, 0.15625, ((0, 16),))
    coarse = scatter_about(arg_keys[5], (SAMPLES, VARS, LAT, LON), 6.0, 36.0, ((0, 32), (3, 16)), jnp.float32)
    grad_fine = scatter_about(arg_keys[6], (SAMPLES, VARS, 4 * LAT, 4 * LON), 0.1, 0.6, ((0, 32), (3, 16)), jnp.float32)
    return {"tokens": tokens, "norm_gain": norm_gain, "query_key_value_weight": query_key_value_weight, "out_weight": out_weight, "head_weight": head_weight, "coarse": coarse, "grad_fine": grad_fine}


EPSILON = 1e-05

def layer_norm(values, norm_gain):
    average = lax.optimization_barrier(jnp.mean(values, axis=-1, keepdims=True))
    centred = values - average
    variance = lax.optimization_barrier(jnp.mean(centred * centred, axis=-1, keepdims=True))
    inverse_dev = lax.rsqrt(variance + EPSILON)
    return (centred * inverse_dev, inverse_dev)

def norm_backward(grad_normed, standard, inverse_dev, norm_gain):
    grad_standard = grad_normed * norm_gain
    first_mean = lax.optimization_barrier(jnp.mean(grad_standard, axis=-1, keepdims=True))
    second_mean = lax.optimization_barrier(jnp.mean(grad_standard * standard, axis=-1, keepdims=True))
    return inverse_dev * (grad_standard - first_mean - standard * second_mean)

def widen(values):
    return lax.optimization_barrier(values.astype(jnp.bfloat16)).astype(jnp.float32)

def attend_tile(queries, keys_values, grad_attended):
    query_count = queries.shape[0]
    key_count = keys_values.shape[0]
    score_scale = HEAD_DIM ** (-0.5)
    query_heads = queries.reshape(query_count, HEADS, HEAD_DIM).astype(jnp.float32)
    key_heads = keys_values[:, :INNER].reshape(key_count, HEADS, HEAD_DIM).astype(jnp.float32)
    value_heads = keys_values[:, INNER:].reshape(key_count, HEADS, HEAD_DIM).astype(jnp.float32)
    scores = jnp.einsum('qhd,khd->hqk', query_heads, key_heads) * score_scale
    biggest = lax.optimization_barrier(jnp.max(scores, axis=-1, keepdims=True))
    exponent = jnp.exp(scores - biggest)
    softmax_out = exponent / lax.optimization_barrier(jnp.sum(exponent, axis=-1, keepdims=True))
    softmax_low = widen(softmax_out)
    attended = jnp.einsum('hqk,khd->qhd', softmax_low, value_heads).astype(jnp.bfloat16)
    grad_heads = grad_attended.reshape(query_count, HEADS, HEAD_DIM).astype(jnp.float32)
    grad_values = jnp.einsum('hqk,qhd->khd', softmax_low, grad_heads)
    grad_weights = jnp.einsum('qhd,khd->hqk', grad_heads, value_heads)
    weighted = lax.optimization_barrier(jnp.sum(softmax_out * grad_weights, axis=-1, keepdims=True))
    grad_scores = widen(softmax_out * (grad_weights - weighted))
    grad_queries = (jnp.einsum('hqk,khd->qhd', grad_scores, key_heads) * score_scale).astype(jnp.bfloat16)
    grad_keys = jnp.einsum('hqk,qhd->khd', grad_scores, query_heads) * score_scale
    pair_gradient_rows = jnp.concatenate([grad_keys.reshape(key_count, INNER), grad_values.reshape(key_count, INNER)], axis=1)
    return (attended.reshape(query_count, INNER), grad_queries.reshape(query_count, INNER), pair_gradient_rows)

def interp_matrix(count, periodic):
    fine_index = jnp.arange(4 * count, dtype=jnp.int32)
    coarse_cell = fine_index // 4
    phase_index = fine_index % 4
    lower_shift = (phase_index < 2).astype(jnp.int32)
    lower_cell = coarse_cell - lower_shift
    upper_weight = (2 * phase_index - 3 + 8 * lower_shift).astype(jnp.float32) / 8.0
    if periodic:
        upper_cell = (lower_cell + 1) % count
        lower_cell = lower_cell % count
    else:
        upper_cell = jnp.clip(lower_cell + 1, 0, count - 1)
        lower_cell = jnp.clip(lower_cell, 0, count - 1)
    columns = jnp.arange(count, dtype=jnp.int32)
    lower_part = jnp.where(columns[None, :] == lower_cell[:, None], 1.0 - upper_weight[:, None], 0.0)
    upper_portion = jnp.where(columns[None, :] == upper_cell[:, None], upper_weight[:, None], 0.0)
    return (lower_part + upper_portion).astype(jnp.float32)

def one_sample(tokens, coarse, grad_fine, norm_gain, query_key_value_weight, out_weight, head_weight):
    flattened_rows = tokens.reshape(LAT * LON, D).astype(jnp.float32)
    standard, inverse_dev = layer_norm(flattened_rows, norm_gain)
    normed = (standard * norm_gain).astype(jnp.bfloat16)
    projected = jnp.dot(normed, query_key_value_weight, preferred_element_type=jnp.float32).astype(jnp.bfloat16)
    projected = projected.reshape(LAT, LON, 3 * INNER)
    grad_rows = grad_fine.reshape(VARS, LAT, 4, LON, 4).transpose(1, 3, 0, 2, 4).reshape(LAT * LON, HEAD_OUT)
    grad_rows = grad_rows.astype(jnp.bfloat16)
    grad_hidden = jnp.dot(grad_rows, head_weight.T, preferred_element_type=jnp.float32)
    grad_attended = jnp.dot(grad_hidden.astype(jnp.bfloat16), out_weight.T, preferred_element_type=jnp.float32)
    grad_attended = grad_attended.astype(jnp.bfloat16).reshape(LAT, LON, INNER)

    def per_tile(current_tile_index):
        first_col = current_tile_index * LON_DEV
        queries = lax.dynamic_slice_in_dim(projected[:, :, :INNER], first_col, LON_DEV, 1)
        columns = (first_col - MARGIN + jnp.arange(LON_DEV + 2 * MARGIN, dtype=jnp.int32)) % LON
        columns = columns.astype(jnp.int32)
        keys_values = jnp.take(projected[:, :, INNER:], columns, axis=1)
        grad_tile = lax.dynamic_slice_in_dim(grad_attended, first_col, LON_DEV, 1)
        attended, grad_queries, pair_gradient_rows = attend_tile(queries.reshape(-1, INNER), keys_values.reshape(-1, 2 * INNER), grad_tile.reshape(-1, INNER))
        return (attended.reshape(LAT, LON_DEV, INNER), grad_queries.reshape(LAT, LON_DEV, INNER), pair_gradient_rows.reshape(LAT, LON_DEV + 2 * MARGIN, 2 * INNER), columns)
    attended, grad_queries, pair_gradient_rows, columns = lax.map(per_tile, jnp.arange(N_TILE, dtype=jnp.int32))
    attended = attended.transpose(1, 0, 2, 3).reshape(LAT * LON, INNER)
    grad_queries = grad_queries.transpose(1, 0, 2, 3).reshape(LAT * LON, INNER)
    pair_total = jnp.zeros((LAT, LON, 2 * INNER), jnp.float32).at[:, columns].add(pair_gradient_rows.transpose(1, 0, 2, 3))
    mixed_out = jnp.dot(attended, out_weight, preferred_element_type=jnp.float32)
    hidden = (flattened_rows + mixed_out).astype(jnp.bfloat16)
    head_out = jnp.dot(hidden, head_weight, preferred_element_type=jnp.float32)
    fine_head = head_out.reshape(LAT, LON, VARS, 4, 4).transpose(2, 0, 3, 1, 4).reshape(VARS, 4 * LAT, 4 * LON)
    latitude_matrix = interp_matrix(LAT, False)
    lon_matrix = interp_matrix(LON, True)
    incomplete_grid = jnp.einsum('lj,kji->kli', latitude_matrix, coarse, precision=lax.Precision.HIGHEST)
    residual = jnp.einsum('vrb,cb->vrc', incomplete_grid, lon_matrix, precision=lax.Precision.HIGHEST)
    fine_grid = fine_head + residual
    head_term = jnp.dot(hidden.T, grad_rows, preferred_element_type=jnp.float32)
    grad_all = jnp.concatenate([grad_queries, pair_total.reshape(LAT * LON, 2 * INNER).astype(jnp.bfloat16)], axis=1)
    grad_normed = jnp.dot(grad_all, query_key_value_weight.T, preferred_element_type=jnp.float32)
    grad_input = grad_hidden + norm_backward(grad_normed, standard, inverse_dev, norm_gain)
    return (fine_grid, grad_input.astype(jnp.bfloat16).reshape(LAT, LON, D), head_term)

def reference(tokens, norm_gain, query_key_value_weight, out_weight, head_weight, coarse, grad_fine):

    def sample_step(running, inputs):
        fine_grid, grad_input, head_term = one_sample(inputs[0], inputs[1], inputs[2], norm_gain, query_key_value_weight, out_weight, head_weight)
        return (running + head_term, (fine_grid, grad_input))
    grad_head, outputs = lax.scan(sample_step, jnp.zeros((D, HEAD_OUT), jnp.float32), (tokens, coarse, grad_fine))
    return (outputs[0], outputs[1], grad_head)
```

```python
import jax
import jax.numpy as jnp
from jax import lax
from jax.sharding import Mesh
from jax.sharding import PartitionSpec as P

D = 1536
HEADS = 8
HEAD_DIM = 96
VARS = 20
MARGIN = 8
INNER = 768
HEAD_OUT = 320


EPSILON = 1e-05


def with_halo(shard, sides, width):
    for axis, dim in sides:
        devices, length = (lax.axis_size(axis), shard.shape[dim])
        up = [(i, (i + 1) % devices) for i in range(devices)]
        down = [(j, i) for i, j in up]
        last = lax.slice_in_dim(shard, length - width, length, axis=dim)
        leading = lax.slice_in_dim(shard, 0, width, axis=dim)
        before = lax.ppermute(last, axis, up)
        after = lax.ppermute(leading, axis, down)
        shard = jnp.concatenate([before, shard, after], axis=dim)
    return shard


def from_behind(value, axis, steps):
    count = lax.axis_size(axis)
    pairs = [(source, (source + steps) % count) for source in range(count)]
    return lax.ppermute(value, axis, pairs)


def layer_norm(values):
    average = jnp.mean(values, axis=-1, keepdims=True)
    centred = values - average
    variance = jnp.mean(centred * centred, axis=-1, keepdims=True)
    inverse_dev = lax.rsqrt(variance + EPSILON)
    return (centred * inverse_dev, inverse_dev)


def norm_backward(grad_normed, standard, inverse_dev, norm_gain):
    grad_standard = grad_normed * norm_gain
    first_mean = jnp.mean(grad_standard, axis=-1, keepdims=True)
    second_mean = jnp.mean(grad_standard * standard, axis=-1, keepdims=True)
    return inverse_dev * (grad_standard - first_mean - standard * second_mean)


def attend_forward(queries, keys_values):
    query_count = queries.shape[0]
    key_count = keys_values.shape[0]
    score_scale = HEAD_DIM ** (-0.5)
    query_heads = queries.reshape(query_count, HEADS, HEAD_DIM)
    key_heads = keys_values[:, :INNER].reshape(key_count, HEADS, HEAD_DIM)
    value_heads = keys_values[:, INNER:].reshape(key_count, HEADS, HEAD_DIM)
    scores = (
        jnp.einsum("qhd,khd->hqk", query_heads, key_heads, preferred_element_type=jnp.float32)
        * score_scale
    )
    biggest = jnp.max(scores, axis=-1, keepdims=True)
    exponent = jnp.exp(scores - biggest)
    softmax_out = exponent / jnp.sum(exponent, axis=-1, keepdims=True)
    softmax_low = softmax_out.astype(jnp.bfloat16)
    attended = jnp.einsum(
        "hqk,khd->qhd", softmax_low, value_heads, preferred_element_type=jnp.float32
    )
    return (attended.astype(jnp.bfloat16).reshape(query_count, INNER), softmax_out)


def attend_backward(softmax_out, queries, keys_values, grad_attended):
    query_count = queries.shape[0]
    key_count = keys_values.shape[0]
    score_scale = HEAD_DIM ** (-0.5)
    query_heads = queries.reshape(query_count, HEADS, HEAD_DIM)
    key_heads = keys_values[:, :INNER].reshape(key_count, HEADS, HEAD_DIM)
    value_heads = keys_values[:, INNER:].reshape(key_count, HEADS, HEAD_DIM)
    grad_heads = grad_attended.reshape(query_count, HEADS, HEAD_DIM)
    softmax_low = softmax_out.astype(jnp.bfloat16)
    grad_values = jnp.einsum(
        "hqk,qhd->khd", softmax_low, grad_heads, preferred_element_type=jnp.float32
    )
    grad_weights = jnp.einsum(
        "qhd,khd->hqk", grad_heads, value_heads, preferred_element_type=jnp.float32
    )
    weighted = jnp.sum(softmax_out * grad_weights, axis=-1, keepdims=True)
    grad_scores = (softmax_out * (grad_weights - weighted)).astype(jnp.bfloat16)
    grad_queries = (
        jnp.einsum("hqk,khd->qhd", grad_scores, key_heads, preferred_element_type=jnp.float32)
        * score_scale
    )
    grad_keys = (
        jnp.einsum("hqk,qhd->khd", grad_scores, query_heads, preferred_element_type=jnp.float32)
        * score_scale
    )
    pair_gradient_rows = jnp.concatenate(
        [grad_keys.reshape(key_count, INNER), grad_values.reshape(key_count, INNER)], axis=1
    )
    return (grad_queries.astype(jnp.bfloat16).reshape(query_count, INNER), pair_gradient_rows)


def interp_weights(fine_index):
    coarse_cell = fine_index // 4
    phase_index = fine_index % 4
    lower_shift = (phase_index < 2).astype(jnp.int32)
    upper_weight = (2 * phase_index - 3 + 8 * lower_shift).astype(jnp.float32) / 8.0
    return (coarse_cell - lower_shift, upper_weight)


def build_matrix(lower_cell, upper_cell, upper_weight, count):
    columns = jnp.arange(count, dtype=jnp.int32)
    lower_part = jnp.where(
        columns[None, :] == lower_cell[:, None], 1.0 - upper_weight[:, None], 0.0
    )
    upper_portion = jnp.where(columns[None, :] == upper_cell[:, None], upper_weight[:, None], 0.0)
    return lower_part + upper_portion


def contract_last(left_side, right_side):
    return lax.dot_general(
        left_side, right_side, (((1,), (1,)), ((), ())), preferred_element_type=jnp.float32
    )


ZS = 8
CORES = 2
YS = 4
XS = 4
FSDP = ("z", "c")
TILE = ("y", "x")
HALF_QKV = 1152
HALF_OUT = 768


def gather_weights(qkv, out_w, head_w):
    half = lax.axis_index("dp")
    qkv_half = lax.dynamic_slice_in_dim(qkv, half * HALF_QKV, HALF_QKV, 1)
    out_half = lax.dynamic_slice_in_dim(out_w, half * HALF_OUT, HALF_OUT, 1)
    out_half = jnp.concatenate([out_half[:, :384], out_half[:, 384:]], axis=0)
    head_half = lax.dynamic_slice_in_dim(head_w, half * 160, 160, 1)
    packed = jnp.concatenate([qkv_half, out_half, head_half], axis=1)
    full = lax.all_gather(packed, ("dp",) + FSDP, axis=0, tiled=True)
    full = full.reshape(2, D, 1696)
    full_qkv = jnp.concatenate([full[0, :, :HALF_QKV], full[1, :, :HALF_QKV]], axis=1)
    out_part = full[:, :, HALF_QKV:1536].reshape(2, 16, 2, 48, 384)
    full_out = out_part.transpose(1, 3, 0, 2, 4).reshape(INNER, D)
    full_head = jnp.concatenate([full[0, :, 1536:], full[1, :, 1536:]], axis=1)
    return full_qkv, full_out, full_head


def reduce_head(head_term):
    core = lax.axis_index("c")
    parts = head_term.reshape(ZS, CORES, 96, HEAD_OUT)
    own = lax.dynamic_index_in_dim(parts, core, 1, keepdims=False)
    other = lax.dynamic_index_in_dim(parts, 1 - core, 1, keepdims=False)
    pair = own + lax.ppermute(other, "c", [(0, 1), (1, 0)])
    pieces = pair.reshape(ZS, 16, 6, HEAD_OUT).transpose(1, 0, 2, 3).astype(jnp.bfloat16)
    pieces = lax.all_to_all(pieces, TILE, 0, 0, tiled=True)
    over_tile = jnp.sum(pieces.astype(jnp.float32), axis=0)
    both = jnp.broadcast_to(over_tile[None], (2, ZS, 6, HEAD_OUT)).reshape(2 * ZS, 6, HEAD_OUT)
    both = lax.all_to_all(both, ("dp", "z"), 0, 0, tiled=True)
    total = jnp.sum(both, axis=0)
    spread = jnp.broadcast_to(total[None], (16, 6, HEAD_OUT))
    return lax.all_to_all(spread, TILE, 0, 0, tiled=True).reshape(96, HEAD_OUT)


def shards(tokens, norm_gain, query_key_value_weight, out_weight, head_weight, coarse, grad_fine):
    lat_rows = tokens.shape[1]
    lon_cols = tokens.shape[2]
    row_count = lat_rows * lon_cols
    flattened_rows = tokens[0].reshape(row_count, D).astype(jnp.float32)
    standard, inverse_dev = layer_norm(flattened_rows)
    normed = (standard * norm_gain).astype(jnp.bfloat16)
    full_qkv, full_out, full_head = gather_weights(query_key_value_weight, out_weight, head_weight)
    projected = jnp.dot(normed, full_qkv, preferred_element_type=jnp.float32).astype(jnp.bfloat16)
    queries = projected[:, :INNER]
    pairs_local = projected[:, INNER:]
    margin_pairs = with_halo(
        pairs_local.reshape(lat_rows, lon_cols, 2 * INNER), ((TILE, 1),), MARGIN
    )
    keys_values = margin_pairs.reshape(lat_rows * (lon_cols + 2 * MARGIN), 2 * INNER)
    attended, softmax_out = attend_forward(queries, keys_values)
    mixed_out = jnp.dot(attended, full_out, preferred_element_type=jnp.float32)
    hidden = (flattened_rows + mixed_out).astype(jnp.bfloat16)
    head_out = jnp.dot(hidden, full_head, preferred_element_type=jnp.float32)
    fine_head = (
        head_out.reshape(lat_rows, lon_cols, VARS, 4, 4)
        .transpose(2, 0, 3, 1, 4)
        .reshape(VARS, 4 * lat_rows, 4 * lon_cols)
    )
    coarse_padded_grid = with_halo(coarse[0], ((TILE, 2),), 1)
    lat_lower, lat_upper_weight = interp_weights(jnp.arange(4 * lat_rows, dtype=jnp.int32))
    latitude_matrix = build_matrix(
        jnp.clip(lat_lower, 0, lat_rows - 1),
        jnp.clip(lat_lower + 1, 0, lat_rows - 1),
        lat_upper_weight,
        lat_rows,
    )
    lon_lower, lon_upper_weight = interp_weights(jnp.arange(4 * lon_cols, dtype=jnp.int32))
    lon_matrix = build_matrix(lon_lower + 1, lon_lower + 2, lon_upper_weight, lon_cols + 2)
    incomplete_grid = jnp.einsum(
        "lj,kji->kli", latitude_matrix, coarse_padded_grid, precision=lax.Precision.HIGHEST
    )
    residual = jnp.einsum(
        "vrb,cb->vrc", incomplete_grid, lon_matrix, precision=lax.Precision.HIGHEST
    )
    fine_grid = fine_head + residual
    grad_rows = (
        grad_fine[0]
        .reshape(VARS, lat_rows, 4, lon_cols, 4)
        .transpose(1, 3, 0, 2, 4)
        .reshape(row_count, HEAD_OUT)
    )
    grad_rows = grad_rows.astype(jnp.bfloat16)
    head_term = lax.dot_general(
        hidden, grad_rows, (((0,), (0,)), ((), ())), preferred_element_type=jnp.float32
    )
    grad_head = reduce_head(head_term)
    grad_hidden = contract_last(grad_rows, full_head)
    grad_attended = contract_last(grad_hidden.astype(jnp.bfloat16), full_out).astype(jnp.bfloat16)
    grad_queries, pair_gradient_rows = attend_backward(
        softmax_out, queries, keys_values, grad_attended
    )
    pair_gradient_rows = pair_gradient_rows.reshape(lat_rows, lon_cols + 2 * MARGIN, 2 * INNER)
    from_left = from_behind(pair_gradient_rows[:, lon_cols + MARGIN :], TILE, 1)
    from_right = from_behind(pair_gradient_rows[:, :MARGIN], TILE, -1)
    own_cells = pair_gradient_rows[:, MARGIN : MARGIN + lon_cols]
    own_cells = own_cells + jnp.pad(from_left, ((0, 0), (0, lon_cols - MARGIN), (0, 0)))
    own_cells = own_cells + jnp.pad(from_right, ((0, 0), (lon_cols - MARGIN, 0), (0, 0)))
    grad_all = jnp.concatenate(
        [grad_queries, own_cells.reshape(row_count, 2 * INNER).astype(jnp.bfloat16)], axis=1
    )
    grad_normed = contract_last(grad_all, full_qkv)
    grad_input = grad_hidden + norm_backward(grad_normed, standard, inverse_dev, norm_gain)
    grad_tokens = grad_input.astype(jnp.bfloat16).reshape(1, lat_rows, lon_cols, D)
    return (fine_grid[None], grad_tokens, grad_head)


def solution(mesh):
    fine_mesh = Mesh(mesh.devices.reshape(2, ZS, CORES, YS, XS), ("dp", "z", "c", "y", "x"))
    samples = ("dp", "z", "c")
    placed = (
        P(samples, None, TILE, None),
        P(),
        P(FSDP, None),
        P(FSDP, None),
        P(FSDP, None),
        P(samples, None, None, TILE),
        P(samples, None, None, TILE),
    )
    return jax.shard_map(
        shards,
        mesh=fine_mesh,
        in_specs=placed,
        out_specs=(P(samples, None, None, TILE), P(samples, None, TILE, None), P(FSDP, None)),
        check_vma=False,
    )
```

```python
import functools
import jax
import jax.numpy as jnp
from jax import lax
from jax.experimental import pallas as pl
from jax.experimental.pallas import tpu as pltpu
from jax.sharding import Mesh
from jax.sharding import PartitionSpec as P

D = 1536
HEADS = 8
HEAD_DIM = 96
VARS = 20
MARGIN = 8
LAT = 8
LON_DEV = 32
INNER = 768
HEAD_OUT = 320
ROWS = 256
EDGE = 64
GROUP = 384
PAIR = 2 * INNER
ZS = 8
CORES = 2
YS = 4
XS = 4
TILES = 16
FSDP = ("z", "c")
TILE = ("y", "x")
HALF_QKV = 1152
HALF_OUT = 768
PACKED = 1696
PHASES = 4
CHANNELS = 80
LANES = 128
PADDED = PHASES * LANES
EPSILON = 1e-05
SCALE = HEAD_DIM ** (-0.5)
F32 = jnp.float32
BF16 = jnp.bfloat16
WHOLE = pl.BlockSpec(memory_space=pltpu.VMEM)


def dot(left, right):
    return lax.dot_general(left, right, (((1,), (0,)), ((), ())), preferred_element_type=F32)


def dot_last(left, right):
    return lax.dot_general(left, right, (((1,), (1,)), ((), ())), preferred_element_type=F32)


def dot_first(left, right):
    return lax.dot_general(left, right, (((0,), (0,)), ((), ())), preferred_element_type=F32)


def spread_matrix():
    row = lax.broadcasted_iota(jnp.int32, (LANES, LANES), 0)
    lane = lax.broadcasted_iota(jnp.int32, (LANES, LANES), 1)
    target = (row % LON_DEV) * PHASES + row // LON_DEV
    return jnp.where(lane == target, 1.0, 0.0).astype(BF16)


def prepare_kernel(tokens_ref, gain_ref, fine_ref, normed_ref, rows_ref):
    values = tokens_ref[...].astype(F32)
    average = jnp.mean(values, axis=-1, keepdims=True)
    centred = values - average
    variance = jnp.mean(centred * centred, axis=-1, keepdims=True)
    standard = centred * lax.rsqrt(variance + EPSILON)
    normed_ref[...] = (standard * gain_ref[...]).astype(BF16)
    select = spread_matrix()
    empty = jnp.zeros((LANES - CHANNELS, LANES), BF16)
    for lat in range(LAT):
        block = fine_ref[:, PHASES * lat : PHASES * (lat + 1), :].reshape(CHANNELS, LANES)
        block = jnp.concatenate([block.astype(BF16), empty], axis=0)
        picked = dot_last(select, block).astype(BF16)
        for phase in range(PHASES):
            rows_ref[lat * LON_DEV : (lat + 1) * LON_DEV, phase * LANES : (phase + 1) * LANES] = picked[
                phase * LON_DEV : (phase + 1) * LON_DEV
            ]


def prepare(tokens, gain, grad_fine):
    return pl.pallas_call(
        prepare_kernel,
        out_shape=(
            jax.ShapeDtypeStruct((ROWS, D), BF16),
            jax.ShapeDtypeStruct((ROWS, PADDED), BF16),
        ),
        in_specs=[WHOLE, WHOLE, WHOLE],
        out_specs=(WHOLE, WHOLE),
        name="prepare",
    )(tokens, gain, grad_fine)


def project_kernel(normed_ref, weight_ref, out_ref):
    out_ref[...] = dot(normed_ref[...], weight_ref[0]).astype(BF16)


def project(normed, full, first, count):
    return pl.pallas_call(
        project_kernel,
        out_shape=jax.ShapeDtypeStruct((ROWS, count * GROUP), BF16),
        grid=(count,),
        in_specs=[
            pl.BlockSpec((ROWS, D), lambda n: (0, 0)),
            pl.BlockSpec((1, D, GROUP), lambda n: ((n + first) // 3, 0, (n + first) % 3)),
        ],
        out_specs=pl.BlockSpec((ROWS, GROUP), lambda n: (0, n)),
        name="project",
    )(normed, full)


def out_quarter(weight_ref, part):
    block = weight_ref[0].reshape(16, 2, 48, GROUP)[:, part]
    return block.reshape(INNER, GROUP)


def hidden_grad_kernel(rows_ref, head_ref, low_out_ref, up_out_ref, hidden_ref, attended_ref):
    rows = rows_ref[...]
    grad_hidden = dot_last(rows[:, :256], head_ref[0]) + dot_last(rows[:, 256:], head_ref[1])
    hidden_ref[...] = grad_hidden
    low = grad_hidden.astype(BF16)
    total = None
    for quarter in range(4):
        weight = out_quarter(low_out_ref if quarter < 2 else up_out_ref, quarter % 2)
        term = dot_last(low[:, quarter * GROUP : (quarter + 1) * GROUP], weight)
        total = term if total is None else total + term
    attended_ref[...] = total.astype(BF16)


def out_specs_of(count):
    low = pl.BlockSpec((1, D, GROUP), lambda n: (0, 0, 3))
    up = pl.BlockSpec((1, D, GROUP), lambda n: (1, 0, 3))
    return [low, up][:count]


def whole_block(shape):
    return pl.BlockSpec(shape, lambda n: (0,) * len(shape))


def hidden_grad(rows, head, full):
    return pl.pallas_call(
        hidden_grad_kernel,
        out_shape=(
            jax.ShapeDtypeStruct((ROWS, D), F32),
            jax.ShapeDtypeStruct((ROWS, INNER), BF16),
        ),
        grid=(1,),
        in_specs=[whole_block((ROWS, PADDED)), whole_block((2, D, 256))] + out_specs_of(2),
        out_specs=(whole_block((ROWS, D)), whole_block((ROWS, INNER))),
        name="hidden_grad",
    )(rows, head, full, full)


def head_window(head):
    first = head * HEAD_DIM // LANES * LANES
    last = -(-(head + 1) * HEAD_DIM // LANES) * LANES
    lane = lax.broadcasted_iota(jnp.int32, (1, last - first), 1) + first
    inside = (lane >= head * HEAD_DIM) & (lane < (head + 1) * HEAD_DIM)
    return first, last, inside


def masked(values, inside):
    return jnp.where(inside, values, jnp.zeros_like(values))


def softmax_of(query, key):
    scores = dot_last(query, key) * SCALE
    biggest = jnp.max(scores, axis=-1, keepdims=True)
    exponent = jnp.exp(scores - biggest)
    return exponent / jnp.sum(exponent, axis=-1, keepdims=True)


def joined(own_ref, left_ref, right_ref):
    return jnp.concatenate([own_ref[...], left_ref[...], right_ref[...]], axis=0)


def forward_kernel(q_ref, k_ref, v_ref, kl_ref, vl_ref, kr_ref, vr_ref, out_ref):
    queries = q_ref[...]
    keys = joined(k_ref, kl_ref, kr_ref)
    values = joined(v_ref, vl_ref, vr_ref)
    parts = [None, None, None]
    for head in range(4):
        first, last, inside = head_window(head)
        softmax = softmax_of(masked(queries[:, first:last], inside), keys[:, first:last])
        result = dot(softmax.astype(BF16), masked(values[:, first:last], inside))
        for tile in range(first // LANES, last // LANES):
            piece = result[:, tile * LANES - first : (tile + 1) * LANES - first]
            parts[tile] = piece if parts[tile] is None else parts[tile] + piece
    for tile in range(3):
        out_ref[:, tile * LANES : (tile + 1) * LANES] = parts[tile].astype(BF16)


def attention_specs():
    def spec(rows, offset):
        return pl.BlockSpec((rows, GROUP), lambda n: (0, n + offset))

    return [spec(ROWS, 0), spec(ROWS, 0), spec(ROWS, 2), spec(EDGE, 0), spec(EDGE, 2), spec(EDGE, 0), spec(EDGE, 2)]


def attend_forward(queries, pairs, left, right):
    return pl.pallas_call(
        forward_kernel,
        out_shape=jax.ShapeDtypeStruct((ROWS, INNER), BF16),
        grid=(2,),
        in_specs=attention_specs(),
        out_specs=pl.BlockSpec((ROWS, GROUP), lambda n: (0, n)),
        name="attend_forward",
    )(queries, pairs, pairs, left, left, right, right)


def backward_kernel(
    q_ref, k_ref, v_ref, kl_ref, vl_ref, kr_ref, vr_ref, grad_ref,
    dq_ref, dk_ref, dv_ref, dkl_ref, dvl_ref, dkr_ref, dvr_ref,
):
    queries = q_ref[...]
    grads = grad_ref[...]
    keys = joined(k_ref, kl_ref, kr_ref)
    values = joined(v_ref, vl_ref, vr_ref)
    sums = [[None, None, None] for _ in range(3)]
    for head in range(4):
        first, last, inside = head_window(head)
        query = masked(queries[:, first:last], inside)
        grad = masked(grads[:, first:last], inside)
        softmax = softmax_of(query, keys[:, first:last])
        grad_weights = dot_last(grad, values[:, first:last])
        weighted = jnp.sum(softmax * grad_weights, axis=-1, keepdims=True)
        grad_scores = (softmax * (grad_weights - weighted)).astype(BF16)
        results = (
            dot(grad_scores, masked(keys[:, first:last], inside)),
            dot_first(grad_scores, query),
            dot_first(softmax.astype(BF16), grad),
        )
        for kept, result in zip(sums, results):
            for tile in range(first // LANES, last // LANES):
                piece = result[:, tile * LANES - first : (tile + 1) * LANES - first]
                kept[tile] = piece if kept[tile] is None else kept[tile] + piece
    for tile in range(3):
        at = slice(tile * LANES, (tile + 1) * LANES)
        dq_ref[:, at] = (sums[0][tile] * SCALE).astype(BF16)
        grad_keys = sums[1][tile] * SCALE
        grad_values = sums[2][tile]
        for grads_of, own, left, right in (
            (grad_keys, dk_ref, dkl_ref, dkr_ref),
            (grad_values, dv_ref, dvl_ref, dvr_ref),
        ):
            own[:, at] = grads_of[:ROWS]
            left[:, at] = grads_of[ROWS : ROWS + EDGE]
            right[:, at] = grads_of[ROWS + EDGE :]


def attend_backward(queries, pairs, left, right, grad_attended):
    def block(rows):
        return pl.BlockSpec((rows, GROUP), lambda n: (0, n))

    def shape(rows, kind):
        return jax.ShapeDtypeStruct((rows, INNER), kind)

    return pl.pallas_call(
        backward_kernel,
        out_shape=(
            shape(ROWS, BF16),
            shape(ROWS, F32),
            shape(ROWS, F32),
            shape(EDGE, F32),
            shape(EDGE, F32),
            shape(EDGE, F32),
            shape(EDGE, F32),
        ),
        grid=(2,),
        in_specs=attention_specs() + [block(ROWS)],
        out_specs=(block(ROWS), block(ROWS), block(ROWS), block(EDGE), block(EDGE), block(EDGE), block(EDGE)),
        name="attend_backward",
    )(queries, pairs, pairs, left, left, right, right, grad_attended)


def hidden_kernel(
    tokens_ref, attended_ref, low_out_ref, up_out_ref, head_ref, rows_ref, residual_ref, fine_ref, pieces_ref
):
    attended = attended_ref[...]
    rows = rows_ref[...]
    head_out = [None, None]
    for quarter in range(4):
        weight = out_quarter(low_out_ref if quarter < 2 else up_out_ref, quarter % 2)
        at = slice(quarter * GROUP, (quarter + 1) * GROUP)
        hidden = (tokens_ref[:, at].astype(F32) + dot(attended, weight)).astype(BF16)
        for half in range(2):
            term = dot(hidden, head_ref[half, at, :])
            head_out[half] = term if head_out[half] is None else head_out[half] + term
        products = dot_first(hidden, rows).astype(BF16)
        for fsdp in range(4):
            place = quarter * 4 + fsdp
            for quad in range(4):
                top = fsdp * 96 + quad * 24
                for phase in range(PHASES):
                    pieces_ref[place % 2, quad * 4 + phase, place // 2] = products[
                        top : top + 24, phase * LANES : (phase + 1) * LANES
                    ]
    select = spread_matrix()
    for lat in range(LAT):
        at = slice(lat * LON_DEV, (lat + 1) * LON_DEV)
        stacked = jnp.concatenate(
            [head_out[phase // 2][at, phase % 2 * LANES : (phase % 2 + 1) * LANES] for phase in range(PHASES)],
            axis=0,
        )
        high = stacked.astype(BF16)
        low = (stacked - high.astype(F32)).astype(BF16)
        spread = dot_first(high, select) + dot_first(low, select)
        across = slice(PHASES * lat, PHASES * (lat + 1))
        fine_ref[:, across, :] = spread[:CHANNELS].reshape(VARS, PHASES, LANES) + residual_ref[:, across, :]


def hidden_and_head(tokens, attended, full, head, rows, residual):
    pieces = (CORES, TILES, ZS, 24, LANES)
    return pl.pallas_call(
        hidden_kernel,
        out_shape=(
            jax.ShapeDtypeStruct((VARS, 4 * LAT, LANES), F32),
            jax.ShapeDtypeStruct(pieces, BF16),
        ),
        grid=(1,),
        in_specs=[whole_block((ROWS, D)), whole_block((ROWS, INNER))]
        + out_specs_of(2)
        + [whole_block((2, D, 256)), whole_block((ROWS, PADDED)), whole_block((VARS, 4 * LAT, LANES))],
        out_specs=(whole_block((VARS, 4 * LAT, LANES)), whole_block(pieces)),
        name="hidden_and_head",
    )(tokens, attended, full, full, head, rows, residual)


def norm_grad_kernel(
    dq_ref, dk_ref, dv_ref, kl_ref, vl_ref, kr_ref, vr_ref, weight_ref, tokens_ref, gain_ref, hidden_ref, out_ref, total
):
    step = pl.program_id(0)

    def add(grad):
        term = dot_last(grad, weight_ref[0])

        @pl.when(step == 0)
        def _():
            total[...] = term

        @pl.when(step > 0)
        def _():
            total[...] += term

    def with_edges(own_ref, left_ref, right_ref):
        own = own_ref[...].reshape(LAT, LON_DEV, GROUP)
        left = left_ref[...].reshape(LAT, MARGIN, GROUP)
        right = right_ref[...].reshape(LAT, MARGIN, GROUP)
        own = jnp.concatenate(
            [own[:, :MARGIN] + left, own[:, MARGIN : LON_DEV - MARGIN], own[:, LON_DEV - MARGIN :] + right], axis=1
        )
        return own.reshape(ROWS, GROUP).astype(BF16)

    @pl.when(step < 2)
    def _():
        add(dq_ref[...])

    @pl.when((step >= 2) & (step < 4))
    def _():
        add(with_edges(dk_ref, kl_ref, kr_ref))

    @pl.when(step >= 4)
    def _():
        add(with_edges(dv_ref, vl_ref, vr_ref))

    @pl.when(step == 5)
    def _():
        values = tokens_ref[...].astype(F32)
        average = jnp.mean(values, axis=-1, keepdims=True)
        centred = values - average
        variance = jnp.mean(centred * centred, axis=-1, keepdims=True)
        inverse_dev = lax.rsqrt(variance + EPSILON)
        standard = centred * inverse_dev
        grad_standard = total[...] * gain_ref[...]
        first_mean = jnp.mean(grad_standard, axis=-1, keepdims=True)
        second_mean = jnp.mean(grad_standard * standard, axis=-1, keepdims=True)
        grad = inverse_dev * (grad_standard - first_mean - standard * second_mean)
        out_ref[...] = (hidden_ref[...] + grad).astype(BF16)


def norm_grad(dq, dk, dv, from_left, from_right, full, tokens, gain, grad_hidden):
    def spec(rows, first, offset):
        return pl.BlockSpec((rows, GROUP), lambda n: (0, jnp.clip(n - first, 0, 1) + offset))

    return pl.pallas_call(
        norm_grad_kernel,
        out_shape=jax.ShapeDtypeStruct((ROWS, D), BF16),
        grid=(6,),
        in_specs=[
            spec(ROWS, 0, 0),
            spec(ROWS, 2, 0),
            spec(ROWS, 4, 0),
            spec(EDGE, 2, 0),
            spec(EDGE, 4, 2),
            spec(EDGE, 2, 0),
            spec(EDGE, 4, 2),
            pl.BlockSpec((1, D, GROUP), lambda n: (n // 3, 0, n % 3)),
            whole_block((ROWS, D)),
            whole_block((1, D)),
            whole_block((ROWS, D)),
        ],
        out_specs=whole_block((ROWS, D)),
        scratch_shapes=[pltpu.VMEM((ROWS, D), F32)],
        name="norm_grad",
    )(dq, dk, dv, from_left, from_left, from_right, from_right, full, tokens, gain, grad_hidden)


def interp_weights(fine_index):
    coarse_cell = fine_index // 4
    phase_index = fine_index % 4
    lower_shift = (phase_index < 2).astype(jnp.int32)
    upper_weight = (2 * phase_index - 3 + 8 * lower_shift).astype(F32) / 8.0
    return (coarse_cell - lower_shift, upper_weight)


def build_matrix(lower_cell, upper_cell, upper_weight, count):
    columns = jnp.arange(count, dtype=jnp.int32)
    lower_part = jnp.where(columns[None, :] == lower_cell[:, None], 1.0 - upper_weight[:, None], 0.0)
    upper_portion = jnp.where(columns[None, :] == upper_cell[:, None], upper_weight[:, None], 0.0)
    return lower_part + upper_portion


def shifted(value, steps):
    return lax.ppermute(value, TILE, [(i, (i + steps) % TILES) for i in range(TILES)])


def residual_of(coarse):
    before = shifted(coarse[:, :, -1:], 1)
    after = shifted(coarse[:, :, :1], -1)
    padded = jnp.concatenate([before, coarse, after], axis=2)
    lat_lower, lat_upper_weight = interp_weights(jnp.arange(4 * LAT, dtype=jnp.int32))
    latitude_matrix = build_matrix(
        jnp.clip(lat_lower, 0, LAT - 1), jnp.clip(lat_lower + 1, 0, LAT - 1), lat_upper_weight, LAT
    )
    lon_lower, lon_upper_weight = interp_weights(jnp.arange(4 * LON_DEV, dtype=jnp.int32))
    lon_matrix = build_matrix(lon_lower + 1, lon_lower + 2, lon_upper_weight, LON_DEV + 2)
    incomplete_grid = jnp.einsum("lj,kji->kli", latitude_matrix, padded, precision=lax.Precision.HIGHEST)
    return jnp.einsum("vrb,cb->vrc", incomplete_grid, lon_matrix, precision=lax.Precision.HIGHEST)


def head_columns():
    target = jnp.arange(PADDED, dtype=jnp.int32)
    phase, channel = target // LANES, target % LANES
    source = jnp.where(channel < CHANNELS, channel * PHASES + phase, -1)
    return (jnp.arange(HEAD_OUT, dtype=jnp.int32)[:, None] == source[None, :]).astype(F32)


def gather_weights(qkv, out_w, head_w):
    half = lax.axis_index("dp")
    qkv_half = lax.dynamic_slice_in_dim(qkv, half * HALF_QKV, HALF_QKV, 1)
    out_half = lax.dynamic_slice_in_dim(out_w, half * HALF_OUT, HALF_OUT, 1)
    out_half = jnp.concatenate([out_half[:, :GROUP], out_half[:, GROUP:]], axis=0)
    head_half = lax.dynamic_slice_in_dim(head_w, half * 160, 160, 1)
    packed = jnp.concatenate([qkv_half, out_half, head_half], axis=1)
    full = lax.all_gather(packed, ("dp",) + FSDP, axis=0, tiled=True)
    return full.reshape(2, D, PACKED)


def head_of(full):
    columns = head_columns().astype(BF16)
    low = full[0, :, 4 * GROUP :]
    up = full[1, :, 4 * GROUP :]
    parts = [
        (dot(low, columns[:160, at : at + 256]) + dot(up, columns[160:, at : at + 256])).astype(BF16)
        for at in (0, 256)
    ]
    return jnp.stack(parts)


def reduce_head(pieces):
    pieces = lax.all_to_all(pieces.reshape(CORES * TILES, ZS, 24, LANES), ("c",) + TILE, 0, 0, tiled=True)
    over_tile = jnp.sum(pieces.astype(F32), axis=0)
    both = jnp.broadcast_to(over_tile[None], (2, ZS, 24, LANES)).reshape(2 * ZS, 24, LANES)
    both = lax.all_to_all(both, ("dp", "z"), 0, 0, tiled=True)
    total = jnp.sum(both, axis=0)
    spread = jnp.broadcast_to(total[None], (TILES, 24, LANES))
    spread = lax.all_to_all(spread, TILE, 0, 0, tiled=True)
    padded = spread.reshape(4, PHASES, 24, LANES).transpose(0, 2, 1, 3).reshape(96, PADDED)
    return lax.dot_general(
        padded, head_columns(), (((1,), (1,)), ((), ())), precision=lax.Precision.HIGHEST, preferred_element_type=F32
    )


def local_edges(pairs):
    grid = pairs.reshape(LAT, LON_DEV, PAIR)
    return grid[:, :MARGIN].reshape(EDGE, PAIR), grid[:, LON_DEV - MARGIN :].reshape(EDGE, PAIR)


def shards(tokens, norm_gain, query_key_value_weight, out_weight, head_weight, coarse, grad_fine):
    tokens = tokens[0].reshape(ROWS, D)
    gain = norm_gain.reshape(1, D)
    full = gather_weights(query_key_value_weight, out_weight, head_weight)
    residual = residual_of(coarse[0])
    normed, rows = prepare(tokens, gain, grad_fine[0])
    pairs = project(normed, full, 2, 4)
    leading, last = local_edges(pairs)
    left = shifted(last, 1)
    right = shifted(leading, -1)
    normed_later = lax.optimization_barrier((normed, pairs))[0]
    queries = project(normed_later, full, 0, 2)
    head = head_of(full)
    grad_hidden, grad_attended = hidden_grad(rows, head, full)
    attended = attend_forward(queries, pairs, left, right)
    fine_grid, pieces = hidden_and_head(tokens, attended, full, head, rows, residual)
    grad_head = reduce_head(pieces)
    dq, dk, dv, dkl, dvl, dkr, dvr = attend_backward(queries, pairs, left, right, grad_attended)
    from_right = shifted(jnp.concatenate([dkl, dvl], axis=1), -1)
    from_left = shifted(jnp.concatenate([dkr, dvr], axis=1), 1)
    grad_tokens = norm_grad(dq, dk, dv, from_left, from_right, full, tokens, gain, grad_hidden)
    return (fine_grid[None], grad_tokens.reshape(1, LAT, LON_DEV, D), grad_head)


def solution(mesh):
    fine_mesh = Mesh(mesh.devices.reshape(2, ZS, CORES, YS, XS), ("dp", "z", "c", "y", "x"))
    samples = ("dp", "z", "c")
    placed = (
        P(samples, None, TILE, None),
        P(),
        P(FSDP, None),
        P(FSDP, None),
        P(FSDP, None),
        P(samples, None, None, TILE),
        P(samples, None, None, TILE),
    )
    return jax.shard_map(
        shards,
        mesh=fine_mesh,
        in_specs=placed,
        out_specs=(P(samples, None, None, TILE), P(samples, None, TILE, None), P(FSDP, None)),
        check_vma=False,
    )
```

```python
import functools
import jax
import jax.numpy as jnp
from jax import lax
from jax.experimental import pallas as pl
from jax.experimental.pallas import tpu as pltpu
from jax.sharding import Mesh
from jax.sharding import PartitionSpec as P

D = 1536
HEADS = 8
HEAD_DIM = 96
VARS = 20
MARGIN = 8
LAT = 8
LON_DEV = 32
INNER = 768
HEAD_OUT = 320
ROWS = 256
EDGE = 64
GROUP = 384
PAIR = 2 * INNER
ZS = 8
CORES = 2
YS = 4
XS = 4
TILES = 16
FSDP = ("z", "c")
TILE = ("y", "x")
HALF_QKV = 1152
HALF_OUT = 768
PIECE = 64
WIDE = ZS * 80
PHASES = 4
CHANNELS = 80
LANES = 128
PADDED = PHASES * LANES
EPSILON = 1e-05
SCALE = HEAD_DIM ** (-0.5)
F32 = jnp.float32
BF16 = jnp.bfloat16
WHOLE = pl.BlockSpec(memory_space=pltpu.VMEM)


def dot(left, right):
    return lax.dot_general(left, right, (((1,), (0,)), ((), ())), preferred_element_type=F32)


def dot_last(left, right):
    return lax.dot_general(left, right, (((1,), (1,)), ((), ())), preferred_element_type=F32)


def dot_first(left, right):
    return lax.dot_general(left, right, (((0,), (0,)), ((), ())), preferred_element_type=F32)


def spread_matrix():
    row = lax.broadcasted_iota(jnp.int32, (LANES, LANES), 0)
    lane = lax.broadcasted_iota(jnp.int32, (LANES, LANES), 1)
    target = (row % LON_DEV) * PHASES + row // LON_DEV
    return jnp.where(lane == target, 1.0, 0.0).astype(BF16)


def prepare_kernel(tokens_ref, gain_ref, fine_ref, normed_ref, rows_ref):
    values = tokens_ref[...].astype(F32)
    average = jnp.mean(values, axis=-1, keepdims=True)
    centred = values - average
    variance = jnp.mean(centred * centred, axis=-1, keepdims=True)
    standard = centred * lax.rsqrt(variance + EPSILON)
    normed_ref[...] = (standard * gain_ref[...]).astype(BF16)
    select = spread_matrix()
    empty = jnp.zeros((LANES - CHANNELS, LANES), BF16)
    for lat in range(LAT):
        block = fine_ref[:, PHASES * lat : PHASES * (lat + 1), :].reshape(CHANNELS, LANES)
        block = jnp.concatenate([block.astype(BF16), empty], axis=0)
        picked = dot_last(select, block).astype(BF16)
        for phase in range(PHASES):
            rows_ref[lat * LON_DEV : (lat + 1) * LON_DEV, phase * LANES : (phase + 1) * LANES] = picked[
                phase * LON_DEV : (phase + 1) * LON_DEV
            ]


def prepare(tokens, gain, grad_fine):
    return pl.pallas_call(
        prepare_kernel,
        out_shape=(
            jax.ShapeDtypeStruct((ROWS, D), BF16),
            jax.ShapeDtypeStruct((ROWS, PADDED), BF16),
        ),
        in_specs=[WHOLE, WHOLE, WHOLE],
        out_specs=(WHOLE, WHOLE),
        name="prepare",
    )(tokens, gain, grad_fine)


def project_kernel(normed_ref, weight_ref, out_ref):
    out_ref[...] = dot(normed_ref[...], weight_ref[0]).astype(BF16)


def project_pairs_kernel(normed_ref, weight_ref, out_ref, leading_ref, last_ref):
    values = dot(normed_ref[...], weight_ref[0])
    out_ref[...] = values.astype(BF16)
    grid = values.reshape(LAT, LON_DEV, GROUP)
    leading_ref[...] = grid[:, :MARGIN].reshape(EDGE, GROUP).astype(BF16)
    last_ref[...] = grid[:, LON_DEV - MARGIN :].reshape(EDGE, GROUP).astype(BF16)


def project_specs(first):
    return [
        pl.BlockSpec((ROWS, D), lambda n: (0, 0)),
        pl.BlockSpec((1, D, GROUP), lambda n: ((n + first) // 3, 0, (n + first) % 3)),
    ]


def project(normed, full):
    return pl.pallas_call(
        project_kernel,
        out_shape=jax.ShapeDtypeStruct((ROWS, INNER), BF16),
        grid=(2,),
        in_specs=project_specs(0),
        out_specs=pl.BlockSpec((ROWS, GROUP), lambda n: (0, n)),
        name="project",
    )(normed, full)


def project_pairs(normed, full):
    edge = jax.ShapeDtypeStruct((EDGE, PAIR), BF16)
    return pl.pallas_call(
        project_pairs_kernel,
        out_shape=(jax.ShapeDtypeStruct((ROWS, PAIR), BF16), edge, edge),
        grid=(4,),
        in_specs=project_specs(2),
        out_specs=(
            pl.BlockSpec((ROWS, GROUP), lambda n: (0, n)),
            pl.BlockSpec((EDGE, GROUP), lambda n: (0, n)),
            pl.BlockSpec((EDGE, GROUP), lambda n: (0, n)),
        ),
        name="project_pairs",
    )(normed, full)


def unpack_kernel(pieces_ref, out_ref, head_ref):
    for core in range(CORES):
        for z in range(ZS):
            shard = z * CORES + core
            for tile in range(60):
                block = pieces_ref[core, tile // 4, z, tile % 4 * 16 : (tile % 4 + 1) * 16, :]
                if tile < 36:
                    top = shard * 48 + tile % 3 * 16
                    out_ref[top : top + 16, tile // 3 * LANES : (tile // 3 + 1) * LANES] = block
                else:
                    top = shard * 96 + tile % 6 * 16
                    phase = (tile - 36) // 6
                    head_ref[top : top + 16, phase * LANES : (phase + 1) * LANES] = block


def unpack(pieces):
    return pl.pallas_call(
        unpack_kernel,
        out_shape=(
            jax.ShapeDtypeStruct((INNER, D), BF16),
            jax.ShapeDtypeStruct((D, PADDED), BF16),
        ),
        in_specs=[WHOLE],
        out_specs=(WHOLE, WHOLE),
        name="unpack",
    )(pieces)


def hidden_grad_kernel(rows_ref, head_ref, out_ref, hidden_ref, attended_ref):
    grad_hidden = dot_last(rows_ref[...], head_ref[...])
    hidden_ref[...] = grad_hidden
    attended_ref[...] = dot_last(grad_hidden.astype(BF16), out_ref[...]).astype(BF16)


def hidden_grad(rows, head, out_weight):
    return pl.pallas_call(
        hidden_grad_kernel,
        out_shape=(
            jax.ShapeDtypeStruct((ROWS, D), F32),
            jax.ShapeDtypeStruct((ROWS, INNER), BF16),
        ),
        in_specs=[WHOLE, WHOLE, WHOLE],
        out_specs=(WHOLE, WHOLE),
        name="hidden_grad",
    )(rows, head, out_weight)


def whole_block(shape):
    return pl.BlockSpec(shape, lambda n: (0,) * len(shape))


def head_window(head):
    first = head * HEAD_DIM // LANES * LANES
    last = -(-(head + 1) * HEAD_DIM // LANES) * LANES
    lane = lax.broadcasted_iota(jnp.int32, (1, last - first), 1) + first
    inside = (lane >= head * HEAD_DIM) & (lane < (head + 1) * HEAD_DIM)
    return first, last, inside


def masked(values, inside):
    return jnp.where(inside, values, jnp.zeros_like(values))


def softmax_of(query, key):
    scores = dot_last(query, key) * SCALE
    biggest = jnp.max(scores, axis=-1, keepdims=True)
    exponent = jnp.exp(scores - biggest)
    return exponent / jnp.sum(exponent, axis=-1, keepdims=True)


def joined(own_ref, left_ref, right_ref):
    return jnp.concatenate([own_ref[...], left_ref[...], right_ref[...]], axis=0)


def forward_group(q_ref, k_ref, v_ref, kl_ref, vl_ref, kr_ref, vr_ref):
    queries = q_ref[...]
    keys = joined(k_ref, kl_ref, kr_ref)
    values = joined(v_ref, vl_ref, vr_ref)
    parts = [None, None, None]
    for head in range(4):
        first, last, inside = head_window(head)
        softmax = softmax_of(masked(queries[:, first:last], inside), keys[:, first:last])
        result = dot(softmax.astype(BF16), masked(values[:, first:last], inside))
        for tile in range(first // LANES, last // LANES):
            piece = result[:, tile * LANES - first : (tile + 1) * LANES - first]
            parts[tile] = piece if parts[tile] is None else parts[tile] + piece
    return jnp.concatenate([part.astype(BF16) for part in parts], axis=1)


def forward_kernel(
    q_ref, k_ref, v_ref, kl_ref, vl_ref, kr_ref, vr_ref,
    tokens_hbm, out_hbm, head_hbm, rows_hbm, residual_hbm,
    fine_ref, pieces_ref,
    attended, tokens_ref, out_ref, head_ref, rows_ref, residual_ref, products, sems,
):
    step = pl.program_id(0)
    copies = [
        pltpu.make_async_copy(source, target, sems.at[place])
        for place, (source, target) in enumerate(
            (
                (tokens_hbm, tokens_ref),
                (out_hbm, out_ref),
                (head_hbm, head_ref),
                (rows_hbm, rows_ref),
                (residual_hbm, residual_ref),
            )
        )
    ]

    @pl.when(step == 0)
    def _():
        for copy in copies:
            copy.start()

    attended[step] = forward_group(q_ref, k_ref, v_ref, kl_ref, vl_ref, kr_ref, vr_ref)

    @pl.when(step == 1)
    def _():
        for copy in copies:
            copy.wait()
        mixed = dot(attended[0], out_ref[:GROUP]) + dot(attended[1], out_ref[GROUP:])
        hidden = (tokens_ref[...].astype(F32) + mixed).astype(BF16)
        head_out = dot(hidden, head_ref[...])
        products[...] = dot_first(hidden, rows_ref[...])
        for core in range(CORES):
            for quad in range(4):
                for phase in range(PHASES):
                    row = [
                        products[
                            (z * CORES + core) * 96 + quad * 24 : (z * CORES + core) * 96 + quad * 24 + 24,
                            phase * LANES : phase * LANES + CHANNELS,
                        ]
                        for z in range(ZS)
                    ]
                    pieces_ref[core * TILES + quad * 4 + phase] = jnp.concatenate(row, axis=1).astype(BF16)
        select = spread_matrix()
        for lat in range(LAT):
            at = slice(lat * LON_DEV, (lat + 1) * LON_DEV)
            stacked = jnp.concatenate(
                [head_out[at, phase * LANES : (phase + 1) * LANES] for phase in range(PHASES)], axis=0
            )
            high = stacked.astype(BF16)
            low = (stacked - high.astype(F32)).astype(BF16)
            spread = dot_first(high, select) + dot_first(low, select)
            across = slice(PHASES * lat, PHASES * (lat + 1))
            fine_ref[:, across, :] = spread[:CHANNELS].reshape(VARS, PHASES, LANES) + residual_ref[:, across, :]


def attention_specs():
    def spec(rows, offset):
        return pl.BlockSpec((rows, GROUP), lambda n: (0, n + offset))

    return [spec(ROWS, 0), spec(ROWS, 0), spec(ROWS, 2), spec(EDGE, 0), spec(EDGE, 2), spec(EDGE, 0), spec(EDGE, 2)]


def forward(queries, pairs, left, right, tokens, out_weight, head, rows, residual):
    fine = (VARS, 4 * LAT, LANES)
    pieces = (CORES * TILES, 24, WIDE)
    return pl.pallas_call(
        forward_kernel,
        out_shape=(jax.ShapeDtypeStruct(fine, F32), jax.ShapeDtypeStruct(pieces, BF16)),
        grid=(2,),
        in_specs=attention_specs() + [pl.BlockSpec(memory_space=pl.ANY)] * 5,
        out_specs=(whole_block(fine), whole_block(pieces)),
        scratch_shapes=[
            pltpu.VMEM((2, ROWS, GROUP), BF16),
            pltpu.VMEM((ROWS, D), BF16),
            pltpu.VMEM((INNER, D), BF16),
            pltpu.VMEM((D, PADDED), BF16),
            pltpu.VMEM((ROWS, PADDED), BF16),
            pltpu.VMEM(fine, F32),
            pltpu.VMEM((D, PADDED), F32),
            pltpu.SemaphoreType.DMA((5,)),
        ],
        name="forward",
    )(queries, pairs, pairs, left, left, right, right, tokens, out_weight, head, rows, residual)


def backward_kernel(
    q_ref, k_ref, v_ref, kl_ref, vl_ref, kr_ref, vr_ref, grad_ref,
    dq_ref, dk_ref, dv_ref, left_ref, right_ref,
):
    queries = q_ref[...]
    grads = grad_ref[...]
    keys = joined(k_ref, kl_ref, kr_ref)
    values = joined(v_ref, vl_ref, vr_ref)
    sums = [[None, None, None] for _ in range(3)]
    for head in range(4):
        first, last, inside = head_window(head)
        query = masked(queries[:, first:last], inside)
        grad = masked(grads[:, first:last], inside)
        softmax = softmax_of(query, keys[:, first:last])
        grad_weights = dot_last(grad, values[:, first:last])
        weighted = jnp.sum(softmax * grad_weights, axis=-1, keepdims=True)
        grad_scores = (softmax * (grad_weights - weighted)).astype(BF16)
        results = (
            dot(grad_scores, masked(keys[:, first:last], inside)),
            dot_first(grad_scores, query),
            dot_first(softmax.astype(BF16), grad),
        )
        for kept, result in zip(sums, results):
            for tile in range(first // LANES, last // LANES):
                piece = result[:, tile * LANES - first : (tile + 1) * LANES - first]
                kept[tile] = piece if kept[tile] is None else kept[tile] + piece
    for tile in range(3):
        at = slice(tile * LANES, (tile + 1) * LANES)
        dq_ref[:, at] = (sums[0][tile] * SCALE).astype(BF16)
        grad_keys = sums[1][tile] * SCALE
        grad_values = sums[2][tile]
        for kind, (grads_of, own) in enumerate(((grad_keys, dk_ref), (grad_values, dv_ref))):
            own[:, at] = grads_of[:ROWS]
            left_ref[kind, :, at] = grads_of[ROWS : ROWS + EDGE].astype(BF16)
            right_ref[kind, :, at] = grads_of[ROWS + EDGE :].astype(BF16)


def attend_backward(queries, pairs, left, right, grad_attended):
    def block(rows):
        return pl.BlockSpec((rows, GROUP), lambda n: (0, n))

    def shape(rows, kind):
        return jax.ShapeDtypeStruct((rows, INNER), kind)

    edge = jax.ShapeDtypeStruct((2, EDGE, INNER), BF16)
    edge_block = pl.BlockSpec((2, EDGE, GROUP), lambda n: (0, 0, n))
    return pl.pallas_call(
        backward_kernel,
        out_shape=(shape(ROWS, BF16), shape(ROWS, F32), shape(ROWS, F32), edge, edge),
        grid=(2,),
        in_specs=attention_specs() + [block(ROWS)],
        out_specs=(block(ROWS), block(ROWS), block(ROWS), edge_block, edge_block),
        name="attend_backward",
    )(queries, pairs, pairs, left, left, right, right, grad_attended)


def norm_grad_kernel(
    dq_ref, dk_ref, dv_ref, left_ref, right_ref, low_ref, up_ref, gain_ref, tokens_hbm, hidden_hbm,
    out_ref, grads, total, tokens_ref, hidden_ref, sems,
):
    step = pl.program_id(0)
    copies = (
        pltpu.make_async_copy(tokens_hbm, tokens_ref, sems.at[0]),
        pltpu.make_async_copy(hidden_hbm, hidden_ref, sems.at[1]),
    )

    @pl.when(step == 0)
    def _():
        for copy in copies:
            copy.start()
        grads[:, :INNER] = dq_ref[...]
        for kind, own_ref in enumerate((dk_ref, dv_ref)):
            own = own_ref[...].reshape(LAT, LON_DEV, INNER)
            left = left_ref[kind].astype(F32).reshape(LAT, MARGIN, INNER)
            right = right_ref[kind].astype(F32).reshape(LAT, MARGIN, INNER)
            own = jnp.concatenate(
                [own[:, :MARGIN] + left, own[:, MARGIN : LON_DEV - MARGIN], own[:, LON_DEV - MARGIN :] + right],
                axis=1,
            )
            grads[:, (kind + 1) * INNER : (kind + 2) * INNER] = own.reshape(ROWS, INNER).astype(BF16)

    at = pl.ds(pl.multiple_of(step * 256, 256), 256)
    total[:, at] = dot_last(grads[:, :HALF_QKV], low_ref[0]) + dot_last(grads[:, HALF_QKV:], up_ref[0])

    @pl.when(step == 5)
    def _():
        for copy in copies:
            copy.wait()
        values = tokens_ref[...].astype(F32)
        average = jnp.mean(values, axis=-1, keepdims=True)
        centred = values - average
        variance = jnp.mean(centred * centred, axis=-1, keepdims=True)
        inverse_dev = lax.rsqrt(variance + EPSILON)
        standard = centred * inverse_dev
        grad_standard = total[...] * gain_ref[...]
        first_mean = jnp.mean(grad_standard, axis=-1, keepdims=True)
        second_mean = jnp.mean(grad_standard * standard, axis=-1, keepdims=True)
        grad = inverse_dev * (grad_standard - first_mean - standard * second_mean)
        out_ref[...] = (hidden_ref[...] + grad).astype(BF16)


def norm_grad(dq, dk, dv, from_left, from_right, full, tokens, gain, grad_hidden):
    return pl.pallas_call(
        norm_grad_kernel,
        out_shape=jax.ShapeDtypeStruct((ROWS, D), BF16),
        grid=(6,),
        in_specs=[
            whole_block((ROWS, INNER)),
            whole_block((ROWS, INNER)),
            whole_block((ROWS, INNER)),
            whole_block((2, EDGE, INNER)),
            whole_block((2, EDGE, INNER)),
            pl.BlockSpec((1, 256, HALF_QKV), lambda n: (0, n, 0)),
            pl.BlockSpec((1, 256, HALF_QKV), lambda n: (1, n, 0)),
            whole_block((1, D)),
            pl.BlockSpec(memory_space=pl.ANY),
            pl.BlockSpec(memory_space=pl.ANY),
        ],
        out_specs=whole_block((ROWS, D)),
        scratch_shapes=[
            pltpu.VMEM((ROWS, 3 * INNER), BF16),
            pltpu.VMEM((ROWS, D), F32),
            pltpu.VMEM((ROWS, D), BF16),
            pltpu.VMEM((ROWS, D), F32),
            pltpu.SemaphoreType.DMA((2,)),
        ],
        name="norm_grad",
    )(dq, dk, dv, from_left, from_right, full, full, gain, tokens, grad_hidden)


def sum_kernel(pieces_ref, out_ref):
    total = pieces_ref[0].astype(F32)
    for place in range(1, CORES * TILES):
        total = total + pieces_ref[place].astype(F32)
    empty = jnp.zeros((24, LANES - CHANNELS), F32)
    for z in range(ZS):
        part = jnp.concatenate([total[:, z * CHANNELS : (z + 1) * CHANNELS], empty], axis=1)
        out_ref[z] = part
        out_ref[ZS + z] = part


def sum_pieces(pieces):
    return pl.pallas_call(
        sum_kernel,
        out_shape=jax.ShapeDtypeStruct((2 * ZS, 24, LANES), F32),
        in_specs=[WHOLE],
        out_specs=WHOLE,
        name="sum_pieces",
    )(pieces)


def interp_weights(fine_index):
    coarse_cell = fine_index // 4
    phase_index = fine_index % 4
    lower_shift = (phase_index < 2).astype(jnp.int32)
    upper_weight = (2 * phase_index - 3 + 8 * lower_shift).astype(F32) / 8.0
    return (coarse_cell - lower_shift, upper_weight)


def build_matrix(lower_cell, upper_cell, upper_weight, count):
    columns = jnp.arange(count, dtype=jnp.int32)
    lower_part = jnp.where(columns[None, :] == lower_cell[:, None], 1.0 - upper_weight[:, None], 0.0)
    upper_portion = jnp.where(columns[None, :] == upper_cell[:, None], upper_weight[:, None], 0.0)
    return lower_part + upper_portion


def shifted(value, steps):
    return lax.ppermute(value, TILE, [(i, (i + steps) % TILES) for i in range(TILES)])


def residual_of(coarse):
    before = shifted(coarse[:, :, -1:], 1)
    after = shifted(coarse[:, :, :1], -1)
    padded = jnp.concatenate([before, coarse, after], axis=2)
    lat_lower, lat_upper_weight = interp_weights(jnp.arange(4 * LAT, dtype=jnp.int32))
    latitude_matrix = build_matrix(
        jnp.clip(lat_lower, 0, LAT - 1), jnp.clip(lat_lower + 1, 0, LAT - 1), lat_upper_weight, LAT
    )
    lon_lower, lon_upper_weight = interp_weights(jnp.arange(4 * LON_DEV, dtype=jnp.int32))
    lon_matrix = build_matrix(lon_lower + 1, lon_lower + 2, lon_upper_weight, LON_DEV + 2)
    incomplete_grid = jnp.einsum("lj,kji->kli", latitude_matrix, padded, precision=lax.Precision.HIGHEST)
    return jnp.einsum("vrb,cb->vrc", incomplete_grid, lon_matrix, precision=lax.Precision.HIGHEST)


def head_columns():
    target = jnp.arange(PADDED, dtype=jnp.int32)
    phase, channel = target // LANES, target % LANES
    source = jnp.where(channel < CHANNELS, channel * PHASES + phase, -1)
    return (jnp.arange(HEAD_OUT, dtype=jnp.int32)[:, None] == source[None, :]).astype(F32)


def gather_qkv(qkv):
    half = lax.axis_index("dp")
    qkv_half = lax.dynamic_slice_in_dim(qkv, half * HALF_QKV, HALF_QKV, 1)
    full = lax.all_gather(qkv_half, ("dp",) + FSDP, axis=0, tiled=True)
    return full.reshape(2, D, HALF_QKV)


def to_all(value, axes, count):
    copies = jnp.broadcast_to(value[None], (count,) + value.shape)
    return lax.all_to_all(copies, axes, 0, 0, tiled=True)


def gather_rest(out_w, head_w):
    out_rows = out_w.reshape(48, 12, LANES).transpose(1, 0, 2).reshape(576, LANES)
    head_pad = dot(head_w, head_columns().astype(BF16)).astype(BF16)
    head_rows = head_pad.reshape(96, PHASES, LANES).transpose(1, 0, 2).reshape(384, LANES)
    rows = jnp.concatenate([out_rows, head_rows, jnp.zeros((PIECE, LANES), BF16)], axis=0)
    own = lax.dynamic_slice_in_dim(rows, lax.axis_index(TILE) * PIECE, PIECE, 0)
    over_z = to_all(own, ("z",), ZS)
    over_tile = to_all(over_z, TILE, TILES)
    return unpack(to_all(over_tile, ("c",), CORES))


def reduce_head(pieces):
    pieces = lax.all_to_all(pieces, ("c",) + TILE, 0, 0, tiled=True)
    both = lax.all_to_all(sum_pieces(pieces), ("dp", "z"), 0, 0, tiled=True)
    spread = to_all(jnp.sum(both, axis=0), TILE, TILES)
    padded = spread.reshape(4, PHASES, 24, LANES).transpose(0, 2, 1, 3).reshape(96, PADDED)
    return lax.dot_general(
        padded, head_columns(), (((1,), (1,)), ((), ())), precision=lax.Precision.HIGHEST, preferred_element_type=F32
    )


def shards(tokens, norm_gain, query_key_value_weight, out_weight, head_weight, coarse, grad_fine):
    tokens = tokens[0].reshape(ROWS, D)
    gain = norm_gain.reshape(1, D)
    full = gather_qkv(query_key_value_weight)
    residual = residual_of(coarse[0])
    normed, rows = prepare(tokens, gain, grad_fine[0])
    out_full, head = gather_rest(out_weight, head_weight)
    grad_hidden, grad_attended = hidden_grad(rows, head, out_full)
    pairs, leading, last = project_pairs(normed, full)
    left = shifted(last, 1)
    right = shifted(leading, -1)
    queries = project(lax.optimization_barrier((normed, pairs))[0], full)
    fine_grid, pieces = forward(queries, pairs, left, right, tokens, out_full, head, rows, residual)
    grad_head = reduce_head(pieces)
    dq, dk, dv, to_left, to_right = attend_backward(queries, pairs, left, right, grad_attended)
    from_right = shifted(to_left, -1)
    from_left = shifted(to_right, 1)
    grad_tokens = norm_grad(dq, dk, dv, from_left, from_right, full, tokens, gain, grad_hidden)
    return (fine_grid[None], grad_tokens.reshape(1, LAT, LON_DEV, D), grad_head)


def solution(mesh):
    fine_mesh = Mesh(mesh.devices.reshape(2, ZS, CORES, YS, XS), ("dp", "z", "c", "y", "x"))
    samples = ("dp", "z", "c")
    placed = (
        P(samples, None, TILE, None),
        P(),
        P(FSDP, None),
        P(FSDP, None),
        P(FSDP, None),
        P(samples, None, None, TILE),
        P(samples, None, None, TILE),
    )
    return jax.shard_map(
        shards,
        mesh=fine_mesh,
        in_specs=placed,
        out_specs=(P(samples, None, None, TILE), P(samples, None, TILE, None), P(FSDP, None)),
        check_vma=False,
    )
```

```python
import functools
import jax
import jax.numpy as jnp
from jax import lax
from jax.experimental import pallas as pl
from jax.experimental.pallas import tpu as pltpu
from jax.sharding import Mesh
from jax.sharding import PartitionSpec as P

D = 1536
HEADS = 8
HEAD_DIM = 96
VARS = 20
MARGIN = 8
LAT = 8
LON_DEV = 32
INNER = 768
HEAD_OUT = 320
ROWS = 256
EDGE = 64
KEYS = ROWS + 2 * EDGE
GROUP = 384
PAIR = 2 * INNER
ZS = 8
CORES = 2
YS = 4
XS = 4
TILES = 16
FSDP = ("z", "c")
TILE = ("y", "x")
HALF_QKV = 1152
HALF_OUT = 768
PIECE = 64
UNPACK = 4
WIDE = ZS * 80
PHASES = 4
CHANNELS = 80
LANES = 128
PADDED = PHASES * LANES
EPSILON = 1e-05
SCALE = HEAD_DIM ** (-0.5)
F32 = jnp.float32
BF16 = jnp.bfloat16
WHOLE = pl.BlockSpec(memory_space=pltpu.VMEM)


def dot(left, right):
    return lax.dot_general(left, right, (((1,), (0,)), ((), ())), preferred_element_type=F32)


def dot_last(left, right):
    return lax.dot_general(left, right, (((1,), (1,)), ((), ())), preferred_element_type=F32)


def dot_first(left, right):
    return lax.dot_general(left, right, (((0,), (0,)), ((), ())), preferred_element_type=F32)


def spread_matrix():
    row = lax.broadcasted_iota(jnp.int32, (LANES, LANES), 0)
    lane = lax.broadcasted_iota(jnp.int32, (LANES, LANES), 1)
    target = (row % LON_DEV) * PHASES + row // LON_DEV
    return jnp.where(lane == target, 1.0, 0.0).astype(BF16)


def standardized(values):
    average = jnp.mean(values, axis=-1, keepdims=True)
    centred = values - average
    variance = jnp.mean(centred * centred, axis=-1, keepdims=True)
    inverse_dev = lax.rsqrt(variance + EPSILON)
    return centred * inverse_dev, inverse_dev


def prepare_kernel(tokens_ref, left_ref, right_ref, gain_ref, fine_ref, normed_ref, rows_ref):
    for source, first in ((tokens_ref, 0), (left_ref, ROWS), (right_ref, ROWS + EDGE)):
        standard, _ = standardized(source[...].astype(F32))
        normed_ref[first : first + source.shape[0]] = (standard * gain_ref[...]).astype(BF16)
    select = spread_matrix()
    empty = jnp.zeros((LANES - CHANNELS, LANES), BF16)
    for lat in range(LAT):
        block = fine_ref[:, PHASES * lat : PHASES * (lat + 1), :].reshape(CHANNELS, LANES)
        block = jnp.concatenate([block.astype(BF16), empty], axis=0)
        picked = dot_last(select, block).astype(BF16)
        for phase in range(PHASES):
            rows_ref[lat * LON_DEV : (lat + 1) * LON_DEV, phase * LANES : (phase + 1) * LANES] = picked[
                phase * LON_DEV : (phase + 1) * LON_DEV
            ]


def prepare(tokens, left, right, gain, grad_fine):
    return pl.pallas_call(
        prepare_kernel,
        out_shape=(
            jax.ShapeDtypeStruct((KEYS, D), BF16),
            jax.ShapeDtypeStruct((ROWS, PADDED), BF16),
        ),
        in_specs=[WHOLE] * 5,
        out_specs=(WHOLE, WHOLE),
        name="prepare",
    )(tokens, left, right, gain, grad_fine)


def unpack_kernel(core_ref, own_ref, other_ref, out_ref, head_ref):
    core = core_ref[0]
    for source, place in ((own_ref, core), (other_ref, 1 - core)):
        for tile in range(60):
            for z in range(UNPACK):
                block = source[tile // 4, z, tile % 4 * 16 : (tile % 4 + 1) * 16, :]
                if tile < 36:
                    top = pl.multiple_of(z * 96 + place * 48 + tile % 3 * 16, 16)
                    out_ref[pl.ds(top, 16), tile // 3 * LANES : (tile // 3 + 1) * LANES] = block
                else:
                    top = pl.multiple_of(z * 192 + place * 96 + tile % 6 * 16, 16)
                    phase = (tile - 36) // 6
                    head_ref[pl.ds(top, 16), phase * LANES : (phase + 1) * LANES] = block


def unpack(core, own, other):
    block = pl.BlockSpec((TILES, UNPACK, PIECE, LANES), lambda z: (0, z, 0, 0))
    return pl.pallas_call(
        unpack_kernel,
        out_shape=(
            jax.ShapeDtypeStruct((INNER, D), BF16),
            jax.ShapeDtypeStruct((D, PADDED), BF16),
        ),
        grid=(ZS // UNPACK,),
        in_specs=[pl.BlockSpec(memory_space=pltpu.SMEM), block, block],
        out_specs=(
            pl.BlockSpec((UNPACK * 96, D), lambda z: (z, 0)),
            pl.BlockSpec((UNPACK * 192, PADDED), lambda z: (z, 0)),
        ),
        name="unpack",
    )(core, own, other)


def hidden_grad_kernel(rows_ref, head_ref, out_ref, hidden_ref, attended_ref):
    grad_hidden = dot_last(rows_ref[...], head_ref[...])
    hidden_ref[...] = grad_hidden
    attended_ref[...] = dot_last(grad_hidden.astype(BF16), out_ref[...]).astype(BF16)


def hidden_grad(rows, head, out_weight):
    return pl.pallas_call(
        hidden_grad_kernel,
        out_shape=(
            jax.ShapeDtypeStruct((ROWS, D), F32),
            jax.ShapeDtypeStruct((ROWS, INNER), BF16),
        ),
        in_specs=[WHOLE, WHOLE, WHOLE],
        out_specs=(WHOLE, WHOLE),
        name="hidden_grad",
    )(rows, head, out_weight)


def whole_block(shape):
    return pl.BlockSpec(shape, lambda n: (0,) * len(shape))


def head_window(head):
    first = head * HEAD_DIM // LANES * LANES
    last = -(-(head + 1) * HEAD_DIM // LANES) * LANES
    lane = lax.broadcasted_iota(jnp.int32, (1, last - first), 1) + first
    inside = (lane >= head * HEAD_DIM) & (lane < (head + 1) * HEAD_DIM)
    return first, last, inside


def masked(values, inside):
    return jnp.where(inside, values, jnp.zeros_like(values))


def softmax_of(query, key):
    scores = dot_last(query, key) * SCALE
    biggest = jnp.max(scores, axis=-1, keepdims=True)
    exponent = jnp.exp(scores - biggest)
    return exponent / jnp.sum(exponent, axis=-1, keepdims=True)


def forward_group(queries, keys, values):
    parts = [None, None, None]
    for head in range(4):
        first, last, inside = head_window(head)
        softmax = softmax_of(masked(queries[:, first:last], inside), keys[:, first:last])
        result = dot(softmax.astype(BF16), masked(values[:, first:last], inside))
        for tile in range(first // LANES, last // LANES):
            piece = result[:, tile * LANES - first : (tile + 1) * LANES - first]
            parts[tile] = piece if parts[tile] is None else parts[tile] + piece
    return jnp.concatenate([part.astype(BF16) for part in parts], axis=1)


def forward_kernel(
    normed_ref, weight_ref,
    tokens_hbm, out_hbm, head_hbm, rows_hbm, residual_hbm,
    projected_ref, fine_ref, pieces_ref,
    tokens_ref, out_ref, head_ref, rows_ref, residual_ref, products, sems,
):
    step = pl.program_id(0)
    copies = [
        pltpu.make_async_copy(source, target, sems.at[place])
        for place, (source, target) in enumerate(
            (
                (tokens_hbm, tokens_ref),
                (out_hbm, out_ref),
                (head_hbm, head_ref),
                (rows_hbm, rows_ref),
                (residual_hbm, residual_ref),
            )
        )
    ]

    @pl.when(step == 3)
    def _():
        for copy in copies:
            copy.start()

    @pl.when(step < 2)
    def _():
        projected_ref[step, :ROWS] = dot(normed_ref[:ROWS], weight_ref[0]).astype(BF16)

    @pl.when(step >= 2)
    def _():
        projected_ref[step] = dot(normed_ref[...], weight_ref[0]).astype(BF16)

    @pl.when(step == 5)
    def _():
        attended = [
            forward_group(projected_ref[group, :ROWS], projected_ref[2 + group], projected_ref[4 + group])
            for group in range(2)
        ]
        for copy in copies:
            copy.wait()
        mixed = dot(attended[0], out_ref[:GROUP]) + dot(attended[1], out_ref[GROUP:])
        hidden = (tokens_ref[...].astype(F32) + mixed).astype(BF16)
        head_out = dot(hidden, head_ref[...])
        products[...] = dot_first(hidden, rows_ref[...])
        for core in range(CORES):
            for quad in range(4):
                for phase in range(PHASES):
                    row = [
                        products[
                            (z * CORES + core) * 96 + quad * 24 : (z * CORES + core) * 96 + quad * 24 + 24,
                            phase * LANES : phase * LANES + CHANNELS,
                        ]
                        for z in range(ZS)
                    ]
                    pieces_ref[core * TILES + quad * 4 + phase] = jnp.concatenate(row, axis=1).astype(BF16)
        select = spread_matrix()
        for lat in range(LAT):
            at = slice(lat * LON_DEV, (lat + 1) * LON_DEV)
            stacked = jnp.concatenate(
                [head_out[at, phase * LANES : (phase + 1) * LANES] for phase in range(PHASES)], axis=0
            )
            high = stacked.astype(BF16)
            low = (stacked - high.astype(F32)).astype(BF16)
            spread = dot_first(high, select) + dot_first(low, select)
            across = slice(PHASES * lat, PHASES * (lat + 1))
            fine_ref[:, across, :] = spread[:CHANNELS].reshape(VARS, PHASES, LANES) + residual_ref[:, across, :]


def forward(normed, full, tokens, out_weight, head, rows, residual):
    fine = (VARS, 4 * LAT, LANES)
    pieces = (CORES * TILES, 24, WIDE)
    projected = (6, KEYS, GROUP)
    return pl.pallas_call(
        forward_kernel,
        out_shape=(
            jax.ShapeDtypeStruct(projected, BF16),
            jax.ShapeDtypeStruct(fine, F32),
            jax.ShapeDtypeStruct(pieces, BF16),
        ),
        grid=(6,),
        in_specs=[
            whole_block((KEYS, D)),
            pl.BlockSpec((1, D, GROUP), lambda n: (n // 3, 0, n % 3)),
        ]
        + [pl.BlockSpec(memory_space=pl.ANY)] * 5,
        out_specs=(whole_block(projected), whole_block(fine), whole_block(pieces)),
        scratch_shapes=[
            pltpu.VMEM((ROWS, D), BF16),
            pltpu.VMEM((INNER, D), BF16),
            pltpu.VMEM((D, PADDED), BF16),
            pltpu.VMEM((ROWS, PADDED), BF16),
            pltpu.VMEM(fine, F32),
            pltpu.VMEM((D, PADDED), F32),
            pltpu.SemaphoreType.DMA((5,)),
        ],
        name="forward",
    )(normed, full, tokens, out_weight, head, rows, residual)


def backward_kernel(
    q_ref, k_ref, v_ref, grad_ref,
    dq_ref, dk_ref, dv_ref, left_ref, right_ref,
):
    queries = q_ref[0, :ROWS]
    grads = grad_ref[...]
    keys = k_ref[0]
    values = v_ref[0]
    sums = [[None, None, None] for _ in range(3)]
    for head in range(4):
        first, last, inside = head_window(head)
        query = masked(queries[:, first:last], inside)
        grad = masked(grads[:, first:last], inside)
        softmax = softmax_of(query, keys[:, first:last])
        grad_weights = dot_last(grad, values[:, first:last])
        weighted = jnp.sum(softmax * grad_weights, axis=-1, keepdims=True)
        grad_scores = (softmax * (grad_weights - weighted)).astype(BF16)
        results = (
            dot(grad_scores, masked(keys[:, first:last], inside)),
            dot_first(grad_scores, query),
            dot_first(softmax.astype(BF16), grad),
        )
        for kept, result in zip(sums, results):
            for tile in range(first // LANES, last // LANES):
                piece = result[:, tile * LANES - first : (tile + 1) * LANES - first]
                kept[tile] = piece if kept[tile] is None else kept[tile] + piece
    for tile in range(3):
        at = slice(tile * LANES, (tile + 1) * LANES)
        dq_ref[:, at] = (sums[0][tile] * SCALE).astype(BF16)
        grad_keys = sums[1][tile] * SCALE
        grad_values = sums[2][tile]
        for kind, (grads_of, own) in enumerate(((grad_keys, dk_ref), (grad_values, dv_ref))):
            own[:, at] = grads_of[:ROWS]
            left_ref[kind, :, at] = grads_of[ROWS : ROWS + EDGE].astype(BF16)
            right_ref[kind, :, at] = grads_of[ROWS + EDGE :].astype(BF16)


def attend_backward(projected, grad_attended):
    def block(rows):
        return pl.BlockSpec((rows, GROUP), lambda n: (0, n))

    def shape(rows, kind):
        return jax.ShapeDtypeStruct((rows, INNER), kind)

    edge = jax.ShapeDtypeStruct((2, EDGE, INNER), BF16)
    edge_block = pl.BlockSpec((2, EDGE, GROUP), lambda n: (0, 0, n))
    return pl.pallas_call(
        backward_kernel,
        out_shape=(shape(ROWS, BF16), shape(ROWS, F32), shape(ROWS, F32), edge, edge),
        grid=(2,),
        in_specs=[pl.BlockSpec((1, KEYS, GROUP), lambda n, first=first: (first + n, 0, 0)) for first in (0, 2, 4)]
        + [block(ROWS)],
        out_specs=(block(ROWS), block(ROWS), block(ROWS), edge_block, edge_block),
        name="attend_backward",
    )(projected, projected, projected, grad_attended)


def norm_grad_kernel(
    dq_ref, dk_ref, dv_ref, left_ref, right_ref, low_ref, up_ref, gain_ref, tokens_hbm, hidden_hbm,
    out_ref, grads, total, tokens_ref, hidden_ref, sems,
):
    step = pl.program_id(0)
    copies = (
        pltpu.make_async_copy(tokens_hbm, tokens_ref, sems.at[0]),
        pltpu.make_async_copy(hidden_hbm, hidden_ref, sems.at[1]),
    )

    @pl.when(step == 0)
    def _():
        for copy in copies:
            copy.start()
        grads[:, :INNER] = dq_ref[...]
        for kind, own_ref in enumerate((dk_ref, dv_ref)):
            own = own_ref[...].reshape(LAT, LON_DEV, INNER)
            left = left_ref[kind].astype(F32).reshape(LAT, MARGIN, INNER)
            right = right_ref[kind].astype(F32).reshape(LAT, MARGIN, INNER)
            own = jnp.concatenate(
                [own[:, :MARGIN] + left, own[:, MARGIN : LON_DEV - MARGIN], own[:, LON_DEV - MARGIN :] + right],
                axis=1,
            )
            grads[:, (kind + 1) * INNER : (kind + 2) * INNER] = own.reshape(ROWS, INNER).astype(BF16)

    at = pl.ds(pl.multiple_of(step * 256, 256), 256)
    total[:, at] = dot_last(grads[:, :HALF_QKV], low_ref[0]) + dot_last(grads[:, HALF_QKV:], up_ref[0])

    @pl.when(step == 5)
    def _():
        for copy in copies:
            copy.wait()
        values = tokens_ref[...].astype(F32)
        standard, inverse_dev = standardized(values)
        grad_standard = total[...] * gain_ref[...]
        first_mean = jnp.mean(grad_standard, axis=-1, keepdims=True)
        second_mean = jnp.mean(grad_standard * standard, axis=-1, keepdims=True)
        grad = inverse_dev * (grad_standard - first_mean - standard * second_mean)
        out_ref[...] = (hidden_ref[...] + grad).astype(BF16)


def norm_grad(dq, dk, dv, from_left, from_right, full, tokens, gain, grad_hidden):
    return pl.pallas_call(
        norm_grad_kernel,
        out_shape=jax.ShapeDtypeStruct((ROWS, D), BF16),
        grid=(6,),
        in_specs=[
            whole_block((ROWS, INNER)),
            whole_block((ROWS, INNER)),
            whole_block((ROWS, INNER)),
            whole_block((2, EDGE, INNER)),
            whole_block((2, EDGE, INNER)),
            pl.BlockSpec((1, 256, HALF_QKV), lambda n: (0, n, 0)),
            pl.BlockSpec((1, 256, HALF_QKV), lambda n: (1, n, 0)),
            whole_block((1, D)),
            pl.BlockSpec(memory_space=pl.ANY),
            pl.BlockSpec(memory_space=pl.ANY),
        ],
        out_specs=whole_block((ROWS, D)),
        scratch_shapes=[
            pltpu.VMEM((ROWS, 3 * INNER), BF16),
            pltpu.VMEM((ROWS, D), F32),
            pltpu.VMEM((ROWS, D), BF16),
            pltpu.VMEM((ROWS, D), F32),
            pltpu.SemaphoreType.DMA((2,)),
        ],
        name="norm_grad",
    )(dq, dk, dv, from_left, from_right, full, full, gain, tokens, grad_hidden)


def sum_kernel(pieces_ref, out_ref):
    total = pieces_ref[0].astype(F32)
    for place in range(1, CORES * TILES):
        total = total + pieces_ref[place].astype(F32)
    empty = jnp.zeros((24, LANES - CHANNELS), F32)
    for z in range(ZS):
        part = jnp.concatenate([total[:, z * CHANNELS : (z + 1) * CHANNELS], empty], axis=1)
        out_ref[z] = part
        out_ref[ZS + z] = part


def sum_pieces(pieces):
    return pl.pallas_call(
        sum_kernel,
        out_shape=jax.ShapeDtypeStruct((2 * ZS, 24, LANES), F32),
        in_specs=[WHOLE],
        out_specs=WHOLE,
        name="sum_pieces",
    )(pieces)


def interp_weights(fine_index):
    coarse_cell = fine_index // 4
    phase_index = fine_index % 4
    lower_shift = (phase_index < 2).astype(jnp.int32)
    upper_weight = (2 * phase_index - 3 + 8 * lower_shift).astype(F32) / 8.0
    return (coarse_cell - lower_shift, upper_weight)


def build_matrix(lower_cell, upper_cell, upper_weight, count):
    columns = jnp.arange(count, dtype=jnp.int32)
    lower_part = jnp.where(columns[None, :] == lower_cell[:, None], 1.0 - upper_weight[:, None], 0.0)
    upper_portion = jnp.where(columns[None, :] == upper_cell[:, None], upper_weight[:, None], 0.0)
    return lower_part + upper_portion


def shifted(value, steps):
    return lax.ppermute(value, TILE, [(i, (i + steps) % TILES) for i in range(TILES)])


def residual_of(coarse):
    before = shifted(coarse[:, :, -1:], 1)
    after = shifted(coarse[:, :, :1], -1)
    padded = jnp.concatenate([before, coarse, after], axis=2)
    lat_lower, lat_upper_weight = interp_weights(jnp.arange(4 * LAT, dtype=jnp.int32))
    latitude_matrix = build_matrix(
        jnp.clip(lat_lower, 0, LAT - 1), jnp.clip(lat_lower + 1, 0, LAT - 1), lat_upper_weight, LAT
    )
    lon_lower, lon_upper_weight = interp_weights(jnp.arange(4 * LON_DEV, dtype=jnp.int32))
    lon_matrix = build_matrix(lon_lower + 1, lon_lower + 2, lon_upper_weight, LON_DEV + 2)
    incomplete_grid = jnp.einsum("lj,kji->kli", latitude_matrix, padded, precision=lax.Precision.HIGHEST)
    return jnp.einsum("vrb,cb->vrc", incomplete_grid, lon_matrix, precision=lax.Precision.HIGHEST)


def head_columns():
    target = jnp.arange(PADDED, dtype=jnp.int32)
    phase, channel = target // LANES, target % LANES
    source = jnp.where(channel < CHANNELS, channel * PHASES + phase, -1)
    return (jnp.arange(HEAD_OUT, dtype=jnp.int32)[:, None] == source[None, :]).astype(F32)


def gather_qkv(qkv):
    half = lax.axis_index("dp")
    qkv_half = lax.dynamic_slice_in_dim(qkv, half * HALF_QKV, HALF_QKV, 1)
    full = lax.all_gather(qkv_half, ("dp",) + FSDP, axis=0, tiled=True)
    return full.reshape(2, D, HALF_QKV)


def to_all(value, axes, count):
    copies = jnp.broadcast_to(value[None], (count,) + value.shape)
    return lax.all_to_all(copies, axes, 0, 0, tiled=True)


def gather_rest(out_w, head_w, ready):
    out_rows = out_w.reshape(48, 12, LANES).transpose(1, 0, 2).reshape(576, LANES)
    head_pad = dot(head_w, head_columns().astype(BF16)).astype(BF16)
    head_rows = head_pad.reshape(96, PHASES, LANES).transpose(1, 0, 2).reshape(384, LANES)
    rows = jnp.concatenate([out_rows, head_rows, jnp.zeros((PIECE, LANES), BF16)], axis=0)
    own = lax.dynamic_slice_in_dim(rows, lax.axis_index(TILE) * PIECE, PIECE, 0)
    over_z = to_all(own, ("z",), ZS)
    over_tile = to_all(over_z, TILE, TILES)
    over_tile = lax.optimization_barrier((over_tile, ready))[0]
    other = lax.ppermute(over_tile, "c", [(0, 1), (1, 0)])
    return unpack(lax.axis_index("c").reshape(1).astype(jnp.int32), over_tile, other)


def reduce_head(pieces):
    pieces = lax.all_to_all(pieces, ("c",) + TILE, 0, 0, tiled=True)
    both = lax.all_to_all(sum_pieces(pieces), ("dp", "z"), 0, 0, tiled=True)
    spread = to_all(jnp.sum(both, axis=0), TILE, TILES)
    padded = spread.reshape(4, PHASES, 24, LANES).transpose(0, 2, 1, 3).reshape(96, PADDED)
    return lax.dot_general(
        padded, head_columns(), (((1,), (1,)), ((), ())), precision=lax.Precision.HIGHEST, preferred_element_type=F32
    )


def shards(tokens, norm_gain, query_key_value_weight, out_weight, head_weight, coarse, grad_fine):
    tokens = tokens[0].reshape(ROWS, D)
    gain = norm_gain.reshape(1, D)
    full = gather_qkv(query_key_value_weight)
    grid = tokens.reshape(LAT, LON_DEV, D)
    left = shifted(grid[:, LON_DEV - MARGIN :].reshape(EDGE, D), 1)
    right = shifted(grid[:, :MARGIN].reshape(EDGE, D), -1)
    residual = residual_of(coarse[0])
    normed, rows = prepare(tokens, left, right, gain, grad_fine[0])
    out_full, head = gather_rest(out_weight, head_weight, (normed, residual))
    grad_hidden, grad_attended = hidden_grad(rows, head, out_full)
    full, grad_hidden, grad_attended, residual = lax.optimization_barrier(
        (full, grad_hidden, grad_attended, residual)
    )
    projected, fine_grid, pieces = forward(normed, full, tokens, out_full, head, rows, residual)
    grad_head = reduce_head(pieces)
    dq, dk, dv, to_left, to_right = attend_backward(projected, grad_attended)
    from_right = shifted(to_left, -1)
    from_left = shifted(to_right, 1)
    grad_tokens = norm_grad(dq, dk, dv, from_left, from_right, full, tokens, gain, grad_hidden)
    return (fine_grid[None], grad_tokens.reshape(1, LAT, LON_DEV, D), grad_head)


def solution(mesh):
    fine_mesh = Mesh(mesh.devices.reshape(2, ZS, CORES, YS, XS), ("dp", "z", "c", "y", "x"))
    samples = ("dp", "z", "c")
    placed = (
        P(samples, None, TILE, None),
        P(),
        P(FSDP, None),
        P(FSDP, None),
        P(FSDP, None),
        P(samples, None, None, TILE),
        P(samples, None, None, TILE),
    )
    return jax.shard_map(
        shards,
        mesh=fine_mesh,
        in_specs=placed,
        out_specs=(P(samples, None, None, TILE), P(samples, None, TILE, None), P(FSDP, None)),
        check_vma=False,
    )
```

```python
import functools
import jax
import jax.numpy as jnp
from jax import lax
from jax.experimental import pallas as pl
from jax.experimental.pallas import tpu as pltpu
from jax.sharding import Mesh
from jax.sharding import PartitionSpec as P

D = 1536
HEADS = 8
HEAD_DIM = 96
VARS = 20
MARGIN = 8
LAT = 8
LON_DEV = 32
INNER = 768
HEAD_OUT = 320
ROWS = 256
EDGE = 64
KEYS = ROWS + 2 * EDGE
GROUP = 384
PAIR = 2 * INNER
ZS = 8
CORES = 2
YS = 4
XS = 4
TILES = 16
FSDP = ("z", "c")
TILE = ("y", "x")
HALF_QKV = 1152
HALF_OUT = 768
PIECE = 64
UNPACK = 4
WIDE = ZS * 80
PHASES = 4
CHANNELS = 80
LANES = 128
PADDED = PHASES * LANES
EPSILON = 1e-05
SCALE = HEAD_DIM ** (-0.5)
F32 = jnp.float32
BF16 = jnp.bfloat16
WHOLE = pl.BlockSpec(memory_space=pltpu.VMEM)


def dot(left, right):
    return lax.dot_general(left, right, (((1,), (0,)), ((), ())), preferred_element_type=F32)


def dot_last(left, right):
    return lax.dot_general(left, right, (((1,), (1,)), ((), ())), preferred_element_type=F32)


def dot_first(left, right):
    return lax.dot_general(left, right, (((0,), (0,)), ((), ())), preferred_element_type=F32)


def spread_matrix():
    row = lax.broadcasted_iota(jnp.int32, (LANES, LANES), 0)
    lane = lax.broadcasted_iota(jnp.int32, (LANES, LANES), 1)
    target = (row % LON_DEV) * PHASES + row // LON_DEV
    return jnp.where(lane == target, 1.0, 0.0).astype(BF16)


def standardized(values):
    average = jnp.mean(values, axis=-1, keepdims=True)
    centred = values - average
    variance = jnp.mean(centred * centred, axis=-1, keepdims=True)
    inverse_dev = lax.rsqrt(variance + EPSILON)
    return centred * inverse_dev, inverse_dev


def prepare_kernel(tokens_ref, left_ref, right_ref, gain_ref, fine_ref, normed_ref, rows_ref):
    for source, first in ((tokens_ref, 0), (left_ref, ROWS), (right_ref, ROWS + EDGE)):
        standard, _ = standardized(source[...].astype(F32))
        normed_ref[first : first + source.shape[0]] = (standard * gain_ref[...]).astype(BF16)
    select = spread_matrix()
    empty = jnp.zeros((LANES - CHANNELS, LANES), BF16)
    for lat in range(LAT):
        block = fine_ref[:, PHASES * lat : PHASES * (lat + 1), :].reshape(CHANNELS, LANES)
        block = jnp.concatenate([block.astype(BF16), empty], axis=0)
        picked = dot_last(select, block).astype(BF16)
        for phase in range(PHASES):
            rows_ref[lat * LON_DEV : (lat + 1) * LON_DEV, phase * LANES : (phase + 1) * LANES] = picked[
                phase * LON_DEV : (phase + 1) * LON_DEV
            ]


def prepare(tokens, left, right, gain, grad_fine):
    return pl.pallas_call(
        prepare_kernel,
        out_shape=(
            jax.ShapeDtypeStruct((KEYS, D), BF16),
            jax.ShapeDtypeStruct((ROWS, PADDED), BF16),
        ),
        in_specs=[WHOLE] * 5,
        out_specs=(WHOLE, WHOLE),
        name="prepare",
    )(tokens, left, right, gain, grad_fine)


def unpack_kernel(core_ref, own_ref, other_ref, out_ref, head_ref):
    core = core_ref[0]
    for source, place in ((own_ref, core), (other_ref, 1 - core)):
        for tile in range(60):
            for z in range(UNPACK):
                block = source[tile // 4, z, tile % 4 * 16 : (tile % 4 + 1) * 16, :]
                if tile < 36:
                    top = pl.multiple_of(z * 96 + place * 48 + tile % 3 * 16, 16)
                    out_ref[pl.ds(top, 16), tile // 3 * LANES : (tile // 3 + 1) * LANES] = block
                else:
                    top = pl.multiple_of(z * 192 + place * 96 + tile % 6 * 16, 16)
                    phase = (tile - 36) // 6
                    head_ref[pl.ds(top, 16), phase * LANES : (phase + 1) * LANES] = block


def unpack(core, own, other):
    block = pl.BlockSpec((TILES, UNPACK, PIECE, LANES), lambda z: (0, z, 0, 0))
    return pl.pallas_call(
        unpack_kernel,
        out_shape=(
            jax.ShapeDtypeStruct((INNER, D), BF16),
            jax.ShapeDtypeStruct((D, PADDED), BF16),
        ),
        grid=(ZS // UNPACK,),
        in_specs=[pl.BlockSpec(memory_space=pltpu.SMEM), block, block],
        out_specs=(
            pl.BlockSpec((UNPACK * 96, D), lambda z: (z, 0)),
            pl.BlockSpec((UNPACK * 192, PADDED), lambda z: (z, 0)),
        ),
        name="unpack",
    )(core, own, other)


def hidden_grad_kernel(rows_ref, head_ref, out_ref, hidden_ref, attended_ref):
    grad_hidden = dot_last(rows_ref[...], head_ref[...])
    hidden_ref[...] = grad_hidden
    attended_ref[...] = dot_last(grad_hidden.astype(BF16), out_ref[...]).astype(BF16)


def hidden_grad(rows, head, out_weight):
    return pl.pallas_call(
        hidden_grad_kernel,
        out_shape=(
            jax.ShapeDtypeStruct((ROWS, D), F32),
            jax.ShapeDtypeStruct((ROWS, INNER), BF16),
        ),
        in_specs=[WHOLE, WHOLE, WHOLE],
        out_specs=(WHOLE, WHOLE),
        name="hidden_grad",
    )(rows, head, out_weight)


def whole_block(shape):
    return pl.BlockSpec(shape, lambda n: (0,) * len(shape))


def head_window(head):
    first = head * HEAD_DIM // LANES * LANES
    last = -(-(head + 1) * HEAD_DIM // LANES) * LANES
    lane = lax.broadcasted_iota(jnp.int32, (1, last - first), 1) + first
    inside = (lane >= head * HEAD_DIM) & (lane < (head + 1) * HEAD_DIM)
    return first, last, inside


def masked(values, inside):
    return jnp.where(inside, values, jnp.zeros_like(values))


def softmax_of(query, key):
    scores = dot_last(query, key) * SCALE
    biggest = jnp.max(scores, axis=-1, keepdims=True)
    exponent = jnp.exp(scores - biggest)
    return exponent / jnp.sum(exponent, axis=-1, keepdims=True)


def forward_group(queries, keys, values):
    parts = [None, None, None]
    for head in range(4):
        first, last, inside = head_window(head)
        softmax = softmax_of(masked(queries[:, first:last], inside), keys[:, first:last])
        result = dot(softmax.astype(BF16), masked(values[:, first:last], inside))
        for tile in range(first // LANES, last // LANES):
            piece = result[:, tile * LANES - first : (tile + 1) * LANES - first]
            parts[tile] = piece if parts[tile] is None else parts[tile] + piece
    return jnp.concatenate([part.astype(BF16) for part in parts], axis=1)


def forward_kernel(
    core_ref, normed_ref, weight_ref,
    tokens_hbm, out_hbm, head_hbm, rows_hbm, residual_hbm,
    projected_ref, fine_ref, own_ref, send_ref,
    tokens_ref, out_ref, head_ref, rows_ref, residual_ref, products, sems,
):
    step = pl.program_id(0)
    copies = [
        pltpu.make_async_copy(source, target, sems.at[place])
        for place, (source, target) in enumerate(
            (
                (tokens_hbm, tokens_ref),
                (out_hbm, out_ref),
                (head_hbm, head_ref),
                (rows_hbm, rows_ref),
                (residual_hbm, residual_ref),
            )
        )
    ]

    @pl.when(step == 3)
    def _():
        for copy in copies:
            copy.start()

    @pl.when(step < 2)
    def _():
        projected_ref[step, :ROWS] = dot(normed_ref[:ROWS], weight_ref[0]).astype(BF16)

    @pl.when(step >= 2)
    def _():
        projected_ref[step] = dot(normed_ref[...], weight_ref[0]).astype(BF16)

    @pl.when(step == 5)
    def _():
        attended = [
            forward_group(projected_ref[group, :ROWS], projected_ref[2 + group], projected_ref[4 + group])
            for group in range(2)
        ]
        for copy in copies:
            copy.wait()
        mixed = dot(attended[0], out_ref[:GROUP]) + dot(attended[1], out_ref[GROUP:])
        hidden = (tokens_ref[...].astype(F32) + mixed).astype(BF16)
        head_out = dot(hidden, head_ref[...])
        products[...] = dot_first(hidden, rows_ref[...])
        core = core_ref[0]
        for target, place in ((own_ref, core), (send_ref, 1 - core)):
            for quad in range(4):
                for phase in range(PHASES):
                    row = []
                    for z in range(ZS):
                        top = pl.multiple_of(place * 96 + z * 192 + quad * 24, 8)
                        row.append(products[pl.ds(top, 24), phase * LANES : phase * LANES + CHANNELS])
                    target[quad * 4 + phase] = jnp.concatenate(row, axis=1).astype(target.dtype)
        select = spread_matrix()
        for lat in range(LAT):
            at = slice(lat * LON_DEV, (lat + 1) * LON_DEV)
            stacked = jnp.concatenate(
                [head_out[at, phase * LANES : (phase + 1) * LANES] for phase in range(PHASES)], axis=0
            )
            high = stacked.astype(BF16)
            low = (stacked - high.astype(F32)).astype(BF16)
            spread = dot_first(high, select) + dot_first(low, select)
            across = slice(PHASES * lat, PHASES * (lat + 1))
            fine_ref[:, across, :] = spread[:CHANNELS].reshape(VARS, PHASES, LANES) + residual_ref[:, across, :]


def forward(core, normed, full, tokens, out_weight, head, rows, residual):
    fine = (VARS, 4 * LAT, LANES)
    pieces = (TILES, 24, WIDE)
    projected = (6, KEYS, GROUP)
    return pl.pallas_call(
        forward_kernel,
        out_shape=(
            jax.ShapeDtypeStruct(projected, BF16),
            jax.ShapeDtypeStruct(fine, F32),
            jax.ShapeDtypeStruct(pieces, F32),
            jax.ShapeDtypeStruct(pieces, BF16),
        ),
        grid=(6,),
        in_specs=[
            pl.BlockSpec(memory_space=pltpu.SMEM),
            whole_block((KEYS, D)),
            pl.BlockSpec((1, D, GROUP), lambda n: (n // 3, 0, n % 3)),
        ]
        + [pl.BlockSpec(memory_space=pl.ANY)] * 5,
        out_specs=(whole_block(projected), whole_block(fine), whole_block(pieces), whole_block(pieces)),
        scratch_shapes=[
            pltpu.VMEM((ROWS, D), BF16),
            pltpu.VMEM((INNER, D), BF16),
            pltpu.VMEM((D, PADDED), BF16),
            pltpu.VMEM((ROWS, PADDED), BF16),
            pltpu.VMEM(fine, F32),
            pltpu.VMEM((D, PADDED), F32),
            pltpu.SemaphoreType.DMA((5,)),
        ],
        name="forward",
    )(core, normed, full, tokens, out_weight, head, rows, residual)


def backward_kernel(
    q_ref, k_ref, v_ref, grad_ref,
    dq_ref, dk_ref, dv_ref, left_ref, right_ref,
):
    queries = q_ref[0, :ROWS]
    grads = grad_ref[...]
    keys = k_ref[0]
    values = v_ref[0]
    sums = [[None, None, None] for _ in range(3)]
    for head in range(4):
        first, last, inside = head_window(head)
        query = masked(queries[:, first:last], inside)
        grad = masked(grads[:, first:last], inside)
        softmax = softmax_of(query, keys[:, first:last])
        grad_weights = dot_last(grad, values[:, first:last])
        weighted = jnp.sum(softmax * grad_weights, axis=-1, keepdims=True)
        grad_scores = (softmax * (grad_weights - weighted)).astype(BF16)
        results = (
            dot(grad_scores, masked(keys[:, first:last], inside)),
            dot_first(grad_scores, query),
            dot_first(softmax.astype(BF16), grad),
        )
        for kept, result in zip(sums, results):
            for tile in range(first // LANES, last // LANES):
                piece = result[:, tile * LANES - first : (tile + 1) * LANES - first]
                kept[tile] = piece if kept[tile] is None else kept[tile] + piece
    for tile in range(3):
        at = slice(tile * LANES, (tile + 1) * LANES)
        dq_ref[:, at] = (sums[0][tile] * SCALE).astype(BF16)
        grad_keys = sums[1][tile] * SCALE
        grad_values = sums[2][tile]
        for kind, (grads_of, own) in enumerate(((grad_keys, dk_ref), (grad_values, dv_ref))):
            own[:, at] = grads_of[:ROWS]
            left_ref[kind, :, at] = grads_of[ROWS : ROWS + EDGE].astype(BF16)
            right_ref[kind, :, at] = grads_of[ROWS + EDGE :].astype(BF16)


def attend_backward(projected, grad_attended):
    def block(rows):
        return pl.BlockSpec((rows, GROUP), lambda n: (0, n))

    def shape(rows, kind):
        return jax.ShapeDtypeStruct((rows, INNER), kind)

    edge = jax.ShapeDtypeStruct((2, EDGE, INNER), BF16)
    edge_block = pl.BlockSpec((2, EDGE, GROUP), lambda n: (0, 0, n))
    return pl.pallas_call(
        backward_kernel,
        out_shape=(shape(ROWS, BF16), shape(ROWS, F32), shape(ROWS, F32), edge, edge),
        grid=(2,),
        in_specs=[pl.BlockSpec((1, KEYS, GROUP), lambda n, first=first: (first + n, 0, 0)) for first in (0, 2, 4)]
        + [block(ROWS)],
        out_specs=(block(ROWS), block(ROWS), block(ROWS), edge_block, edge_block),
        name="attend_backward",
    )(projected, projected, projected, grad_attended)


def norm_grad_kernel(
    dq_ref, dk_ref, dv_ref, left_ref, right_ref, low_ref, up_ref, gain_ref, tokens_hbm, hidden_hbm,
    out_ref, grads, total, tokens_ref, hidden_ref, sems,
):
    step = pl.program_id(0)
    copies = (
        pltpu.make_async_copy(tokens_hbm, tokens_ref, sems.at[0]),
        pltpu.make_async_copy(hidden_hbm, hidden_ref, sems.at[1]),
    )

    @pl.when(step == 0)
    def _():
        for copy in copies:
            copy.start()
        grads[:, :INNER] = dq_ref[...]
        for kind, own_ref in enumerate((dk_ref, dv_ref)):
            own = own_ref[...].reshape(LAT, LON_DEV, INNER)
            left = left_ref[kind].astype(F32).reshape(LAT, MARGIN, INNER)
            right = right_ref[kind].astype(F32).reshape(LAT, MARGIN, INNER)
            own = jnp.concatenate(
                [own[:, :MARGIN] + left, own[:, MARGIN : LON_DEV - MARGIN], own[:, LON_DEV - MARGIN :] + right],
                axis=1,
            )
            grads[:, (kind + 1) * INNER : (kind + 2) * INNER] = own.reshape(ROWS, INNER).astype(BF16)

    at = pl.ds(pl.multiple_of(step * 256, 256), 256)
    total[:, at] = dot_last(grads[:, :HALF_QKV], low_ref[0]) + dot_last(grads[:, HALF_QKV:], up_ref[0])

    @pl.when(step == 5)
    def _():
        for copy in copies:
            copy.wait()
        values = tokens_ref[...].astype(F32)
        standard, inverse_dev = standardized(values)
        grad_standard = total[...] * gain_ref[...]
        first_mean = jnp.mean(grad_standard, axis=-1, keepdims=True)
        second_mean = jnp.mean(grad_standard * standard, axis=-1, keepdims=True)
        grad = inverse_dev * (grad_standard - first_mean - standard * second_mean)
        out_ref[...] = (hidden_ref[...] + grad).astype(BF16)


def norm_grad(dq, dk, dv, from_left, from_right, full, tokens, gain, grad_hidden):
    return pl.pallas_call(
        norm_grad_kernel,
        out_shape=jax.ShapeDtypeStruct((ROWS, D), BF16),
        grid=(6,),
        in_specs=[
            whole_block((ROWS, INNER)),
            whole_block((ROWS, INNER)),
            whole_block((ROWS, INNER)),
            whole_block((2, EDGE, INNER)),
            whole_block((2, EDGE, INNER)),
            pl.BlockSpec((1, 256, HALF_QKV), lambda n: (0, n, 0)),
            pl.BlockSpec((1, 256, HALF_QKV), lambda n: (1, n, 0)),
            whole_block((1, D)),
            pl.BlockSpec(memory_space=pl.ANY),
            pl.BlockSpec(memory_space=pl.ANY),
        ],
        out_specs=whole_block((ROWS, D)),
        scratch_shapes=[
            pltpu.VMEM((ROWS, 3 * INNER), BF16),
            pltpu.VMEM((ROWS, D), F32),
            pltpu.VMEM((ROWS, D), BF16),
            pltpu.VMEM((ROWS, D), F32),
            pltpu.SemaphoreType.DMA((2,)),
        ],
        name="norm_grad",
    )(dq, dk, dv, from_left, from_right, full, full, gain, tokens, grad_hidden)


def sum_kernel(pieces_ref, out_ref):
    total = pieces_ref[0].astype(F32)
    for place in range(1, TILES):
        total = total + pieces_ref[place].astype(F32)
    empty = jnp.zeros((24, LANES - CHANNELS), F32)
    for z in range(ZS):
        part = jnp.concatenate([total[:, z * CHANNELS : (z + 1) * CHANNELS], empty], axis=1)
        out_ref[z] = part
        out_ref[ZS + z] = part


def sum_pieces(pieces):
    return pl.pallas_call(
        sum_kernel,
        out_shape=jax.ShapeDtypeStruct((2 * ZS, 24, LANES), F32),
        in_specs=[WHOLE],
        out_specs=WHOLE,
        name="sum_pieces",
    )(pieces)


def interp_weights(fine_index):
    coarse_cell = fine_index // 4
    phase_index = fine_index % 4
    lower_shift = (phase_index < 2).astype(jnp.int32)
    upper_weight = (2 * phase_index - 3 + 8 * lower_shift).astype(F32) / 8.0
    return (coarse_cell - lower_shift, upper_weight)


def build_matrix(lower_cell, upper_cell, upper_weight, count):
    columns = jnp.arange(count, dtype=jnp.int32)
    lower_part = jnp.where(columns[None, :] == lower_cell[:, None], 1.0 - upper_weight[:, None], 0.0)
    upper_portion = jnp.where(columns[None, :] == upper_cell[:, None], upper_weight[:, None], 0.0)
    return lower_part + upper_portion


def shifted(value, steps):
    return lax.ppermute(value, TILE, [(i, (i + steps) % TILES) for i in range(TILES)])


def residual_of(coarse):
    before = shifted(coarse[:, :, -1:], 1)
    after = shifted(coarse[:, :, :1], -1)
    padded = jnp.concatenate([before, coarse, after], axis=2)
    lat_lower, lat_upper_weight = interp_weights(jnp.arange(4 * LAT, dtype=jnp.int32))
    latitude_matrix = build_matrix(
        jnp.clip(lat_lower, 0, LAT - 1), jnp.clip(lat_lower + 1, 0, LAT - 1), lat_upper_weight, LAT
    )
    lon_lower, lon_upper_weight = interp_weights(jnp.arange(4 * LON_DEV, dtype=jnp.int32))
    lon_matrix = build_matrix(lon_lower + 1, lon_lower + 2, lon_upper_weight, LON_DEV + 2)
    incomplete_grid = jnp.einsum("lj,kji->kli", latitude_matrix, padded, precision=lax.Precision.HIGHEST)
    return jnp.einsum("vrb,cb->vrc", incomplete_grid, lon_matrix, precision=lax.Precision.HIGHEST)


def head_columns():
    target = jnp.arange(PADDED, dtype=jnp.int32)
    phase, channel = target // LANES, target % LANES
    source = jnp.where(channel < CHANNELS, channel * PHASES + phase, -1)
    return (jnp.arange(HEAD_OUT, dtype=jnp.int32)[:, None] == source[None, :]).astype(F32)


def gather_qkv(qkv):
    half = lax.axis_index("dp")
    qkv_half = lax.dynamic_slice_in_dim(qkv, half * HALF_QKV, HALF_QKV, 1)
    full = lax.all_gather(qkv_half, ("dp",) + FSDP, axis=0, tiled=True)
    return full.reshape(2, D, HALF_QKV)


def to_all(value, axes, count):
    copies = jnp.broadcast_to(value[None], (count,) + value.shape)
    return lax.all_to_all(copies, axes, 0, 0, tiled=True)


def gather_rest(core, out_w, head_w, ready):
    out_rows = out_w.reshape(48, 12, LANES).transpose(1, 0, 2).reshape(576, LANES)
    head_pad = dot(head_w, head_columns().astype(BF16)).astype(BF16)
    head_rows = head_pad.reshape(96, PHASES, LANES).transpose(1, 0, 2).reshape(384, LANES)
    rows = jnp.concatenate([out_rows, head_rows, jnp.zeros((PIECE, LANES), BF16)], axis=0)
    own = lax.dynamic_slice_in_dim(rows, lax.axis_index(TILE) * PIECE, PIECE, 0)
    over_z = to_all(own, ("z",), ZS)
    over_tile = to_all(over_z, TILE, TILES)
    over_tile = lax.optimization_barrier((over_tile, ready))[0]
    other = lax.ppermute(over_tile, "c", [(0, 1), (1, 0)])
    return unpack(core, over_tile, other)


def over_tiles(own, send):
    pair = own + lax.ppermute(send, "c", [(0, 1), (1, 0)]).astype(F32)
    return lax.all_to_all(pair.astype(BF16), TILE, 0, 0, tiled=True)


def over_samples(summed):
    both = lax.all_to_all(summed, ("dp", "z"), 0, 0, tiled=True)
    spread = to_all(jnp.sum(both, axis=0), TILE, TILES)
    padded = spread.reshape(4, PHASES, 24, LANES).transpose(0, 2, 1, 3).reshape(96, PADDED)
    return lax.dot_general(
        padded, head_columns(), (((1,), (1,)), ((), ())), precision=lax.Precision.HIGHEST, preferred_element_type=F32
    )


def shards(tokens, norm_gain, query_key_value_weight, out_weight, head_weight, coarse, grad_fine):
    tokens = tokens[0].reshape(ROWS, D)
    gain = norm_gain.reshape(1, D)
    full = gather_qkv(query_key_value_weight)
    grid = tokens.reshape(LAT, LON_DEV, D)
    left = shifted(grid[:, LON_DEV - MARGIN :].reshape(EDGE, D), 1)
    right = shifted(grid[:, :MARGIN].reshape(EDGE, D), -1)
    residual = residual_of(coarse[0])
    normed, rows = prepare(tokens, left, right, gain, grad_fine[0])
    core = lax.axis_index("c").reshape(1).astype(jnp.int32)
    out_full, head = gather_rest(core, out_weight, head_weight, (normed, residual))
    full, out_full, head, residual = lax.optimization_barrier((full, out_full, head, residual))
    projected, fine_grid, own, send = forward(core, normed, full, tokens, out_full, head, rows, residual)
    pieces = over_tiles(own, send)
    grad_hidden, grad_attended = hidden_grad(rows, head, out_full)
    dq, dk, dv, to_left, to_right = attend_backward(projected, grad_attended)
    pieces, to_left, to_right = lax.optimization_barrier((pieces, to_left, to_right))
    summed = sum_pieces(pieces)
    grad_head = over_samples(summed)
    to_left, to_right = lax.optimization_barrier((to_left, to_right, summed))[:2]
    from_right = shifted(to_left, -1)
    from_left = shifted(to_right, 1)
    grad_tokens = norm_grad(dq, dk, dv, from_left, from_right, full, tokens, gain, grad_hidden)
    return (fine_grid[None], grad_tokens.reshape(1, LAT, LON_DEV, D), grad_head)


def solution(mesh):
    fine_mesh = Mesh(mesh.devices.reshape(2, ZS, CORES, YS, XS), ("dp", "z", "c", "y", "x"))
    samples = ("dp", "z", "c")
    placed = (
        P(samples, None, TILE, None),
        P(),
        P(FSDP, None),
        P(FSDP, None),
        P(FSDP, None),
        P(samples, None, None, TILE),
        P(samples, None, None, TILE),
    )
    return jax.shard_map(
        shards,
        mesh=fine_mesh,
        in_specs=placed,
        out_specs=(P(samples, None, None, TILE), P(samples, None, TILE, None), P(FSDP, None)),
        check_vma=False,
    )
```

```python
import functools
import jax
import jax.numpy as jnp
from jax import lax
from jax.experimental import pallas as pl
from jax.experimental.pallas import tpu as pltpu
from jax.sharding import Mesh
from jax.sharding import PartitionSpec as P

D = 1536
HEADS = 8
HEAD_DIM = 96
VARS = 20
MARGIN = 8
LAT = 8
LON_DEV = 32
INNER = 768
HEAD_OUT = 320
ROWS = 256
EDGE = 64
KEYS = ROWS + 2 * EDGE
GROUP = 384
PAIR = 2 * INNER
ZS = 8
CORES = 2
YS = 4
XS = 4
TILES = 16
FSDP = ("z", "c")
TILE = ("y", "x")
HALF_QKV = 1152
HALF_OUT = 768
PIECE = 64
UNPACK = 4
WIDE = ZS * 80
PHASES = 4
CHANNELS = 80
LANES = 128
PADDED = PHASES * LANES
EPSILON = 1e-05
SCALE = HEAD_DIM ** (-0.5)
LOG2_E = 1.4426950408889634
F32 = jnp.float32
BF16 = jnp.bfloat16
WHOLE = pl.BlockSpec(memory_space=pltpu.VMEM)


def dot(left, right):
    return lax.dot_general(left, right, (((1,), (0,)), ((), ())), preferred_element_type=F32)


def dot_last(left, right):
    return lax.dot_general(left, right, (((1,), (1,)), ((), ())), preferred_element_type=F32)


def dot_first(left, right):
    return lax.dot_general(left, right, (((0,), (0,)), ((), ())), preferred_element_type=F32)


def spread_matrix():
    row = lax.broadcasted_iota(jnp.int32, (LANES, LANES), 0)
    lane = lax.broadcasted_iota(jnp.int32, (LANES, LANES), 1)
    target = (row % LON_DEV) * PHASES + row // LON_DEV
    return jnp.where(lane == target, 1.0, 0.0).astype(BF16)


def standardized(values):
    average = jnp.mean(values, axis=-1, keepdims=True)
    centred = values - average
    variance = jnp.mean(centred * centred, axis=-1, keepdims=True)
    inverse_dev = lax.rsqrt(variance + EPSILON)
    return centred * inverse_dev, inverse_dev


def prepare_kernel(tokens_ref, left_ref, right_ref, gain_ref, fine_ref, normed_ref, rows_ref):
    for source, first in ((tokens_ref, 0), (left_ref, ROWS), (right_ref, ROWS + EDGE)):
        standard, _ = standardized(source[...].astype(F32))
        normed_ref[first : first + source.shape[0]] = (standard * gain_ref[...]).astype(BF16)
    select = spread_matrix()
    empty = jnp.zeros((LANES - CHANNELS, LANES), BF16)
    for lat in range(LAT):
        block = fine_ref[:, PHASES * lat : PHASES * (lat + 1), :].reshape(CHANNELS, LANES)
        block = jnp.concatenate([block.astype(BF16), empty], axis=0)
        picked = dot_last(select, block).astype(BF16)
        for phase in range(PHASES):
            rows_ref[lat * LON_DEV : (lat + 1) * LON_DEV, phase * LANES : (phase + 1) * LANES] = picked[
                phase * LON_DEV : (phase + 1) * LON_DEV
            ]


def prepare(tokens, left, right, gain, grad_fine):
    return pl.pallas_call(
        prepare_kernel,
        out_shape=(
            jax.ShapeDtypeStruct((KEYS, D), BF16),
            jax.ShapeDtypeStruct((ROWS, PADDED), BF16),
        ),
        in_specs=[WHOLE] * 5,
        out_specs=(WHOLE, WHOLE),
        name="prepare",
    )(tokens, left, right, gain, grad_fine)


def unpack_kernel(core_ref, own_ref, other_ref, out_ref, head_ref):
    core = core_ref[0]
    for source, place in ((own_ref, core), (other_ref, 1 - core)):
        for tile in range(60):
            for z in range(UNPACK):
                block = source[tile // 4, z, tile % 4 * 16 : (tile % 4 + 1) * 16, :]
                if tile < 36:
                    top = pl.multiple_of(z * 96 + place * 48 + tile % 3 * 16, 16)
                    out_ref[pl.ds(top, 16), tile // 3 * LANES : (tile // 3 + 1) * LANES] = block
                else:
                    top = pl.multiple_of(z * 192 + place * 96 + tile % 6 * 16, 16)
                    phase = (tile - 36) // 6
                    head_ref[pl.ds(top, 16), phase * LANES : (phase + 1) * LANES] = block


def unpack(core, own, other):
    block = pl.BlockSpec((TILES, UNPACK, PIECE, LANES), lambda z: (0, z, 0, 0))
    return pl.pallas_call(
        unpack_kernel,
        out_shape=(
            jax.ShapeDtypeStruct((INNER, D), BF16),
            jax.ShapeDtypeStruct((D, PADDED), BF16),
        ),
        grid=(ZS // UNPACK,),
        in_specs=[pl.BlockSpec(memory_space=pltpu.SMEM), block, block],
        out_specs=(
            pl.BlockSpec((UNPACK * 96, D), lambda z: (z, 0)),
            pl.BlockSpec((UNPACK * 192, PADDED), lambda z: (z, 0)),
        ),
        name="unpack",
    )(core, own, other)


def hidden_grad_kernel(rows_ref, head_ref, out_ref, hidden_ref, attended_ref):
    grad_hidden = dot_last(rows_ref[...], head_ref[...])
    hidden_ref[...] = grad_hidden
    attended_ref[...] = dot_last(grad_hidden.astype(BF16), out_ref[...]).astype(BF16)


def hidden_grad(rows, head, out_weight):
    return pl.pallas_call(
        hidden_grad_kernel,
        out_shape=(
            jax.ShapeDtypeStruct((ROWS, D), F32),
            jax.ShapeDtypeStruct((ROWS, INNER), BF16),
        ),
        in_specs=[WHOLE, WHOLE, WHOLE],
        out_specs=(WHOLE, WHOLE),
        name="hidden_grad",
    )(rows, head, out_weight)


def whole_block(shape):
    return pl.BlockSpec(shape, lambda n: (0,) * len(shape))


def head_window(head):
    first = head * HEAD_DIM // LANES * LANES
    last = -(-(head + 1) * HEAD_DIM // LANES) * LANES
    lane = lax.broadcasted_iota(jnp.int32, (1, last - first), 1) + first
    inside = (lane >= head * HEAD_DIM) & (lane < (head + 1) * HEAD_DIM)
    return first, last, inside


def masked(values, inside):
    return jnp.where(inside, values, jnp.zeros_like(values))


def softmax_of(query, key):
    scores = dot_last(query, key)
    biggest = jnp.max(scores, axis=-1, keepdims=True)
    exponent = jnp.exp2((scores - biggest) * (SCALE * LOG2_E))
    return exponent * (1.0 / jnp.sum(exponent, axis=-1, keepdims=True))


def forward_group(queries, keys, values):
    parts = [None, None, None]
    for head in range(4):
        first, last, inside = head_window(head)
        softmax = softmax_of(masked(queries[:, first:last], inside), keys[:, first:last])
        result = dot(softmax.astype(BF16), masked(values[:, first:last], inside))
        for tile in range(first // LANES, last // LANES):
            piece = result[:, tile * LANES - first : (tile + 1) * LANES - first]
            parts[tile] = piece if parts[tile] is None else parts[tile] + piece
    return jnp.concatenate([part.astype(BF16) for part in parts], axis=1)


def forward_kernel(
    core_ref, normed_ref, weight_ref,
    tokens_hbm, out_hbm, head_hbm, rows_hbm, residual_hbm,
    projected_ref, fine_ref, own_ref, send_ref,
    tokens_ref, out_ref, head_ref, rows_ref, residual_ref, products, sems,
):
    step = pl.program_id(0)
    copies = [
        pltpu.make_async_copy(source, target, sems.at[place])
        for place, (source, target) in enumerate(
            (
                (tokens_hbm, tokens_ref),
                (out_hbm, out_ref),
                (head_hbm, head_ref),
                (rows_hbm, rows_ref),
                (residual_hbm, residual_ref),
            )
        )
    ]

    @pl.when(step == 3)
    def _():
        for copy in copies:
            copy.start()

    @pl.when(step < 2)
    def _():
        projected_ref[step, :ROWS] = dot(normed_ref[:ROWS], weight_ref[0]).astype(BF16)

    @pl.when(step >= 2)
    def _():
        projected_ref[step] = dot(normed_ref[...], weight_ref[0]).astype(BF16)

    @pl.when(step == 5)
    def _():
        attended = [
            forward_group(projected_ref[group, :ROWS], projected_ref[2 + group], projected_ref[4 + group])
            for group in range(2)
        ]
        for copy in copies:
            copy.wait()
        mixed = dot(attended[0], out_ref[:GROUP]) + dot(attended[1], out_ref[GROUP:])
        hidden = (tokens_ref[...].astype(F32) + mixed).astype(BF16)
        head_out = dot(hidden, head_ref[...])
        products[...] = dot_first(hidden, rows_ref[...])
        core = core_ref[0]
        for target, place in ((own_ref, core), (send_ref, 1 - core)):
            for quad in range(4):
                for phase in range(PHASES):
                    row = []
                    for z in range(ZS):
                        top = pl.multiple_of(place * 96 + z * 192 + quad * 24, 8)
                        row.append(products[pl.ds(top, 24), phase * LANES : phase * LANES + CHANNELS])
                    target[quad * 4 + phase] = jnp.concatenate(row, axis=1).astype(target.dtype)
        select = spread_matrix()
        for lat in range(LAT):
            at = slice(lat * LON_DEV, (lat + 1) * LON_DEV)
            stacked = jnp.concatenate(
                [head_out[at, phase * LANES : (phase + 1) * LANES] for phase in range(PHASES)], axis=0
            )
            high = stacked.astype(BF16)
            low = (stacked - high.astype(F32)).astype(BF16)
            spread = dot_first(high, select) + dot_first(low, select)
            across = slice(PHASES * lat, PHASES * (lat + 1))
            fine_ref[:, across, :] = spread[:CHANNELS].reshape(VARS, PHASES, LANES) + residual_ref[:, across, :]


def forward(core, normed, full, tokens, out_weight, head, rows, residual):
    fine = (VARS, 4 * LAT, LANES)
    pieces = (TILES, 24, WIDE)
    projected = (6, KEYS, GROUP)
    return pl.pallas_call(
        forward_kernel,
        out_shape=(
            jax.ShapeDtypeStruct(projected, BF16),
            jax.ShapeDtypeStruct(fine, F32),
            jax.ShapeDtypeStruct(pieces, F32),
            jax.ShapeDtypeStruct(pieces, BF16),
        ),
        grid=(6,),
        in_specs=[
            pl.BlockSpec(memory_space=pltpu.SMEM),
            whole_block((KEYS, D)),
            pl.BlockSpec((1, D, GROUP), lambda n: (n // 3, 0, n % 3)),
        ]
        + [pl.BlockSpec(memory_space=pl.ANY)] * 5,
        out_specs=(whole_block(projected), whole_block(fine), whole_block(pieces), whole_block(pieces)),
        scratch_shapes=[
            pltpu.VMEM((ROWS, D), BF16),
            pltpu.VMEM((INNER, D), BF16),
            pltpu.VMEM((D, PADDED), BF16),
            pltpu.VMEM((ROWS, PADDED), BF16),
            pltpu.VMEM(fine, F32),
            pltpu.VMEM((D, PADDED), F32),
            pltpu.SemaphoreType.DMA((5,)),
        ],
        name="forward",
    )(core, normed, full, tokens, out_weight, head, rows, residual)


def backward_kernel(
    q_ref, k_ref, v_ref, grad_ref,
    dq_ref, dk_ref, dv_ref, left_ref, right_ref,
):
    queries = q_ref[0, :ROWS]
    grads = grad_ref[...]
    keys = k_ref[0]
    values = v_ref[0]
    sums = [[None, None, None] for _ in range(3)]
    for head in range(4):
        first, last, inside = head_window(head)
        query = masked(queries[:, first:last], inside)
        grad = masked(grads[:, first:last], inside)
        softmax = softmax_of(query, keys[:, first:last])
        grad_weights = dot_last(grad, values[:, first:last])
        weighted = jnp.sum(softmax * grad_weights, axis=-1, keepdims=True)
        grad_scores = (softmax * (grad_weights - weighted)).astype(BF16)
        results = (
            dot(grad_scores, masked(keys[:, first:last], inside)),
            dot_first(grad_scores, query),
            dot_first(softmax.astype(BF16), grad),
        )
        for kept, result in zip(sums, results):
            for tile in range(first // LANES, last // LANES):
                piece = result[:, tile * LANES - first : (tile + 1) * LANES - first]
                kept[tile] = piece if kept[tile] is None else kept[tile] + piece
    for tile in range(3):
        at = slice(tile * LANES, (tile + 1) * LANES)
        dq_ref[:, at] = (sums[0][tile] * SCALE).astype(BF16)
        grad_keys = sums[1][tile] * SCALE
        grad_values = sums[2][tile]
        for kind, (grads_of, own) in enumerate(((grad_keys, dk_ref), (grad_values, dv_ref))):
            own[:, at] = grads_of[:ROWS]
            left_ref[kind, :, at] = grads_of[ROWS : ROWS + EDGE].astype(BF16)
            right_ref[kind, :, at] = grads_of[ROWS + EDGE :].astype(BF16)


def attend_backward(projected, grad_attended):
    def block(rows):
        return pl.BlockSpec((rows, GROUP), lambda n: (0, n))

    def shape(rows, kind):
        return jax.ShapeDtypeStruct((rows, INNER), kind)

    edge = jax.ShapeDtypeStruct((2, EDGE, INNER), BF16)
    edge_block = pl.BlockSpec((2, EDGE, GROUP), lambda n: (0, 0, n))
    return pl.pallas_call(
        backward_kernel,
        out_shape=(shape(ROWS, BF16), shape(ROWS, F32), shape(ROWS, F32), edge, edge),
        grid=(2,),
        in_specs=[pl.BlockSpec((1, KEYS, GROUP), lambda n, first=first: (first + n, 0, 0)) for first in (0, 2, 4)]
        + [block(ROWS)],
        out_specs=(block(ROWS), block(ROWS), block(ROWS), edge_block, edge_block),
        name="attend_backward",
    )(projected, projected, projected, grad_attended)


def norm_grad_kernel(
    dq_ref, dk_ref, dv_ref, left_ref, right_ref, low_ref, up_ref, gain_ref, tokens_hbm, hidden_hbm,
    out_ref, grads, total, tokens_ref, hidden_ref, sems,
):
    step = pl.program_id(0)
    copies = (
        pltpu.make_async_copy(tokens_hbm, tokens_ref, sems.at[0]),
        pltpu.make_async_copy(hidden_hbm, hidden_ref, sems.at[1]),
    )

    @pl.when(step == 0)
    def _():
        for copy in copies:
            copy.start()
        grads[:, :INNER] = dq_ref[...]
        for kind, own_ref in enumerate((dk_ref, dv_ref)):
            own = own_ref[...].reshape(LAT, LON_DEV, INNER)
            left = left_ref[kind].astype(F32).reshape(LAT, MARGIN, INNER)
            right = right_ref[kind].astype(F32).reshape(LAT, MARGIN, INNER)
            own = jnp.concatenate(
                [own[:, :MARGIN] + left, own[:, MARGIN : LON_DEV - MARGIN], own[:, LON_DEV - MARGIN :] + right],
                axis=1,
            )
            grads[:, (kind + 1) * INNER : (kind + 2) * INNER] = own.reshape(ROWS, INNER).astype(BF16)

    at = pl.ds(pl.multiple_of(step * 256, 256), 256)
    total[:, at] = dot_last(grads[:, :HALF_QKV], low_ref[0]) + dot_last(grads[:, HALF_QKV:], up_ref[0])

    @pl.when(step == 5)
    def _():
        for copy in copies:
            copy.wait()
        values = tokens_ref[...].astype(F32)
        standard, inverse_dev = standardized(values)
        grad_standard = total[...] * gain_ref[...]
        first_mean = jnp.mean(grad_standard, axis=-1, keepdims=True)
        second_mean = jnp.mean(grad_standard * standard, axis=-1, keepdims=True)
        grad = inverse_dev * (grad_standard - first_mean - standard * second_mean)
        out_ref[...] = (hidden_ref[...] + grad).astype(BF16)


def norm_grad(dq, dk, dv, from_left, from_right, full, tokens, gain, grad_hidden):
    return pl.pallas_call(
        norm_grad_kernel,
        out_shape=jax.ShapeDtypeStruct((ROWS, D), BF16),
        grid=(6,),
        in_specs=[
            whole_block((ROWS, INNER)),
            whole_block((ROWS, INNER)),
            whole_block((ROWS, INNER)),
            whole_block((2, EDGE, INNER)),
            whole_block((2, EDGE, INNER)),
            pl.BlockSpec((1, 256, HALF_QKV), lambda n: (0, n, 0)),
            pl.BlockSpec((1, 256, HALF_QKV), lambda n: (1, n, 0)),
            whole_block((1, D)),
            pl.BlockSpec(memory_space=pl.ANY),
            pl.BlockSpec(memory_space=pl.ANY),
        ],
        out_specs=whole_block((ROWS, D)),
        scratch_shapes=[
            pltpu.VMEM((ROWS, 3 * INNER), BF16),
            pltpu.VMEM((ROWS, D), F32),
            pltpu.VMEM((ROWS, D), BF16),
            pltpu.VMEM((ROWS, D), F32),
            pltpu.SemaphoreType.DMA((2,)),
        ],
        name="norm_grad",
    )(dq, dk, dv, from_left, from_right, full, full, gain, tokens, grad_hidden)


def sum_kernel(pieces_ref, out_ref):
    total = pieces_ref[0].astype(F32)
    for place in range(1, TILES):
        total = total + pieces_ref[place].astype(F32)
    empty = jnp.zeros((24, LANES - CHANNELS), F32)
    for z in range(ZS):
        part = jnp.concatenate([total[:, z * CHANNELS : (z + 1) * CHANNELS], empty], axis=1)
        out_ref[z] = part
        out_ref[ZS + z] = part


def sum_pieces(pieces):
    return pl.pallas_call(
        sum_kernel,
        out_shape=jax.ShapeDtypeStruct((2 * ZS, 24, LANES), F32),
        in_specs=[WHOLE],
        out_specs=WHOLE,
        name="sum_pieces",
    )(pieces)


def interp_weights(fine_index):
    coarse_cell = fine_index // 4
    phase_index = fine_index % 4
    lower_shift = (phase_index < 2).astype(jnp.int32)
    upper_weight = (2 * phase_index - 3 + 8 * lower_shift).astype(F32) / 8.0
    return (coarse_cell - lower_shift, upper_weight)


def build_matrix(lower_cell, upper_cell, upper_weight, count):
    columns = jnp.arange(count, dtype=jnp.int32)
    lower_part = jnp.where(columns[None, :] == lower_cell[:, None], 1.0 - upper_weight[:, None], 0.0)
    upper_portion = jnp.where(columns[None, :] == upper_cell[:, None], upper_weight[:, None], 0.0)
    return lower_part + upper_portion


def shifted(value, steps):
    return lax.ppermute(value, TILE, [(i, (i + steps) % TILES) for i in range(TILES)])


def residual_of(coarse):
    before = shifted(coarse[:, :, -1:], 1)
    after = shifted(coarse[:, :, :1], -1)
    padded = jnp.concatenate([before, coarse, after], axis=2)
    lat_lower, lat_upper_weight = interp_weights(jnp.arange(4 * LAT, dtype=jnp.int32))
    latitude_matrix = build_matrix(
        jnp.clip(lat_lower, 0, LAT - 1), jnp.clip(lat_lower + 1, 0, LAT - 1), lat_upper_weight, LAT
    )
    lon_lower, lon_upper_weight = interp_weights(jnp.arange(4 * LON_DEV, dtype=jnp.int32))
    lon_matrix = build_matrix(lon_lower + 1, lon_lower + 2, lon_upper_weight, LON_DEV + 2)
    incomplete_grid = jnp.einsum("lj,kji->kli", latitude_matrix, padded, precision=lax.Precision.HIGHEST)
    return jnp.einsum("vrb,cb->vrc", incomplete_grid, lon_matrix, precision=lax.Precision.HIGHEST)


def head_columns():
    target = jnp.arange(PADDED, dtype=jnp.int32)
    phase, channel = target // LANES, target % LANES
    source = jnp.where(channel < CHANNELS, channel * PHASES + phase, -1)
    return (jnp.arange(HEAD_OUT, dtype=jnp.int32)[:, None] == source[None, :]).astype(F32)


def gather_qkv(qkv):
    half = lax.axis_index("dp")
    qkv_half = lax.dynamic_slice_in_dim(qkv, half * HALF_QKV, HALF_QKV, 1)
    full = lax.all_gather(qkv_half, ("dp",) + FSDP, axis=0, tiled=True)
    return full.reshape(2, D, HALF_QKV)


def to_all(value, axes, count):
    copies = jnp.broadcast_to(value[None], (count,) + value.shape)
    return lax.all_to_all(copies, axes, 0, 0, tiled=True)


def gather_rest(core, out_w, head_w, ready):
    out_rows = out_w.reshape(48, 12, LANES).transpose(1, 0, 2).reshape(576, LANES)
    head_pad = dot(head_w, head_columns().astype(BF16)).astype(BF16)
    head_rows = head_pad.reshape(96, PHASES, LANES).transpose(1, 0, 2).reshape(384, LANES)
    rows = jnp.concatenate([out_rows, head_rows, jnp.zeros((PIECE, LANES), BF16)], axis=0)
    own = lax.dynamic_slice_in_dim(rows, lax.axis_index(TILE) * PIECE, PIECE, 0)
    over_z = to_all(own, ("z",), ZS)
    over_tile = to_all(over_z, TILE, TILES)
    over_tile = lax.optimization_barrier((over_tile, ready))[0]
    other = lax.ppermute(over_tile, "c", [(0, 1), (1, 0)])
    return unpack(core, over_tile, other)


def over_tiles(own, send):
    pair = own + lax.ppermute(send, "c", [(0, 1), (1, 0)]).astype(F32)
    return lax.all_to_all(pair.astype(BF16), TILE, 0, 0, tiled=True)


def over_samples(summed):
    both = lax.all_to_all(summed, ("dp", "z"), 0, 0, tiled=True)
    spread = to_all(jnp.sum(both, axis=0), TILE, TILES)
    padded = spread.reshape(4, PHASES, 24, LANES).transpose(0, 2, 1, 3).reshape(96, PADDED)
    return lax.dot_general(
        padded, head_columns(), (((1,), (1,)), ((), ())), precision=lax.Precision.HIGHEST, preferred_element_type=F32
    )


def shards(tokens, norm_gain, query_key_value_weight, out_weight, head_weight, coarse, grad_fine):
    tokens = tokens[0].reshape(ROWS, D)
    gain = norm_gain.reshape(1, D)
    full = gather_qkv(query_key_value_weight)
    grid = tokens.reshape(LAT, LON_DEV, D)
    left = shifted(grid[:, LON_DEV - MARGIN :].reshape(EDGE, D), 1)
    right = shifted(grid[:, :MARGIN].reshape(EDGE, D), -1)
    residual = residual_of(coarse[0])
    normed, rows = prepare(tokens, left, right, gain, grad_fine[0])
    core = lax.axis_index("c").reshape(1).astype(jnp.int32)
    out_full, head = gather_rest(core, out_weight, head_weight, (normed, residual))
    full, out_full, head, residual = lax.optimization_barrier((full, out_full, head, residual))
    projected, fine_grid, own, send = forward(core, normed, full, tokens, out_full, head, rows, residual)
    pieces = over_tiles(own, send)
    grad_hidden, grad_attended = hidden_grad(rows, head, out_full)
    pieces, grad_attended = lax.optimization_barrier((pieces, grad_attended))
    summed = sum_pieces(pieces)
    grad_attended = lax.optimization_barrier((grad_attended, summed))[0]
    dq, dk, dv, to_left, to_right = attend_backward(projected, grad_attended)
    grad_head = over_samples(summed)
    from_right = shifted(to_left, -1)
    from_left = shifted(to_right, 1)
    grad_tokens = norm_grad(dq, dk, dv, from_left, from_right, full, tokens, gain, grad_hidden)
    return (fine_grid[None], grad_tokens.reshape(1, LAT, LON_DEV, D), grad_head)


def solution(mesh):
    fine_mesh = Mesh(mesh.devices.reshape(2, ZS, CORES, YS, XS), ("dp", "z", "c", "y", "x"))
    samples = ("dp", "z", "c")
    placed = (
        P(samples, None, TILE, None),
        P(),
        P(FSDP, None),
        P(FSDP, None),
        P(FSDP, None),
        P(samples, None, None, TILE),
        P(samples, None, None, TILE),
    )
    return jax.shard_map(
        shards,
        mesh=fine_mesh,
        in_specs=placed,
        out_specs=(P(samples, None, None, TILE), P(samples, None, TILE, None), P(FSDP, None)),
        check_vma=False,
    )
```

```python
import functools
import jax
import jax.numpy as jnp
from jax import lax
from jax.experimental import pallas as pl
from jax.experimental.pallas import tpu as pltpu
from jax.sharding import Mesh
from jax.sharding import PartitionSpec as P

D = 1536
HEADS = 8
HEAD_DIM = 96
VARS = 20
MARGIN = 8
LAT = 8
LON_DEV = 32
INNER = 768
HEAD_OUT = 320
ROWS = 256
EDGE = 64
KEYS = ROWS + 2 * EDGE
GROUP = 384
PAIR = 2 * INNER
ZS = 8
CORES = 2
YS = 4
XS = 4
TILES = 16
FSDP = ("z", "c")
TILE = ("y", "x")
HALF_QKV = 1152
HALF_OUT = 768
PIECE = 64
UNPACK = 4
WIDE = ZS * 80
PHASES = 4
CHANNELS = 80
LANES = 128
PADDED = PHASES * LANES
EPSILON = 1e-05
SCALE = HEAD_DIM ** (-0.5)
LOG2_E = 1.4426950408889634
F32 = jnp.float32
BF16 = jnp.bfloat16
WHOLE = pl.BlockSpec(memory_space=pltpu.VMEM)


def dot(left, right):
    return lax.dot_general(left, right, (((1,), (0,)), ((), ())), preferred_element_type=F32)


def dot_last(left, right):
    return lax.dot_general(left, right, (((1,), (1,)), ((), ())), preferred_element_type=F32)


def dot_first(left, right):
    return lax.dot_general(left, right, (((0,), (0,)), ((), ())), preferred_element_type=F32)


def spread_matrix():
    row = lax.broadcasted_iota(jnp.int32, (LANES, LANES), 0)
    lane = lax.broadcasted_iota(jnp.int32, (LANES, LANES), 1)
    target = (row % LON_DEV) * PHASES + row // LON_DEV
    return jnp.where(lane == target, 1.0, 0.0).astype(BF16)


def standardized(values):
    average = jnp.mean(values, axis=-1, keepdims=True)
    centred = values - average
    variance = jnp.mean(centred * centred, axis=-1, keepdims=True)
    inverse_dev = lax.rsqrt(variance + EPSILON)
    return centred * inverse_dev, inverse_dev


def prepare_kernel(tokens_ref, left_ref, right_ref, gain_ref, fine_ref, normed_ref, rows_ref):
    for source, first in ((tokens_ref, 0), (left_ref, ROWS), (right_ref, ROWS + EDGE)):
        standard, _ = standardized(source[...].astype(F32))
        normed_ref[first : first + source.shape[0]] = (standard * gain_ref[...]).astype(BF16)
    select = spread_matrix()
    empty = jnp.zeros((LANES - CHANNELS, LANES), BF16)
    for lat in range(LAT):
        block = fine_ref[:, PHASES * lat : PHASES * (lat + 1), :].reshape(CHANNELS, LANES)
        block = jnp.concatenate([block.astype(BF16), empty], axis=0)
        picked = dot_last(select, block).astype(BF16)
        for phase in range(PHASES):
            rows_ref[lat * LON_DEV : (lat + 1) * LON_DEV, phase * LANES : (phase + 1) * LANES] = picked[
                phase * LON_DEV : (phase + 1) * LON_DEV
            ]


def prepare(tokens, left, right, gain, grad_fine):
    return pl.pallas_call(
        prepare_kernel,
        out_shape=(
            jax.ShapeDtypeStruct((KEYS, D), BF16),
            jax.ShapeDtypeStruct((ROWS, PADDED), BF16),
        ),
        in_specs=[WHOLE] * 5,
        out_specs=(WHOLE, WHOLE),
        name="prepare",
    )(tokens, left, right, gain, grad_fine)


def unpack_kernel(core_ref, own_ref, other_ref, out_ref, head_ref):
    core = core_ref[0]
    for source, place in ((own_ref, core), (other_ref, 1 - core)):
        for tile in range(60):
            for z in range(UNPACK):
                block = source[tile // 4, z, tile % 4 * 16 : (tile % 4 + 1) * 16, :]
                if tile < 36:
                    top = pl.multiple_of(z * 96 + place * 48 + tile % 3 * 16, 16)
                    out_ref[pl.ds(top, 16), tile // 3 * LANES : (tile // 3 + 1) * LANES] = block
                else:
                    top = pl.multiple_of(z * 192 + place * 96 + tile % 6 * 16, 16)
                    phase = (tile - 36) // 6
                    head_ref[pl.ds(top, 16), phase * LANES : (phase + 1) * LANES] = block


def unpack(core, own, other):
    block = pl.BlockSpec((TILES, UNPACK, PIECE, LANES), lambda z: (0, z, 0, 0))
    return pl.pallas_call(
        unpack_kernel,
        out_shape=(
            jax.ShapeDtypeStruct((INNER, D), BF16),
            jax.ShapeDtypeStruct((D, PADDED), BF16),
        ),
        grid=(ZS // UNPACK,),
        in_specs=[pl.BlockSpec(memory_space=pltpu.SMEM), block, block],
        out_specs=(
            pl.BlockSpec((UNPACK * 96, D), lambda z: (z, 0)),
            pl.BlockSpec((UNPACK * 192, PADDED), lambda z: (z, 0)),
        ),
        name="unpack",
    )(core, own, other)


def hidden_grad_kernel(rows_ref, head_ref, out_ref, hidden_ref, attended_ref):
    grad_hidden = dot_last(rows_ref[...], head_ref[...])
    hidden_ref[...] = grad_hidden
    attended_ref[...] = dot_last(grad_hidden.astype(BF16), out_ref[...]).astype(BF16)


def hidden_grad(rows, head, out_weight):
    return pl.pallas_call(
        hidden_grad_kernel,
        out_shape=(
            jax.ShapeDtypeStruct((ROWS, D), F32),
            jax.ShapeDtypeStruct((ROWS, INNER), BF16),
        ),
        in_specs=[WHOLE, WHOLE, WHOLE],
        out_specs=(WHOLE, WHOLE),
        name="hidden_grad",
    )(rows, head, out_weight)


def whole_block(shape):
    return pl.BlockSpec(shape, lambda n: (0,) * len(shape))


def head_window(head):
    first = head * HEAD_DIM // LANES * LANES
    last = -(-(head + 1) * HEAD_DIM // LANES) * LANES
    lane = lax.broadcasted_iota(jnp.int32, (1, last - first), 1) + first
    inside = (lane >= head * HEAD_DIM) & (lane < (head + 1) * HEAD_DIM)
    return first, last, inside


def masked(values, inside):
    return jnp.where(inside, values, jnp.zeros_like(values))


def softmax_of(query, key):
    scores = dot_last(query, key)
    biggest = jnp.max(scores, axis=-1, keepdims=True)
    exponent = jnp.exp2((scores - biggest) * (SCALE * LOG2_E))
    return exponent * (1.0 / jnp.sum(exponent, axis=-1, keepdims=True))


def forward_group(queries, keys, values):
    parts = [None, None, None]
    for head in range(4):
        first, last, inside = head_window(head)
        softmax = softmax_of(masked(queries[:, first:last], inside), keys[:, first:last])
        result = dot(softmax.astype(BF16), masked(values[:, first:last], inside))
        for tile in range(first // LANES, last // LANES):
            piece = result[:, tile * LANES - first : (tile + 1) * LANES - first]
            parts[tile] = piece if parts[tile] is None else parts[tile] + piece
    return jnp.concatenate([part.astype(BF16) for part in parts], axis=1)


def forward_kernel(
    normed_ref, weight_ref,
    tokens_hbm, out_hbm, head_hbm, rows_hbm, residual_hbm,
    projected_out, fine_ref, pieces_hbm,
    projected_ref, pieces_ref, tokens_ref, out_ref, head_ref, rows_ref, residual_ref, products, sems,
):
    step = pl.program_id(0)
    copies = [
        pltpu.make_async_copy(source, target, sems.at[place])
        for place, (source, target) in enumerate(
            (
                (tokens_hbm, tokens_ref),
                (out_hbm, out_ref),
                (head_hbm, head_ref),
                (rows_hbm, rows_ref),
                (residual_hbm, residual_ref),
            )
        )
    ]

    @pl.when(step == 3)
    def _():
        for copy in copies:
            copy.start()

    @pl.when(step < 2)
    def _():
        queries = dot(normed_ref[:ROWS], weight_ref[0]).astype(BF16)
        projected_ref[step, :ROWS] = queries
        projected_out[0, :ROWS] = queries
        projected_out[0, ROWS:] = jnp.zeros((2 * EDGE, GROUP), BF16)

    @pl.when(step >= 2)
    def _():
        pairs = dot(normed_ref[...], weight_ref[0]).astype(BF16)
        projected_ref[step] = pairs
        projected_out[0] = pairs

    @pl.when(step == 5)
    def _():
        attended = [
            forward_group(projected_ref[group, :ROWS], projected_ref[2 + group], projected_ref[4 + group])
            for group in range(2)
        ]
        for copy in copies:
            copy.wait()
        mixed = dot(attended[0], out_ref[:GROUP]) + dot(attended[1], out_ref[GROUP:])
        hidden = (tokens_ref[...].astype(F32) + mixed).astype(BF16)
        products[...] = dot_first(hidden, rows_ref[...])
        for core in range(CORES):
            for quad in range(4):
                for phase in range(PHASES):
                    row = [
                        products[
                            (z * CORES + core) * 96 + quad * 24 : (z * CORES + core) * 96 + quad * 24 + 24,
                            phase * LANES : phase * LANES + CHANNELS,
                        ]
                        for z in range(ZS)
                    ]
                    pieces_ref[core * TILES + quad * 4 + phase] = jnp.concatenate(row, axis=1).astype(BF16)
        send = pltpu.make_async_copy(pieces_ref, pieces_hbm, sems.at[5])
        send.start()
        head_out = dot(hidden, head_ref[...])
        select = spread_matrix()
        for lat in range(LAT):
            at = slice(lat * LON_DEV, (lat + 1) * LON_DEV)
            stacked = jnp.concatenate(
                [head_out[at, phase * LANES : (phase + 1) * LANES] for phase in range(PHASES)], axis=0
            )
            high = stacked.astype(BF16)
            low = (stacked - high.astype(F32)).astype(BF16)
            spread = dot_first(high, select) + dot_first(low, select)
            across = slice(PHASES * lat, PHASES * (lat + 1))
            fine_ref[:, across, :] = spread[:CHANNELS].reshape(VARS, PHASES, LANES) + residual_ref[:, across, :]
        send.wait()


def forward(normed, full, tokens, out_weight, head, rows, residual):
    fine = (VARS, 4 * LAT, LANES)
    pieces = (CORES * TILES, 24, WIDE)
    projected = (6, KEYS, GROUP)
    return pl.pallas_call(
        forward_kernel,
        out_shape=(
            jax.ShapeDtypeStruct(projected, BF16),
            jax.ShapeDtypeStruct(fine, F32),
            jax.ShapeDtypeStruct(pieces, BF16),
        ),
        grid=(6,),
        in_specs=[
            whole_block((KEYS, D)),
            pl.BlockSpec((1, D, GROUP), lambda n: (n // 3, 0, n % 3)),
        ]
        + [pl.BlockSpec(memory_space=pl.ANY)] * 5,
        out_specs=(
            pl.BlockSpec((1, KEYS, GROUP), lambda n: (n, 0, 0)),
            whole_block(fine),
            pl.BlockSpec(memory_space=pl.ANY),
        ),
        scratch_shapes=[
            pltpu.VMEM(projected, BF16),
            pltpu.VMEM(pieces, BF16),
            pltpu.VMEM((ROWS, D), BF16),
            pltpu.VMEM((INNER, D), BF16),
            pltpu.VMEM((D, PADDED), BF16),
            pltpu.VMEM((ROWS, PADDED), BF16),
            pltpu.VMEM(fine, F32),
            pltpu.VMEM((D, PADDED), F32),
            pltpu.SemaphoreType.DMA((6,)),
        ],
        name="forward",
    )(normed, full, tokens, out_weight, head, rows, residual)


def backward_kernel(
    q_ref, k_ref, v_ref, grad_ref,
    dq_ref, dk_ref, dv_ref, left_ref, right_ref,
):
    queries = q_ref[0, :ROWS]
    grads = grad_ref[...]
    keys = k_ref[0]
    values = v_ref[0]
    sums = [[None, None, None] for _ in range(3)]
    for head in range(4):
        first, last, inside = head_window(head)
        query = masked(queries[:, first:last], inside)
        grad = masked(grads[:, first:last], inside)
        softmax = softmax_of(query, keys[:, first:last])
        grad_weights = dot_last(grad, values[:, first:last])
        weighted = jnp.sum(softmax * grad_weights, axis=-1, keepdims=True)
        grad_scores = (softmax * (grad_weights - weighted)).astype(BF16)
        results = (
            dot(grad_scores, masked(keys[:, first:last], inside)),
            dot_first(grad_scores, query),
            dot_first(softmax.astype(BF16), grad),
        )
        for kept, result in zip(sums, results):
            for tile in range(first // LANES, last // LANES):
                piece = result[:, tile * LANES - first : (tile + 1) * LANES - first]
                kept[tile] = piece if kept[tile] is None else kept[tile] + piece
    for tile in range(3):
        at = slice(tile * LANES, (tile + 1) * LANES)
        dq_ref[:, at] = (sums[0][tile] * SCALE).astype(BF16)
        grad_keys = sums[1][tile] * SCALE
        grad_values = sums[2][tile]
        for kind, (grads_of, own) in enumerate(((grad_keys, dk_ref), (grad_values, dv_ref))):
            own[:, at] = grads_of[:ROWS]
            left_ref[kind, :, at] = grads_of[ROWS : ROWS + EDGE].astype(BF16)
            right_ref[kind, :, at] = grads_of[ROWS + EDGE :].astype(BF16)


def attend_backward(projected, grad_attended):
    def block(rows):
        return pl.BlockSpec((rows, GROUP), lambda n: (0, n))

    def shape(rows, kind):
        return jax.ShapeDtypeStruct((rows, INNER), kind)

    edge = jax.ShapeDtypeStruct((2, EDGE, INNER), BF16)
    edge_block = pl.BlockSpec((2, EDGE, GROUP), lambda n: (0, 0, n))
    return pl.pallas_call(
        backward_kernel,
        out_shape=(shape(ROWS, BF16), shape(ROWS, F32), shape(ROWS, F32), edge, edge),
        grid=(2,),
        in_specs=[pl.BlockSpec((1, KEYS, GROUP), lambda n, first=first: (first + n, 0, 0)) for first in (0, 2, 4)]
        + [block(ROWS)],
        out_specs=(block(ROWS), block(ROWS), block(ROWS), edge_block, edge_block),
        name="attend_backward",
    )(projected, projected, projected, grad_attended)


def norm_grad_kernel(
    dq_ref, dk_ref, dv_ref, left_ref, right_ref, low_ref, up_ref, gain_ref, tokens_hbm, hidden_hbm,
    out_ref, grads, total, tokens_ref, hidden_ref, sems,
):
    step = pl.program_id(0)
    copies = (
        pltpu.make_async_copy(tokens_hbm, tokens_ref, sems.at[0]),
        pltpu.make_async_copy(hidden_hbm, hidden_ref, sems.at[1]),
    )

    @pl.when(step == 0)
    def _():
        for copy in copies:
            copy.start()
        grads[:, :INNER] = dq_ref[...]
        for kind, own_ref in enumerate((dk_ref, dv_ref)):
            own = own_ref[...].reshape(LAT, LON_DEV, INNER)
            left = left_ref[kind].astype(F32).reshape(LAT, MARGIN, INNER)
            right = right_ref[kind].astype(F32).reshape(LAT, MARGIN, INNER)
            own = jnp.concatenate(
                [own[:, :MARGIN] + left, own[:, MARGIN : LON_DEV - MARGIN], own[:, LON_DEV - MARGIN :] + right],
                axis=1,
            )
            grads[:, (kind + 1) * INNER : (kind + 2) * INNER] = own.reshape(ROWS, INNER).astype(BF16)

    at = pl.ds(pl.multiple_of(step * 256, 256), 256)
    total[:, at] = dot_last(grads[:, :HALF_QKV], low_ref[0]) + dot_last(grads[:, HALF_QKV:], up_ref[0])

    @pl.when(step == 5)
    def _():
        for copy in copies:
            copy.wait()
        values = tokens_ref[...].astype(F32)
        standard, inverse_dev = standardized(values)
        grad_standard = total[...] * gain_ref[...]
        first_mean = jnp.mean(grad_standard, axis=-1, keepdims=True)
        second_mean = jnp.mean(grad_standard * standard, axis=-1, keepdims=True)
        grad = inverse_dev * (grad_standard - first_mean - standard * second_mean)
        out_ref[...] = (hidden_ref[...] + grad).astype(BF16)


def norm_grad(dq, dk, dv, from_left, from_right, full, tokens, gain, grad_hidden):
    return pl.pallas_call(
        norm_grad_kernel,
        out_shape=jax.ShapeDtypeStruct((ROWS, D), BF16),
        grid=(6,),
        in_specs=[
            whole_block((ROWS, INNER)),
            whole_block((ROWS, INNER)),
            whole_block((ROWS, INNER)),
            whole_block((2, EDGE, INNER)),
            whole_block((2, EDGE, INNER)),
            pl.BlockSpec((1, 256, HALF_QKV), lambda n: (0, n, 0)),
            pl.BlockSpec((1, 256, HALF_QKV), lambda n: (1, n, 0)),
            whole_block((1, D)),
            pl.BlockSpec(memory_space=pl.ANY),
            pl.BlockSpec(memory_space=pl.ANY),
        ],
        out_specs=whole_block((ROWS, D)),
        scratch_shapes=[
            pltpu.VMEM((ROWS, 3 * INNER), BF16),
            pltpu.VMEM((ROWS, D), F32),
            pltpu.VMEM((ROWS, D), BF16),
            pltpu.VMEM((ROWS, D), F32),
            pltpu.SemaphoreType.DMA((2,)),
        ],
        name="norm_grad",
    )(dq, dk, dv, from_left, from_right, full, full, gain, tokens, grad_hidden)


def sum_kernel(pieces_ref, out_ref):
    total = pieces_ref[0].astype(F32)
    for place in range(1, CORES * TILES):
        total = total + pieces_ref[place].astype(F32)
    empty = jnp.zeros((24, LANES - CHANNELS), F32)
    for z in range(ZS):
        part = jnp.concatenate([total[:, z * CHANNELS : (z + 1) * CHANNELS], empty], axis=1).astype(BF16)
        out_ref[z] = part
        out_ref[ZS + z] = part


def sum_pieces(pieces):
    return pl.pallas_call(
        sum_kernel,
        out_shape=jax.ShapeDtypeStruct((2 * ZS, 24, LANES), BF16),
        in_specs=[WHOLE],
        out_specs=WHOLE,
        name="sum_pieces",
    )(pieces)


def interp_weights(fine_index):
    coarse_cell = fine_index // 4
    phase_index = fine_index % 4
    lower_shift = (phase_index < 2).astype(jnp.int32)
    upper_weight = (2 * phase_index - 3 + 8 * lower_shift).astype(F32) / 8.0
    return (coarse_cell - lower_shift, upper_weight)


def build_matrix(lower_cell, upper_cell, upper_weight, count):
    columns = jnp.arange(count, dtype=jnp.int32)
    lower_part = jnp.where(columns[None, :] == lower_cell[:, None], 1.0 - upper_weight[:, None], 0.0)
    upper_portion = jnp.where(columns[None, :] == upper_cell[:, None], upper_weight[:, None], 0.0)
    return lower_part + upper_portion


def shifted(value, steps):
    return lax.ppermute(value, TILE, [(i, (i + steps) % TILES) for i in range(TILES)])


def residual_of(coarse):
    before = shifted(coarse[:, :, -1:], 1)
    after = shifted(coarse[:, :, :1], -1)
    padded = jnp.concatenate([before, coarse, after], axis=2)
    lat_lower, lat_upper_weight = interp_weights(jnp.arange(4 * LAT, dtype=jnp.int32))
    latitude_matrix = build_matrix(
        jnp.clip(lat_lower, 0, LAT - 1), jnp.clip(lat_lower + 1, 0, LAT - 1), lat_upper_weight, LAT
    )
    lon_lower, lon_upper_weight = interp_weights(jnp.arange(4 * LON_DEV, dtype=jnp.int32))
    lon_matrix = build_matrix(lon_lower + 1, lon_lower + 2, lon_upper_weight, LON_DEV + 2)
    incomplete_grid = jnp.einsum("lj,kji->kli", latitude_matrix, padded, precision=lax.Precision.HIGHEST)
    return jnp.einsum("vrb,cb->vrc", incomplete_grid, lon_matrix, precision=lax.Precision.HIGHEST)


def head_columns():
    target = jnp.arange(PADDED, dtype=jnp.int32)
    phase, channel = target // LANES, target % LANES
    source = jnp.where(channel < CHANNELS, channel * PHASES + phase, -1)
    return (jnp.arange(HEAD_OUT, dtype=jnp.int32)[:, None] == source[None, :]).astype(F32)


def gather_qkv(qkv):
    half = lax.axis_index("dp")
    qkv_half = lax.dynamic_slice_in_dim(qkv, half * HALF_QKV, HALF_QKV, 1)
    full = lax.all_gather(qkv_half, ("dp",) + FSDP, axis=0, tiled=True)
    return full.reshape(2, D, HALF_QKV)


def to_all(value, axes, count):
    copies = jnp.broadcast_to(value[None], (count,) + value.shape)
    return lax.all_to_all(copies, axes, 0, 0, tiled=True)


def gather_rest(core, out_w, head_w, ready):
    out_rows = out_w.reshape(48, 12, LANES).transpose(1, 0, 2).reshape(576, LANES)
    head_pad = dot(head_w, head_columns().astype(BF16)).astype(BF16)
    head_rows = head_pad.reshape(96, PHASES, LANES).transpose(1, 0, 2).reshape(384, LANES)
    rows = jnp.concatenate([out_rows, head_rows, jnp.zeros((PIECE, LANES), BF16)], axis=0)
    own = lax.dynamic_slice_in_dim(rows, lax.axis_index(TILE) * PIECE, PIECE, 0)
    over_z = to_all(own, ("z",), ZS)
    over_tile = to_all(over_z, TILE, TILES)
    over_tile = lax.optimization_barrier((over_tile, ready))[0]
    other = lax.ppermute(over_tile, "c", [(0, 1), (1, 0)])
    return unpack(core, over_tile, other)


def over_samples(summed):
    both = lax.all_to_all(summed, ("dp", "z"), 0, 0, tiled=True)
    spread = to_all(jnp.sum(both.astype(F32), axis=0), TILE, TILES)
    padded = spread.reshape(4, PHASES, 24, LANES).transpose(0, 2, 1, 3).reshape(96, PADDED)
    return lax.dot_general(
        padded, head_columns(), (((1,), (1,)), ((), ())), precision=lax.Precision.HIGHEST, preferred_element_type=F32
    )


def shards(tokens, norm_gain, query_key_value_weight, out_weight, head_weight, coarse, grad_fine):
    tokens = tokens[0].reshape(ROWS, D)
    gain = norm_gain.reshape(1, D)
    full = gather_qkv(query_key_value_weight)
    grid = tokens.reshape(LAT, LON_DEV, D)
    left = shifted(grid[:, LON_DEV - MARGIN :].reshape(EDGE, D), 1)
    right = shifted(grid[:, :MARGIN].reshape(EDGE, D), -1)
    residual = residual_of(coarse[0])
    normed, rows = prepare(tokens, left, right, gain, grad_fine[0])
    core = lax.axis_index("c").reshape(1).astype(jnp.int32)
    out_full, head = gather_rest(core, out_weight, head_weight, (normed, residual))
    full, out_full, head, residual = lax.optimization_barrier((full, out_full, head, residual))
    projected, fine_grid, pieces = forward(normed, full, tokens, out_full, head, rows, residual)
    pieces = lax.all_to_all(pieces, ("c",) + TILE, 0, 0, tiled=True)
    grad_hidden, grad_attended = hidden_grad(rows, head, out_full)
    dq, dk, dv, to_left, to_right = attend_backward(projected, grad_attended)
    pieces, to_left, to_right = lax.optimization_barrier((pieces, to_left, to_right))
    summed = sum_pieces(pieces)
    grad_head = over_samples(summed)
    to_left, to_right = lax.optimization_barrier((to_left, to_right, summed))[:2]
    from_right = shifted(to_left, -1)
    from_left = shifted(to_right, 1)
    grad_tokens = norm_grad(dq, dk, dv, from_left, from_right, full, tokens, gain, grad_hidden)
    return (fine_grid[None], grad_tokens.reshape(1, LAT, LON_DEV, D), grad_head)


def solution(mesh):
    fine_mesh = Mesh(mesh.devices.reshape(2, ZS, CORES, YS, XS), ("dp", "z", "c", "y", "x"))
    samples = ("dp", "z", "c")
    placed = (
        P(samples, None, TILE, None),
        P(),
        P(FSDP, None),
        P(FSDP, None),
        P(FSDP, None),
        P(samples, None, None, TILE),
        P(samples, None, None, TILE),
    )
    return jax.shard_map(
        shards,
        mesh=fine_mesh,
        in_specs=placed,
        out_specs=(P(samples, None, None, TILE), P(samples, None, TILE, None), P(FSDP, None)),
        check_vma=False,
    )
```

```python
import functools
import jax
import jax.numpy as jnp
from jax import lax
from jax.experimental import pallas as pl
from jax.experimental.pallas import tpu as pltpu
from jax.sharding import Mesh
from jax.sharding import PartitionSpec as P

D = 1536
HEADS = 8
HEAD_DIM = 96
VARS = 20
MARGIN = 8
LAT = 8
LON_DEV = 32
INNER = 768
HEAD_OUT = 320
ROWS = 256
EDGE = 64
KEYS = ROWS + 2 * EDGE
GROUP = 384
PAIR = 2 * INNER
ZS = 8
CORES = 2
YS = 4
XS = 4
TILES = 16
FSDP = ("z", "c")
TILE = ("y", "x")
HALF_QKV = 1152
HALF_OUT = 768
PIECE = 64
UNPACK = 4
WIDE = ZS * 80
PHASES = 4
CHANNELS = 80
LANES = 128
PADDED = PHASES * LANES
EPSILON = 1e-05
SCALE = HEAD_DIM ** (-0.5)
LOG2_E = 1.4426950408889634
F32 = jnp.float32
BF16 = jnp.bfloat16
WHOLE = pl.BlockSpec(memory_space=pltpu.VMEM)


def dot(left, right):
    return lax.dot_general(left, right, (((1,), (0,)), ((), ())), preferred_element_type=F32)


def dot_last(left, right):
    return lax.dot_general(left, right, (((1,), (1,)), ((), ())), preferred_element_type=F32)


def dot_first(left, right):
    return lax.dot_general(left, right, (((0,), (0,)), ((), ())), preferred_element_type=F32)


def spread_matrix():
    row = lax.broadcasted_iota(jnp.int32, (LANES, LANES), 0)
    lane = lax.broadcasted_iota(jnp.int32, (LANES, LANES), 1)
    target = (row % LON_DEV) * PHASES + row // LON_DEV
    return jnp.where(lane == target, 1.0, 0.0).astype(BF16)


def standardized(values):
    average = jnp.mean(values, axis=-1, keepdims=True)
    centred = values - average
    variance = jnp.mean(centred * centred, axis=-1, keepdims=True)
    inverse_dev = lax.rsqrt(variance + EPSILON)
    return centred * inverse_dev, inverse_dev


def prepare_kernel(tokens_ref, left_ref, right_ref, gain_ref, fine_ref, normed_ref, rows_ref):
    for source, first in ((tokens_ref, 0), (left_ref, ROWS), (right_ref, ROWS + EDGE)):
        standard, _ = standardized(source[...].astype(F32))
        normed_ref[first : first + source.shape[0]] = (standard * gain_ref[...]).astype(BF16)
    select = spread_matrix()
    empty = jnp.zeros((LANES - CHANNELS, LANES), BF16)
    for lat in range(LAT):
        block = fine_ref[:, PHASES * lat : PHASES * (lat + 1), :].reshape(CHANNELS, LANES)
        block = jnp.concatenate([block.astype(BF16), empty], axis=0)
        picked = dot_last(select, block).astype(BF16)
        for phase in range(PHASES):
            rows_ref[lat * LON_DEV : (lat + 1) * LON_DEV, phase * LANES : (phase + 1) * LANES] = picked[
                phase * LON_DEV : (phase + 1) * LON_DEV
            ]


def prepare(tokens, left, right, gain, grad_fine):
    return pl.pallas_call(
        prepare_kernel,
        out_shape=(
            jax.ShapeDtypeStruct((KEYS, D), BF16),
            jax.ShapeDtypeStruct((ROWS, PADDED), BF16),
        ),
        in_specs=[WHOLE] * 5,
        out_specs=(WHOLE, WHOLE),
        name="prepare",
    )(tokens, left, right, gain, grad_fine)


def unpack_kernel(core_ref, own_ref, other_ref, out_ref, head_ref):
    core = core_ref[0]
    for source, place in ((own_ref, core), (other_ref, 1 - core)):
        for tile in range(60):
            for z in range(UNPACK):
                block = source[tile // 4, z, tile % 4 * 16 : (tile % 4 + 1) * 16, :]
                if tile < 36:
                    top = pl.multiple_of(z * 96 + place * 48 + tile % 3 * 16, 16)
                    out_ref[pl.ds(top, 16), tile // 3 * LANES : (tile // 3 + 1) * LANES] = block
                else:
                    top = pl.multiple_of(z * 192 + place * 96 + tile % 6 * 16, 16)
                    phase = (tile - 36) // 6
                    head_ref[pl.ds(top, 16), phase * LANES : (phase + 1) * LANES] = block


def unpack(core, own, other):
    block = pl.BlockSpec((TILES, UNPACK, PIECE, LANES), lambda z: (0, z, 0, 0))
    return pl.pallas_call(
        unpack_kernel,
        out_shape=(
            jax.ShapeDtypeStruct((INNER, D), BF16),
            jax.ShapeDtypeStruct((D, PADDED), BF16),
        ),
        grid=(ZS // UNPACK,),
        in_specs=[pl.BlockSpec(memory_space=pltpu.SMEM), block, block],
        out_specs=(
            pl.BlockSpec((UNPACK * 96, D), lambda z: (z, 0)),
            pl.BlockSpec((UNPACK * 192, PADDED), lambda z: (z, 0)),
        ),
        name="unpack",
    )(core, own, other)


def hidden_grad_kernel(rows_ref, head_ref, out_ref, hidden_ref, attended_ref):
    grad_hidden = dot_last(rows_ref[...], head_ref[...])
    hidden_ref[...] = grad_hidden
    attended_ref[...] = dot_last(grad_hidden.astype(BF16), out_ref[...]).astype(BF16)


def hidden_grad(rows, head, out_weight):
    return pl.pallas_call(
        hidden_grad_kernel,
        out_shape=(
            jax.ShapeDtypeStruct((ROWS, D), F32),
            jax.ShapeDtypeStruct((ROWS, INNER), BF16),
        ),
        in_specs=[WHOLE, WHOLE, WHOLE],
        out_specs=(WHOLE, WHOLE),
        name="hidden_grad",
    )(rows, head, out_weight)


def whole_block(shape):
    return pl.BlockSpec(shape, lambda n: (0,) * len(shape))


def head_window(head):
    first = head * HEAD_DIM // LANES * LANES
    last = -(-(head + 1) * HEAD_DIM // LANES) * LANES
    lane = lax.broadcasted_iota(jnp.int32, (1, last - first), 1) + first
    inside = (lane >= head * HEAD_DIM) & (lane < (head + 1) * HEAD_DIM)
    return first, last, inside


def masked(values, inside):
    return jnp.where(inside, values, jnp.zeros_like(values))


def softmax_of(query, key):
    scores = dot_last(query, key)
    biggest = jnp.max(scores, axis=-1, keepdims=True)
    exponent = jnp.exp2((scores - biggest) * (SCALE * LOG2_E))
    return exponent * (1.0 / jnp.sum(exponent, axis=-1, keepdims=True))


def forward_group(queries, keys, values):
    parts = [None, None, None]
    for head in range(4):
        first, last, inside = head_window(head)
        softmax = softmax_of(masked(queries[:, first:last], inside), keys[:, first:last])
        result = dot(softmax.astype(BF16), masked(values[:, first:last], inside))
        for tile in range(first // LANES, last // LANES):
            piece = result[:, tile * LANES - first : (tile + 1) * LANES - first]
            parts[tile] = piece if parts[tile] is None else parts[tile] + piece
    return jnp.concatenate([part.astype(BF16) for part in parts], axis=1)


def column_block(step):
    return step % 3 * 2 + step // 3


def forward_kernel(
    normed_ref, weight_ref,
    tokens_hbm, out_hbm, head_hbm, rows_hbm, residual_hbm,
    projected_out, fine_ref, pieces_hbm,
    projected_ref, attended_ref, pieces_ref, tokens_ref, out_ref, head_ref, rows_ref, residual_ref, products, sems,
):
    step = pl.program_id(0)
    place = column_block(step)
    copies = [
        pltpu.make_async_copy(source, target, sems.at[number])
        for number, (source, target) in enumerate(
            (
                (tokens_hbm, tokens_ref),
                (out_hbm, out_ref),
                (head_hbm, head_ref),
                (rows_hbm, rows_ref),
                (residual_hbm, residual_ref),
            )
        )
    ]

    @pl.when(step == 4)
    def _():
        for copy in copies:
            copy.start()

    @pl.when(place < 2)
    def _():
        queries = dot(normed_ref[:ROWS], weight_ref[0]).astype(BF16)
        projected_ref[place, :ROWS] = queries
        projected_out[0, :ROWS] = queries
        projected_out[0, ROWS:] = jnp.zeros((2 * EDGE, GROUP), BF16)

    @pl.when(place >= 2)
    def _():
        pairs = dot(normed_ref[...], weight_ref[0]).astype(BF16)
        projected_ref[place] = pairs
        projected_out[0] = pairs

    @pl.when(step == 3)
    def _():
        attended_ref[...] = forward_group(projected_ref[0, :ROWS], projected_ref[2], projected_ref[4])

    @pl.when(step == 5)
    def _():
        attended = forward_group(projected_ref[1, :ROWS], projected_ref[3], projected_ref[5])
        for copy in copies:
            copy.wait()
        mixed = dot(attended_ref[...], out_ref[:GROUP]) + dot(attended, out_ref[GROUP:])
        hidden = (tokens_ref[...].astype(F32) + mixed).astype(BF16)
        products[...] = dot_first(hidden, rows_ref[...])
        for core in range(CORES):
            for quad in range(4):
                for phase in range(PHASES):
                    row = [
                        products[
                            (z * CORES + core) * 96 + quad * 24 : (z * CORES + core) * 96 + quad * 24 + 24,
                            phase * LANES : phase * LANES + CHANNELS,
                        ]
                        for z in range(ZS)
                    ]
                    pieces_ref[core * TILES + quad * 4 + phase] = jnp.concatenate(row, axis=1).astype(BF16)
        send = pltpu.make_async_copy(pieces_ref, pieces_hbm, sems.at[5])
        send.start()
        head_out = dot(hidden, head_ref[...])
        select = spread_matrix()
        for lat in range(LAT):
            at = slice(lat * LON_DEV, (lat + 1) * LON_DEV)
            stacked = jnp.concatenate(
                [head_out[at, phase * LANES : (phase + 1) * LANES] for phase in range(PHASES)], axis=0
            )
            high = stacked.astype(BF16)
            low = (stacked - high.astype(F32)).astype(BF16)
            spread = dot_first(high, select) + dot_first(low, select)
            across = slice(PHASES * lat, PHASES * (lat + 1))
            fine_ref[:, across, :] = spread[:CHANNELS].reshape(VARS, PHASES, LANES) + residual_ref[:, across, :]
        send.wait()


def forward(normed, full, tokens, out_weight, head, rows, residual):
    fine = (VARS, 4 * LAT, LANES)
    pieces = (CORES * TILES, 24, WIDE)
    projected = (6, KEYS, GROUP)
    return pl.pallas_call(
        forward_kernel,
        out_shape=(
            jax.ShapeDtypeStruct(projected, BF16),
            jax.ShapeDtypeStruct(fine, F32),
            jax.ShapeDtypeStruct(pieces, BF16),
        ),
        grid=(6,),
        in_specs=[
            whole_block((KEYS, D)),
            pl.BlockSpec((1, D, GROUP), lambda n: (column_block(n) // 3, 0, column_block(n) % 3)),
        ]
        + [pl.BlockSpec(memory_space=pl.ANY)] * 5,
        out_specs=(
            pl.BlockSpec((1, KEYS, GROUP), lambda n: (column_block(n), 0, 0)),
            whole_block(fine),
            pl.BlockSpec(memory_space=pl.ANY),
        ),
        scratch_shapes=[
            pltpu.VMEM(projected, BF16),
            pltpu.VMEM((ROWS, GROUP), BF16),
            pltpu.VMEM(pieces, BF16),
            pltpu.VMEM((ROWS, D), BF16),
            pltpu.VMEM((INNER, D), BF16),
            pltpu.VMEM((D, PADDED), BF16),
            pltpu.VMEM((ROWS, PADDED), BF16),
            pltpu.VMEM(fine, F32),
            pltpu.VMEM((D, PADDED), F32),
            pltpu.SemaphoreType.DMA((6,)),
        ],
        name="forward",
    )(normed, full, tokens, out_weight, head, rows, residual)


def backward_kernel(
    q_ref, k_ref, v_ref, grad_ref,
    dq_ref, dk_ref, dv_ref, left_ref, right_ref,
):
    queries = q_ref[0, :ROWS]
    grads = grad_ref[...]
    keys = k_ref[0]
    values = v_ref[0]
    sums = [[None, None, None] for _ in range(3)]
    for head in range(4):
        first, last, inside = head_window(head)
        query = masked(queries[:, first:last], inside)
        grad = masked(grads[:, first:last], inside)
        softmax = softmax_of(query, keys[:, first:last])
        grad_weights = dot_last(grad, values[:, first:last])
        weighted = jnp.sum(softmax * grad_weights, axis=-1, keepdims=True)
        grad_scores = (softmax * (grad_weights - weighted)).astype(BF16)
        results = (
            dot(grad_scores, masked(keys[:, first:last], inside)),
            dot_first(grad_scores, query),
            dot_first(softmax.astype(BF16), grad),
        )
        for kept, result in zip(sums, results):
            for tile in range(first // LANES, last // LANES):
                piece = result[:, tile * LANES - first : (tile + 1) * LANES - first]
                kept[tile] = piece if kept[tile] is None else kept[tile] + piece
    for tile in range(3):
        at = slice(tile * LANES, (tile + 1) * LANES)
        dq_ref[:, at] = (sums[0][tile] * SCALE).astype(BF16)
        grad_keys = sums[1][tile] * SCALE
        grad_values = sums[2][tile]
        for kind, (grads_of, own) in enumerate(((grad_keys, dk_ref), (grad_values, dv_ref))):
            own[:, at] = grads_of[:ROWS]
            left_ref[kind, :, at] = grads_of[ROWS : ROWS + EDGE].astype(BF16)
            right_ref[kind, :, at] = grads_of[ROWS + EDGE :].astype(BF16)


def attend_backward(projected, grad_attended):
    def block(rows):
        return pl.BlockSpec((rows, GROUP), lambda n: (0, n))

    def shape(rows, kind):
        return jax.ShapeDtypeStruct((rows, INNER), kind)

    edge = jax.ShapeDtypeStruct((2, EDGE, INNER), BF16)
    edge_block = pl.BlockSpec((2, EDGE, GROUP), lambda n: (0, 0, n))
    return pl.pallas_call(
        backward_kernel,
        out_shape=(shape(ROWS, BF16), shape(ROWS, F32), shape(ROWS, F32), edge, edge),
        grid=(2,),
        in_specs=[pl.BlockSpec((1, KEYS, GROUP), lambda n, first=first: (first + n, 0, 0)) for first in (0, 2, 4)]
        + [block(ROWS)],
        out_specs=(block(ROWS), block(ROWS), block(ROWS), edge_block, edge_block),
        name="attend_backward",
    )(projected, projected, projected, grad_attended)


def norm_grad_kernel(
    dq_ref, dk_ref, dv_ref, left_ref, right_ref, low_ref, up_ref, gain_ref, tokens_hbm, hidden_hbm,
    out_ref, grads, total, tokens_ref, hidden_ref, sems,
):
    step = pl.program_id(0)
    copies = (
        pltpu.make_async_copy(tokens_hbm, tokens_ref, sems.at[0]),
        pltpu.make_async_copy(hidden_hbm, hidden_ref, sems.at[1]),
    )

    @pl.when(step == 0)
    def _():
        for copy in copies:
            copy.start()
        grads[:, :INNER] = dq_ref[...]
        for kind, own_ref in enumerate((dk_ref, dv_ref)):
            own = own_ref[...].reshape(LAT, LON_DEV, INNER)
            left = left_ref[kind].astype(F32).reshape(LAT, MARGIN, INNER)
            right = right_ref[kind].astype(F32).reshape(LAT, MARGIN, INNER)
            own = jnp.concatenate(
                [own[:, :MARGIN] + left, own[:, MARGIN : LON_DEV - MARGIN], own[:, LON_DEV - MARGIN :] + right],
                axis=1,
            )
            grads[:, (kind + 1) * INNER : (kind + 2) * INNER] = own.reshape(ROWS, INNER).astype(BF16)

    at = pl.ds(pl.multiple_of(step * 256, 256), 256)
    total[:, at] = dot_last(grads[:, :HALF_QKV], low_ref[0]) + dot_last(grads[:, HALF_QKV:], up_ref[0])

    @pl.when(step == 5)
    def _():
        for copy in copies:
            copy.wait()
        values = tokens_ref[...].astype(F32)
        standard, inverse_dev = standardized(values)
        grad_standard = total[...] * gain_ref[...]
        first_mean = jnp.mean(grad_standard, axis=-1, keepdims=True)
        second_mean = jnp.mean(grad_standard * standard, axis=-1, keepdims=True)
        grad = inverse_dev * (grad_standard - first_mean - standard * second_mean)
        out_ref[...] = (hidden_ref[...] + grad).astype(BF16)


def norm_grad(dq, dk, dv, from_left, from_right, full, tokens, gain, grad_hidden):
    return pl.pallas_call(
        norm_grad_kernel,
        out_shape=jax.ShapeDtypeStruct((ROWS, D), BF16),
        grid=(6,),
        in_specs=[
            whole_block((ROWS, INNER)),
            whole_block((ROWS, INNER)),
            whole_block((ROWS, INNER)),
            whole_block((2, EDGE, INNER)),
            whole_block((2, EDGE, INNER)),
            pl.BlockSpec((1, 256, HALF_QKV), lambda n: (0, n, 0)),
            pl.BlockSpec((1, 256, HALF_QKV), lambda n: (1, n, 0)),
            whole_block((1, D)),
            pl.BlockSpec(memory_space=pl.ANY),
            pl.BlockSpec(memory_space=pl.ANY),
        ],
        out_specs=whole_block((ROWS, D)),
        scratch_shapes=[
            pltpu.VMEM((ROWS, 3 * INNER), BF16),
            pltpu.VMEM((ROWS, D), F32),
            pltpu.VMEM((ROWS, D), BF16),
            pltpu.VMEM((ROWS, D), F32),
            pltpu.SemaphoreType.DMA((2,)),
        ],
        name="norm_grad",
    )(dq, dk, dv, from_left, from_right, full, full, gain, tokens, grad_hidden)


def sum_kernel(pieces_ref, out_ref):
    total = pieces_ref[0].astype(F32)
    for place in range(1, CORES * TILES):
        total = total + pieces_ref[place].astype(F32)
    empty = jnp.zeros((24, LANES - CHANNELS), F32)
    for z in range(ZS):
        part = jnp.concatenate([total[:, z * CHANNELS : (z + 1) * CHANNELS], empty], axis=1).astype(BF16)
        out_ref[z] = part
        out_ref[ZS + z] = part


def sum_pieces(pieces):
    return pl.pallas_call(
        sum_kernel,
        out_shape=jax.ShapeDtypeStruct((2 * ZS, 24, LANES), BF16),
        in_specs=[WHOLE],
        out_specs=WHOLE,
        name="sum_pieces",
    )(pieces)


def interp_weights(fine_index):
    coarse_cell = fine_index // 4
    phase_index = fine_index % 4
    lower_shift = (phase_index < 2).astype(jnp.int32)
    upper_weight = (2 * phase_index - 3 + 8 * lower_shift).astype(F32) / 8.0
    return (coarse_cell - lower_shift, upper_weight)


def build_matrix(lower_cell, upper_cell, upper_weight, count):
    columns = jnp.arange(count, dtype=jnp.int32)
    lower_part = jnp.where(columns[None, :] == lower_cell[:, None], 1.0 - upper_weight[:, None], 0.0)
    upper_portion = jnp.where(columns[None, :] == upper_cell[:, None], upper_weight[:, None], 0.0)
    return lower_part + upper_portion


def shifted(value, steps):
    return lax.ppermute(value, TILE, [(i, (i + steps) % TILES) for i in range(TILES)])


def residual_of(coarse):
    before = shifted(coarse[:, :, -1:], 1)
    after = shifted(coarse[:, :, :1], -1)
    padded = jnp.concatenate([before, coarse, after], axis=2)
    lat_lower, lat_upper_weight = interp_weights(jnp.arange(4 * LAT, dtype=jnp.int32))
    latitude_matrix = build_matrix(
        jnp.clip(lat_lower, 0, LAT - 1), jnp.clip(lat_lower + 1, 0, LAT - 1), lat_upper_weight, LAT
    )
    lon_lower, lon_upper_weight = interp_weights(jnp.arange(4 * LON_DEV, dtype=jnp.int32))
    lon_matrix = build_matrix(lon_lower + 1, lon_lower + 2, lon_upper_weight, LON_DEV + 2)
    incomplete_grid = jnp.einsum("lj,kji->kli", latitude_matrix, padded, precision=lax.Precision.HIGHEST)
    return jnp.einsum("vrb,cb->vrc", incomplete_grid, lon_matrix, precision=lax.Precision.HIGHEST)


def head_columns():
    target = jnp.arange(PADDED, dtype=jnp.int32)
    phase, channel = target // LANES, target % LANES
    source = jnp.where(channel < CHANNELS, channel * PHASES + phase, -1)
    return (jnp.arange(HEAD_OUT, dtype=jnp.int32)[:, None] == source[None, :]).astype(F32)


def gather_qkv(qkv):
    half = lax.axis_index("dp")
    qkv_half = lax.dynamic_slice_in_dim(qkv, half * HALF_QKV, HALF_QKV, 1)
    full = lax.all_gather(qkv_half, ("dp",) + FSDP, axis=0, tiled=True)
    return full.reshape(2, D, HALF_QKV)


def to_all(value, axes, count):
    copies = jnp.broadcast_to(value[None], (count,) + value.shape)
    return lax.all_to_all(copies, axes, 0, 0, tiled=True)


def gather_rest(core, out_w, head_w, ready):
    out_rows = out_w.reshape(48, 12, LANES).transpose(1, 0, 2).reshape(576, LANES)
    head_pad = dot(head_w, head_columns().astype(BF16)).astype(BF16)
    head_rows = head_pad.reshape(96, PHASES, LANES).transpose(1, 0, 2).reshape(384, LANES)
    rows = jnp.concatenate([out_rows, head_rows, jnp.zeros((PIECE, LANES), BF16)], axis=0)
    own = lax.dynamic_slice_in_dim(rows, lax.axis_index(TILE) * PIECE, PIECE, 0)
    over_z = to_all(own, ("z",), ZS)
    over_tile = to_all(over_z, TILE, TILES)
    over_tile = lax.optimization_barrier((over_tile, ready))[0]
    other = lax.ppermute(over_tile, "c", [(0, 1), (1, 0)])
    return unpack(core, over_tile, other)


def over_samples(summed):
    both = lax.all_to_all(summed, ("dp", "z"), 0, 0, tiled=True)
    spread = to_all(jnp.sum(both.astype(F32), axis=0), TILE, TILES)
    padded = spread.reshape(4, PHASES, 24, LANES).transpose(0, 2, 1, 3).reshape(96, PADDED)
    return lax.dot_general(
        padded, head_columns(), (((1,), (1,)), ((), ())), precision=lax.Precision.HIGHEST, preferred_element_type=F32
    )


def shards(tokens, norm_gain, query_key_value_weight, out_weight, head_weight, coarse, grad_fine):
    tokens = tokens[0].reshape(ROWS, D)
    gain = norm_gain.reshape(1, D)
    full = gather_qkv(query_key_value_weight)
    grid = tokens.reshape(LAT, LON_DEV, D)
    left = shifted(grid[:, LON_DEV - MARGIN :].reshape(EDGE, D), 1)
    right = shifted(grid[:, :MARGIN].reshape(EDGE, D), -1)
    residual = residual_of(coarse[0])
    normed, rows = prepare(tokens, left, right, gain, grad_fine[0])
    core = lax.axis_index("c").reshape(1).astype(jnp.int32)
    out_full, head = gather_rest(core, out_weight, head_weight, (normed, residual))
    full, out_full, head, residual = lax.optimization_barrier((full, out_full, head, residual))
    projected, fine_grid, pieces = forward(normed, full, tokens, out_full, head, rows, residual)
    pieces = lax.all_to_all(pieces, ("c",) + TILE, 0, 0, tiled=True)
    grad_hidden, grad_attended = hidden_grad(rows, head, out_full)
    dq, dk, dv, to_left, to_right = attend_backward(projected, grad_attended)
    pieces, to_left, to_right = lax.optimization_barrier((pieces, to_left, to_right))
    summed = sum_pieces(pieces)
    grad_head = over_samples(summed)
    to_left, to_right = lax.optimization_barrier((to_left, to_right, summed))[:2]
    from_right = shifted(to_left, -1)
    from_left = shifted(to_right, 1)
    grad_tokens = norm_grad(dq, dk, dv, from_left, from_right, full, tokens, gain, grad_hidden)
    return (fine_grid[None], grad_tokens.reshape(1, LAT, LON_DEV, D), grad_head)


def solution(mesh):
    fine_mesh = Mesh(mesh.devices.reshape(2, ZS, CORES, YS, XS), ("dp", "z", "c", "y", "x"))
    samples = ("dp", "z", "c")
    placed = (
        P(samples, None, TILE, None),
        P(),
        P(FSDP, None),
        P(FSDP, None),
        P(FSDP, None),
        P(samples, None, None, TILE),
        P(samples, None, None, TILE),
    )
    return jax.shard_map(
        shards,
        mesh=fine_mesh,
        in_specs=placed,
        out_specs=(P(samples, None, None, TILE), P(samples, None, TILE, None), P(FSDP, None)),
        check_vma=False,
    )
```

```python
import functools
import jax
import jax.numpy as jnp
from jax import lax
from jax.experimental import pallas as pl
from jax.experimental.pallas import tpu as pltpu
from jax.sharding import Mesh
from jax.sharding import PartitionSpec as P

D = 1536
HEADS = 8
HEAD_DIM = 96
VARS = 20
MARGIN = 8
LAT = 8
LON_DEV = 32
INNER = 768
HEAD_OUT = 320
ROWS = 256
EDGE = 64
KEYS = ROWS + 2 * EDGE
GROUP = 384
PAIR = 2 * INNER
ZS = 8
CORES = 2
YS = 4
XS = 4
TILES = 16
FSDP = ("z", "c")
TILE = ("y", "x")
HALF_QKV = 1152
HALF_OUT = 768
PIECE = 64
UNPACK = 4
WIDE = ZS * 80
PHASES = 4
CHANNELS = 80
LANES = 128
PADDED = PHASES * LANES
EPSILON = 1e-05
SCALE = HEAD_DIM ** (-0.5)
LOG2_E = 1.4426950408889634
F32 = jnp.float32
BF16 = jnp.bfloat16
WHOLE = pl.BlockSpec(memory_space=pltpu.VMEM)


def dot(left, right):
    return lax.dot_general(left, right, (((1,), (0,)), ((), ())), preferred_element_type=F32)


def dot_last(left, right):
    return lax.dot_general(left, right, (((1,), (1,)), ((), ())), preferred_element_type=F32)


def dot_first(left, right):
    return lax.dot_general(left, right, (((0,), (0,)), ((), ())), preferred_element_type=F32)


def spread_matrix():
    row = lax.broadcasted_iota(jnp.int32, (LANES, LANES), 0)
    lane = lax.broadcasted_iota(jnp.int32, (LANES, LANES), 1)
    target = (row % LON_DEV) * PHASES + row // LON_DEV
    return jnp.where(lane == target, 1.0, 0.0).astype(BF16)


def standardized(values):
    average = jnp.mean(values, axis=-1, keepdims=True)
    centred = values - average
    variance = jnp.mean(centred * centred, axis=-1, keepdims=True)
    inverse_dev = lax.rsqrt(variance + EPSILON)
    return centred * inverse_dev, inverse_dev


def prepare_kernel(tokens_ref, left_ref, right_ref, gain_ref, fine_ref, normed_ref, rows_ref):
    for source, first in ((tokens_ref, 0), (left_ref, ROWS), (right_ref, ROWS + EDGE)):
        standard, _ = standardized(source[...].astype(F32))
        normed_ref[first : first + source.shape[0]] = (standard * gain_ref[...]).astype(BF16)
    select = spread_matrix()
    empty = jnp.zeros((LANES - CHANNELS, LANES), BF16)
    for lat in range(LAT):
        block = fine_ref[:, PHASES * lat : PHASES * (lat + 1), :].reshape(CHANNELS, LANES)
        block = jnp.concatenate([block.astype(BF16), empty], axis=0)
        picked = dot_last(select, block).astype(BF16)
        for phase in range(PHASES):
            rows_ref[lat * LON_DEV : (lat + 1) * LON_DEV, phase * LANES : (phase + 1) * LANES] = picked[
                phase * LON_DEV : (phase + 1) * LON_DEV
            ]


def prepare(tokens, left, right, gain, grad_fine):
    return pl.pallas_call(
        prepare_kernel,
        out_shape=(
            jax.ShapeDtypeStruct((KEYS, D), BF16),
            jax.ShapeDtypeStruct((ROWS, PADDED), BF16),
        ),
        in_specs=[WHOLE] * 5,
        out_specs=(WHOLE, WHOLE),
        name="prepare",
    )(tokens, left, right, gain, grad_fine)


def unpack_kernel(core_ref, own_ref, other_ref, out_ref, head_ref):
    core = core_ref[0]
    for source, place in ((own_ref, core), (other_ref, 1 - core)):
        for tile in range(60):
            for z in range(UNPACK):
                block = source[tile // 4, z, tile % 4 * 16 : (tile % 4 + 1) * 16, :]
                if tile < 36:
                    top = pl.multiple_of(z * 96 + place * 48 + tile % 3 * 16, 16)
                    out_ref[pl.ds(top, 16), tile // 3 * LANES : (tile // 3 + 1) * LANES] = block
                else:
                    top = pl.multiple_of(z * 192 + place * 96 + tile % 6 * 16, 16)
                    phase = (tile - 36) // 6
                    head_ref[pl.ds(top, 16), phase * LANES : (phase + 1) * LANES] = block


def unpack(core, own, other):
    block = pl.BlockSpec((TILES, UNPACK, PIECE, LANES), lambda z: (0, z, 0, 0))
    return pl.pallas_call(
        unpack_kernel,
        out_shape=(
            jax.ShapeDtypeStruct((INNER, D), BF16),
            jax.ShapeDtypeStruct((D, PADDED), BF16),
        ),
        grid=(ZS // UNPACK,),
        in_specs=[pl.BlockSpec(memory_space=pltpu.SMEM), block, block],
        out_specs=(
            pl.BlockSpec((UNPACK * 96, D), lambda z: (z, 0)),
            pl.BlockSpec((UNPACK * 192, PADDED), lambda z: (z, 0)),
        ),
        name="unpack",
    )(core, own, other)


def hidden_grad_kernel(rows_ref, head_ref, out_ref, hidden_ref, attended_ref):
    grad_hidden = dot_last(rows_ref[...], head_ref[...])
    hidden_ref[...] = grad_hidden
    attended_ref[...] = dot_last(grad_hidden.astype(BF16), out_ref[...]).astype(BF16)


def hidden_grad(rows, head, out_weight):
    return pl.pallas_call(
        hidden_grad_kernel,
        out_shape=(
            jax.ShapeDtypeStruct((ROWS, D), F32),
            jax.ShapeDtypeStruct((ROWS, INNER), BF16),
        ),
        in_specs=[WHOLE, WHOLE, WHOLE],
        out_specs=(WHOLE, WHOLE),
        name="hidden_grad",
    )(rows, head, out_weight)


def whole_block(shape):
    return pl.BlockSpec(shape, lambda n: (0,) * len(shape))


def head_window(head):
    first = head * HEAD_DIM // LANES * LANES
    last = -(-(head + 1) * HEAD_DIM // LANES) * LANES
    lane = lax.broadcasted_iota(jnp.int32, (1, last - first), 1) + first
    inside = (lane >= head * HEAD_DIM) & (lane < (head + 1) * HEAD_DIM)
    return first, last, inside


def masked(values, inside):
    return jnp.where(inside, values, jnp.zeros_like(values))


def softmax_of(query, key):
    scores = dot_last(query, key)
    biggest = jnp.max(scores, axis=-1, keepdims=True)
    exponent = jnp.exp2((scores - biggest) * (SCALE * LOG2_E))
    return exponent * (1.0 / jnp.sum(exponent, axis=-1, keepdims=True))


def forward_group(queries, keys, values):
    parts = [None, None, None]
    for head in range(4):
        first, last, inside = head_window(head)
        softmax = softmax_of(masked(queries[:, first:last], inside), keys[:, first:last])
        result = dot(softmax.astype(BF16), masked(values[:, first:last], inside))
        for tile in range(first // LANES, last // LANES):
            piece = result[:, tile * LANES - first : (tile + 1) * LANES - first]
            parts[tile] = piece if parts[tile] is None else parts[tile] + piece
    return jnp.concatenate([part.astype(BF16) for part in parts], axis=1)


def column_block(step):
    return step % 3 * 2 + step // 3


def forward_kernel(
    normed_ref, weight_ref,
    tokens_hbm, out_hbm, head_hbm, rows_hbm, residual_hbm,
    projected_out, fine_ref, pieces_hbm,
    projected_ref, attended_ref, pieces_ref, tokens_ref, out_ref, head_ref, rows_ref, residual_ref, products, sems,
):
    step = pl.program_id(0)
    place = column_block(step)
    copies = [
        pltpu.make_async_copy(source, target, sems.at[number])
        for number, (source, target) in enumerate(
            (
                (tokens_hbm, tokens_ref),
                (out_hbm, out_ref),
                (head_hbm, head_ref),
                (rows_hbm, rows_ref),
                (residual_hbm, residual_ref),
            )
        )
    ]

    @pl.when(step == 4)
    def _():
        for copy in copies:
            copy.start()

    @pl.when(place < 2)
    def _():
        queries = dot(normed_ref[:ROWS], weight_ref[0]).astype(BF16)
        projected_ref[place, :ROWS] = queries
        projected_out[0, :ROWS] = queries
        projected_out[0, ROWS:] = jnp.zeros((2 * EDGE, GROUP), BF16)

    @pl.when(place >= 2)
    def _():
        pairs = dot(normed_ref[...], weight_ref[0]).astype(BF16)
        projected_ref[place] = pairs
        projected_out[0] = pairs

    @pl.when(step == 3)
    def _():
        attended_ref[...] = forward_group(projected_ref[0, :ROWS], projected_ref[2], projected_ref[4])

    @pl.when(step == 5)
    def _():
        attended = forward_group(projected_ref[1, :ROWS], projected_ref[3], projected_ref[5])
        for copy in copies:
            copy.wait()
        mixed = dot(attended_ref[...], out_ref[:GROUP]) + dot(attended, out_ref[GROUP:])
        hidden = (tokens_ref[...].astype(F32) + mixed).astype(BF16)
        products[...] = dot_first(hidden, rows_ref[...])
        for core in range(CORES):
            for quad in range(4):
                for phase in range(PHASES):
                    row = [
                        products[
                            (z * CORES + core) * 96 + quad * 24 : (z * CORES + core) * 96 + quad * 24 + 24,
                            phase * LANES : phase * LANES + CHANNELS,
                        ]
                        for z in range(ZS)
                    ]
                    pieces_ref[core * TILES + quad * 4 + phase] = jnp.concatenate(row, axis=1).astype(BF16)
        send = pltpu.make_async_copy(pieces_ref, pieces_hbm, sems.at[5])
        send.start()
        head_out = dot(hidden, head_ref[...])
        select = spread_matrix()
        for lat in range(LAT):
            at = slice(lat * LON_DEV, (lat + 1) * LON_DEV)
            stacked = jnp.concatenate(
                [head_out[at, phase * LANES : (phase + 1) * LANES] for phase in range(PHASES)], axis=0
            )
            high = stacked.astype(BF16)
            low = (stacked - high.astype(F32)).astype(BF16)
            spread = dot_first(high, select) + dot_first(low, select)
            across = slice(PHASES * lat, PHASES * (lat + 1))
            fine_ref[:, across, :] = spread[:CHANNELS].reshape(VARS, PHASES, LANES) + residual_ref[:, across, :]
        send.wait()


def forward(normed, full, tokens, out_weight, head, rows, residual):
    fine = (VARS, 4 * LAT, LANES)
    pieces = (CORES * TILES, 24, WIDE)
    projected = (6, KEYS, GROUP)
    return pl.pallas_call(
        forward_kernel,
        out_shape=(
            jax.ShapeDtypeStruct(projected, BF16),
            jax.ShapeDtypeStruct(fine, F32),
            jax.ShapeDtypeStruct(pieces, BF16),
        ),
        grid=(6,),
        in_specs=[
            whole_block((KEYS, D)),
            pl.BlockSpec((1, D, GROUP), lambda n: (column_block(n) // 3, 0, column_block(n) % 3)),
        ]
        + [pl.BlockSpec(memory_space=pl.ANY)] * 5,
        out_specs=(
            pl.BlockSpec((1, KEYS, GROUP), lambda n: (column_block(n), 0, 0)),
            whole_block(fine),
            pl.BlockSpec(memory_space=pl.ANY),
        ),
        scratch_shapes=[
            pltpu.VMEM(projected, BF16),
            pltpu.VMEM((ROWS, GROUP), BF16),
            pltpu.VMEM(pieces, BF16),
            pltpu.VMEM((ROWS, D), BF16),
            pltpu.VMEM((INNER, D), BF16),
            pltpu.VMEM((D, PADDED), BF16),
            pltpu.VMEM((ROWS, PADDED), BF16),
            pltpu.VMEM(fine, F32),
            pltpu.VMEM((D, PADDED), F32),
            pltpu.SemaphoreType.DMA((6,)),
        ],
        name="forward",
    )(normed, full, tokens, out_weight, head, rows, residual)


def backward_kernel(
    q_ref, k_ref, v_ref, grad_ref,
    dq_ref, dk_ref, dv_ref, left_ref, right_ref,
):
    queries = q_ref[0, :ROWS]
    grads = grad_ref[...]
    keys = k_ref[0]
    values = v_ref[0]
    sums = [[None, None, None] for _ in range(3)]
    for head in range(4):
        first, last, inside = head_window(head)
        query = masked(queries[:, first:last], inside)
        grad = masked(grads[:, first:last], inside)
        softmax = softmax_of(query, keys[:, first:last])
        grad_weights = dot_last(grad, values[:, first:last])
        weighted = jnp.sum(softmax * grad_weights, axis=-1, keepdims=True)
        grad_scores = (softmax * (grad_weights - weighted)).astype(BF16)
        results = (
            dot(grad_scores, masked(keys[:, first:last], inside)),
            dot_first(grad_scores, query),
            dot_first(softmax.astype(BF16), grad),
        )
        for kept, result in zip(sums, results):
            for tile in range(first // LANES, last // LANES):
                piece = result[:, tile * LANES - first : (tile + 1) * LANES - first]
                kept[tile] = piece if kept[tile] is None else kept[tile] + piece
    for tile in range(3):
        at = slice(tile * LANES, (tile + 1) * LANES)
        dq_ref[:, at] = (sums[0][tile] * SCALE).astype(BF16)
        grad_keys = sums[1][tile] * SCALE
        grad_values = sums[2][tile]
        for kind, (grads_of, own) in enumerate(((grad_keys, dk_ref), (grad_values, dv_ref))):
            own[:, at] = grads_of[:ROWS]
            left_ref[kind, :, at] = grads_of[ROWS : ROWS + EDGE].astype(BF16)
            right_ref[kind, :, at] = grads_of[ROWS + EDGE :].astype(BF16)


def attend_backward(projected, grad_attended):
    def block(rows):
        return pl.BlockSpec((rows, GROUP), lambda n: (0, n))

    def shape(rows, kind):
        return jax.ShapeDtypeStruct((rows, INNER), kind)

    edge = jax.ShapeDtypeStruct((2, EDGE, INNER), BF16)
    edge_block = pl.BlockSpec((2, EDGE, GROUP), lambda n: (0, 0, n))
    return pl.pallas_call(
        backward_kernel,
        out_shape=(shape(ROWS, BF16), shape(ROWS, F32), shape(ROWS, F32), edge, edge),
        grid=(2,),
        in_specs=[pl.BlockSpec((1, KEYS, GROUP), lambda n, first=first: (first + n, 0, 0)) for first in (0, 2, 4)]
        + [block(ROWS)],
        out_specs=(block(ROWS), block(ROWS), block(ROWS), edge_block, edge_block),
        name="attend_backward",
    )(projected, projected, projected, grad_attended)


def norm_grad_kernel(
    dq_ref, dk_ref, dv_ref, left_ref, right_ref, low_ref, up_ref, gain_ref, tokens_hbm, hidden_hbm,
    out_ref, grads, total, tokens_ref, hidden_ref, sems,
):
    step = pl.program_id(0)
    copies = (
        pltpu.make_async_copy(tokens_hbm, tokens_ref, sems.at[0]),
        pltpu.make_async_copy(hidden_hbm, hidden_ref, sems.at[1]),
    )

    @pl.when(step == 0)
    def _():
        for copy in copies:
            copy.start()
        grads[:, :INNER] = dq_ref[...]
        for kind, own_ref in enumerate((dk_ref, dv_ref)):
            own = own_ref[...].reshape(LAT, LON_DEV, INNER)
            left = left_ref[kind].astype(F32).reshape(LAT, MARGIN, INNER)
            right = right_ref[kind].astype(F32).reshape(LAT, MARGIN, INNER)
            own = jnp.concatenate(
                [own[:, :MARGIN] + left, own[:, MARGIN : LON_DEV - MARGIN], own[:, LON_DEV - MARGIN :] + right],
                axis=1,
            )
            grads[:, (kind + 1) * INNER : (kind + 2) * INNER] = own.reshape(ROWS, INNER).astype(BF16)

    at = pl.ds(pl.multiple_of(step * 256, 256), 256)
    total[:, at] = dot_last(grads[:, :HALF_QKV], low_ref[0]) + dot_last(grads[:, HALF_QKV:], up_ref[0])

    @pl.when(step == 5)
    def _():
        for copy in copies:
            copy.wait()
        values = tokens_ref[...].astype(F32)
        standard, inverse_dev = standardized(values)
        grad_standard = total[...] * gain_ref[...]
        first_mean = jnp.mean(grad_standard, axis=-1, keepdims=True)
        second_mean = jnp.mean(grad_standard * standard, axis=-1, keepdims=True)
        grad = inverse_dev * (grad_standard - first_mean - standard * second_mean)
        out_ref[...] = (hidden_ref[...] + grad).astype(BF16)


def norm_grad(dq, dk, dv, from_left, from_right, full, tokens, gain, grad_hidden):
    return pl.pallas_call(
        norm_grad_kernel,
        out_shape=jax.ShapeDtypeStruct((ROWS, D), BF16),
        grid=(6,),
        in_specs=[
            whole_block((ROWS, INNER)),
            whole_block((ROWS, INNER)),
            whole_block((ROWS, INNER)),
            whole_block((2, EDGE, INNER)),
            whole_block((2, EDGE, INNER)),
            pl.BlockSpec((1, 256, HALF_QKV), lambda n: (0, n, 0)),
            pl.BlockSpec((1, 256, HALF_QKV), lambda n: (1, n, 0)),
            whole_block((1, D)),
            pl.BlockSpec(memory_space=pl.ANY),
            pl.BlockSpec(memory_space=pl.ANY),
        ],
        out_specs=whole_block((ROWS, D)),
        scratch_shapes=[
            pltpu.VMEM((ROWS, 3 * INNER), BF16),
            pltpu.VMEM((ROWS, D), F32),
            pltpu.VMEM((ROWS, D), BF16),
            pltpu.VMEM((ROWS, D), F32),
            pltpu.SemaphoreType.DMA((2,)),
        ],
        name="norm_grad",
    )(dq, dk, dv, from_left, from_right, full, full, gain, tokens, grad_hidden)


def spread_kernel(total_ref, out_ref):
    total = total_ref[...]
    empty = jnp.zeros((24, LANES - CHANNELS), F32)
    for z in range(ZS):
        part = jnp.concatenate([total[:, z * CHANNELS : (z + 1) * CHANNELS], empty], axis=1).astype(BF16)
        out_ref[z] = part
        out_ref[ZS + z] = part


def sum_pieces(pieces):
    return pl.pallas_call(
        spread_kernel,
        out_shape=jax.ShapeDtypeStruct((2 * ZS, 24, LANES), BF16),
        in_specs=[WHOLE],
        out_specs=WHOLE,
        name="sum_pieces",
    )(jnp.sum(pieces.astype(F32), axis=0))


def interp_weights(fine_index):
    coarse_cell = fine_index // 4
    phase_index = fine_index % 4
    lower_shift = (phase_index < 2).astype(jnp.int32)
    upper_weight = (2 * phase_index - 3 + 8 * lower_shift).astype(F32) / 8.0
    return (coarse_cell - lower_shift, upper_weight)


def build_matrix(lower_cell, upper_cell, upper_weight, count):
    columns = jnp.arange(count, dtype=jnp.int32)
    lower_part = jnp.where(columns[None, :] == lower_cell[:, None], 1.0 - upper_weight[:, None], 0.0)
    upper_portion = jnp.where(columns[None, :] == upper_cell[:, None], upper_weight[:, None], 0.0)
    return lower_part + upper_portion


def shifted(value, steps):
    return lax.ppermute(value, TILE, [(i, (i + steps) % TILES) for i in range(TILES)])


def residual_of(coarse):
    before = shifted(coarse[:, :, -1:], 1)
    after = shifted(coarse[:, :, :1], -1)
    padded = jnp.concatenate([before, coarse, after], axis=2)
    lat_lower, lat_upper_weight = interp_weights(jnp.arange(4 * LAT, dtype=jnp.int32))
    latitude_matrix = build_matrix(
        jnp.clip(lat_lower, 0, LAT - 1), jnp.clip(lat_lower + 1, 0, LAT - 1), lat_upper_weight, LAT
    )
    lon_lower, lon_upper_weight = interp_weights(jnp.arange(4 * LON_DEV, dtype=jnp.int32))
    lon_matrix = build_matrix(lon_lower + 1, lon_lower + 2, lon_upper_weight, LON_DEV + 2)
    incomplete_grid = jnp.einsum("lj,kji->kli", latitude_matrix, padded, precision=lax.Precision.HIGHEST)
    return jnp.einsum("vrb,cb->vrc", incomplete_grid, lon_matrix, precision=lax.Precision.HIGHEST)


def head_columns():
    target = jnp.arange(PADDED, dtype=jnp.int32)
    phase, channel = target // LANES, target % LANES
    source = jnp.where(channel < CHANNELS, channel * PHASES + phase, -1)
    return (jnp.arange(HEAD_OUT, dtype=jnp.int32)[:, None] == source[None, :]).astype(F32)


def gather_qkv(qkv):
    half = lax.axis_index("dp")
    qkv_half = lax.dynamic_slice_in_dim(qkv, half * HALF_QKV, HALF_QKV, 1)
    full = lax.all_gather(qkv_half, ("dp",) + FSDP, axis=0, tiled=True)
    return full.reshape(2, D, HALF_QKV)


def to_all(value, axes, count):
    copies = jnp.broadcast_to(value[None], (count,) + value.shape)
    return lax.all_to_all(copies, axes, 0, 0, tiled=True)


def gather_rest(core, out_w, head_w, ready):
    out_rows = out_w.reshape(48, 12, LANES).transpose(1, 0, 2).reshape(576, LANES)
    head_pad = dot(head_w, head_columns().astype(BF16)).astype(BF16)
    head_rows = head_pad.reshape(96, PHASES, LANES).transpose(1, 0, 2).reshape(384, LANES)
    rows = jnp.concatenate([out_rows, head_rows, jnp.zeros((PIECE, LANES), BF16)], axis=0)
    own = lax.dynamic_slice_in_dim(rows, lax.axis_index(TILE) * PIECE, PIECE, 0)
    over_z = to_all(own, ("z",), ZS)
    over_tile = to_all(over_z, TILE, TILES)
    over_tile = lax.optimization_barrier((over_tile, ready))[0]
    other = lax.ppermute(over_tile, "c", [(0, 1), (1, 0)])
    return unpack(core, over_tile, other)


def over_samples(summed):
    both = lax.all_to_all(summed, ("dp", "z"), 0, 0, tiled=True)
    spread = to_all(jnp.sum(both.astype(F32), axis=0), TILE, TILES)
    padded = spread.reshape(4, PHASES, 24, LANES).transpose(0, 2, 1, 3).reshape(96, PADDED)
    return lax.dot_general(
        padded, head_columns(), (((1,), (1,)), ((), ())), precision=lax.Precision.HIGHEST, preferred_element_type=F32
    )


def shards(tokens, norm_gain, query_key_value_weight, out_weight, head_weight, coarse, grad_fine):
    tokens = tokens[0].reshape(ROWS, D)
    gain = norm_gain.reshape(1, D)
    full = gather_qkv(query_key_value_weight)
    grid = tokens.reshape(LAT, LON_DEV, D)
    left = shifted(grid[:, LON_DEV - MARGIN :].reshape(EDGE, D), 1)
    right = shifted(grid[:, :MARGIN].reshape(EDGE, D), -1)
    residual = residual_of(coarse[0])
    normed, rows = prepare(tokens, left, right, gain, grad_fine[0])
    core = lax.axis_index("c").reshape(1).astype(jnp.int32)
    out_full, head = gather_rest(core, out_weight, head_weight, (normed, residual))
    full, out_full, head, residual = lax.optimization_barrier((full, out_full, head, residual))
    projected, fine_grid, pieces = forward(normed, full, tokens, out_full, head, rows, residual)
    pieces = lax.all_to_all(pieces, ("c",) + TILE, 0, 0, tiled=True)
    grad_hidden, grad_attended = hidden_grad(rows, head, out_full)
    dq, dk, dv, to_left, to_right = attend_backward(projected, grad_attended)
    pieces, to_left, to_right = lax.optimization_barrier((pieces, to_left, to_right))
    summed = sum_pieces(pieces)
    grad_head = over_samples(summed)
    to_left, to_right = lax.optimization_barrier((to_left, to_right, summed))[:2]
    from_right = shifted(to_left, -1)
    from_left = shifted(to_right, 1)
    grad_tokens = norm_grad(dq, dk, dv, from_left, from_right, full, tokens, gain, grad_hidden)
    return (fine_grid[None], grad_tokens.reshape(1, LAT, LON_DEV, D), grad_head)


def solution(mesh):
    fine_mesh = Mesh(mesh.devices.reshape(2, ZS, CORES, YS, XS), ("dp", "z", "c", "y", "x"))
    samples = ("dp", "z", "c")
    placed = (
        P(samples, None, TILE, None),
        P(),
        P(FSDP, None),
        P(FSDP, None),
        P(FSDP, None),
        P(samples, None, None, TILE),
        P(samples, None, None, TILE),
    )
    return jax.shard_map(
        shards,
        mesh=fine_mesh,
        in_specs=placed,
        out_specs=(P(samples, None, None, TILE), P(samples, None, TILE, None), P(FSDP, None)),
        check_vma=False,
    )
```
